32 devices in a mesh: tm: 8 (over z, x), rows: 4 (over y, core).
Axes of the slice: x: 2, y: 2, z: 4, core: 2. Of those that a mesh axis runs over, the one named last changes fastest.
Arguments:
- video: bfloat16 [4, 32, 16, 16, 256], P(None, 'tm', 'rows'), may hold values from -6 to 6
- weight_in: bfloat16 [3, 3, 256, 512], replicated, may hold values from -0.125 to 0.125
- weight_out: bfloat16 [3, 3, 512, 256], replicated, may hold values from -0.09375 to 0.09375
- rates: float32 [512], replicated, may hold values from 0.0001 to 0.05
- gaps: float32 [4, 32], P(None, 'tm'), may hold values from 0.5 to 6000
Outputs:
- output: bfloat16 [4, 32, 16, 16, 256], P(None, 'tm', 'rows')
The draws below stay inside these ranges and needn't reach their ends.
All inputs are finite; a program needn't handle non-finite values.
Results may differ from the reference program's by a relative error of at most 0.0065.
Values may be sent and summed in bfloat16 or wider, within the bound.
No kernel may reach another device: no remote copies, remote signals or barrier semaphores. Data moves between devices by JAX's collectives and lax.ppermute only.
A program may use at most 64 MiB of HBM per device.

```python
import math
import jax
import jax.numpy as jnp
from jax import lax

CHANNELS = 256
STATES = 512
WIDTH = 16
BATCH = 4
FRAMES = 32
HEIGHT = 16


def draw_rates(key, part):
    first = jax.random.fold_in(key, 0)
    return jnp.exp(jax.random.uniform(first, (STATES,), jnp.float32, math.log(0.0001), math.log(0.05))).astype(jnp.float32)


def draw_gaps(key, part):
    first, second, third = jax.random.split(key, 3)
    base = jax.random.uniform(first, (BATCH, FRAMES), jnp.float32, 0.5, 1.5)
    spots = jax.random.randint(second, (BATCH, 3), 0, FRAMES)
    frame_ids = jnp.arange(FRAMES, dtype=jnp.int32)
    struck = jnp.any(frame_ids[None, None, :] == spots[:, :, None], axis=1)
    large = jax.random.uniform(third, (BATCH, FRAMES), jnp.float32, 2000.0, 6000.0)
    return jnp.where(struck, large, base).astype(jnp.float32)


def shard_levels(stream_key, shape, pieces, smallest, largest):
    def one(axis_at, shards_of):
        draws = jax.random.uniform(jax.random.fold_in(jax.random.fold_in(stream_key, 6), axis_at), (shards_of,), jnp.float32, smallest / len(pieces), largest / len(pieces))
        return jnp.repeat(jnp.exp(draws), shape[axis_at] // shards_of).reshape((-1,) + (1,) * (len(shape) - axis_at - 1))

    loudness = one(*pieces[0])
    for cut in pieces[1:]:
        loudness = loudness * one(*cut)
    return loudness


def normal_values(rng, extent, spread, bound, cuts=(), held_as=jnp.bfloat16):
    gain = shard_levels(rng, extent, cuts, -0.22, 0.18) if cuts else 1.0
    drawn = jax.random.normal(rng, extent, jnp.float32) * spread * gain
    return jnp.minimum(jnp.maximum(drawn, -bound), bound).astype(held_as)


def setup_inputs(seed: int = 0) -> dict:
    splits = jax.random.split(jax.random.key(seed), 6)
    return {
        "video": normal_values(splits[0], (BATCH, FRAMES, HEIGHT, WIDTH, CHANNELS), 1.0, 6.0, ((1, 8), (2, 4))),
        "weight_in": normal_values(splits[1], (3, 3, CHANNELS, STATES), (9 * CHANNELS) ** -0.5, 0.125),
        "weight_out": normal_values(splits[2], (3, 3, STATES, CHANNELS), (9 * STATES) ** -0.5, 0.09375),
        "rates": draw_rates(jax.random.fold_in(splits[5], 71), 0),
        "gaps": draw_gaps(jax.random.fold_in(splits[5], 71), 0),
    }


def convolve(field, weight):
    height = field.shape[2]
    columns = field.shape[3]
    outputs = weight.shape[3]

    def per_sample(sample):
        padded = jnp.pad(sample.astype(jnp.float32), ((0, 0), (1, 1), (1, 1), (0, 0)))
        total = jnp.zeros(sample.shape[:3] + (outputs,), jnp.float32)
        for row_shift in range(3):
            for col_shift in range(3):
                window = padded[:, row_shift:row_shift + height, col_shift:col_shift + columns]
                total = total + jnp.einsum('fhwc,cp->fhwp', window, weight[row_shift, col_shift].astype(jnp.float32), precision=lax.Precision.HIGHEST)
        return total
    return lax.map(per_sample, field)

def reference(video, weight_in, weight_out, rates, gaps):
    driven = convolve(video, weight_in)
    decays = jnp.exp(-rates[None, None, :] * gaps[:, :, None])
    gains = jnp.sqrt(1.0 - decays * decays)

    def advance(state, inputs):
        decay_now, gain_now, driven_now = inputs
        state = decay_now[:, None, None, :] * state + gain_now[:, None, None, :] * driven_now
        return (state, state.astype(jnp.bfloat16))
    start = jnp.zeros((video.shape[0], video.shape[2], video.shape[3], weight_in.shape[3]), jnp.float32)
    final, states = lax.scan(advance, start, (jnp.moveaxis(decays, 1, 0), jnp.moveaxis(gains, 1, 0), jnp.moveaxis(driven, 1, 0)))
    states = jnp.moveaxis(states, 0, 1)
    mixed = convolve(states, weight_out)
    return (video.astype(jnp.float32) + jax.nn.gelu(mixed, approximate=False)).astype(jnp.bfloat16)
```

```python
import functools

import jax
import jax.numpy as jnp
from jax import lax
from jax.experimental import pallas as pl
from jax.experimental.pallas import tpu as pltpu
from jax.sharding import PartitionSpec as P

F32 = jnp.float32
BF16 = jnp.bfloat16
SMEM = pl.BlockSpec(memory_space=pltpu.SMEM)
VMEM = pl.BlockSpec(memory_space=pltpu.VMEM)

OWN, OTHER, SWAP_AT, RING_AT, RING_OK, HIGH = range(6)
BITS = 6


def call(kernel, outs, scratch, vmem_mib, flops, *args):
    specs = [SMEM if a.ndim == 1 or (a.dtype == F32 and a.shape[-1] < 128) else VMEM for a in args]
    return pl.pallas_call(
        kernel,
        out_shape=outs,
        in_specs=specs,
        out_specs=[VMEM] * len(outs),
        scratch_shapes=scratch,
        compiler_params=pltpu.CompilerParams(vmem_limit_bytes=vmem_mib << 20),
        cost_estimate=pl.CostEstimate(flops=flops, bytes_accessed=1 << 20, transcendentals=0),
    )(*args)


def shifted(x, width):
    rows = x.shape[0]
    column = lax.broadcasted_iota(jnp.int32, (rows, 1), 0) % width
    left = jnp.where(column == 0, 0.0, pltpu.roll(x, 1, 0))
    right = jnp.where(column == width - 1, 0.0, pltpu.roll(x, rows - 1, 0))
    return left.astype(BF16), right.astype(BF16)


def put(dest, frame, at, x, width):
    rows, c = x.shape
    left, right = shifted(x.astype(F32), width)
    dest[frame, pl.ds(at, rows), 0:c] = left
    dest[frame, pl.ds(at, rows), c : 2 * c] = x.astype(BF16)
    dest[frame, pl.ds(at, rows), 2 * c : 3 * c] = right


def decay_row(rates_ref, gap):
    return jnp.exp(-rates_ref[...] * gap)


def span_tile(spans, states):
    rows = []
    for span in spans:
        high = span.astype(BF16).astype(F32)
        rest = span - high
        middle = rest.astype(BF16).astype(F32)
        rows += [high, middle, rest - middle]
    total = -(-len(rows) // 16) * 16
    index = lax.broadcasted_iota(jnp.int32, (total, states), 0)
    tile = jnp.zeros((total, states), F32)
    for i, row in enumerate(rows):
        tile = jnp.where(index == i, row, tile)
    return tile.astype(BF16)


def spans_of(tile, half):
    tile = tile.astype(F32)
    return [tile[3 * b : 3 * b + 1] + tile[3 * b + 1 : 3 * b + 2] + tile[3 * b + 2 : 3 * b + 3] for b in range(half)]


def conv_in_kernel(which, width, sel, gaps, rates, video, swap, ring, weight, *rest):
    if which == OTHER:
        local, message, framed = rest
    else:
        local, end, framed = rest
    half, frames, cells, states = local.shape
    b0 = sel[which]
    for b in range(half):
        for t in range(frames):
            f = b * frames + t
            put(framed, f, width, video[b0 + b, t], width)
            put(framed, f, pl.multiple_of(sel[SWAP_AT], width), swap[b0 + b, t], width)
            edge = jnp.where(sel[RING_OK] > 0, ring[b0 + b, t].astype(F32), 0.0)
            put(framed, f, pl.multiple_of(sel[RING_AT], width), edge, width)
    spans = []
    for b in range(half):
        block = framed.at[pl.ds(b * frames, frames)]
        total = None
        for d in range(3):
            lhs = block[:, d * width : d * width + cells, :].reshape(frames * cells, -1)
            term = jnp.dot(lhs, weight[d], preferred_element_type=F32)
            total = term if total is None else total + term
        total = total.reshape(frames, cells, states)
        state = None
        span = None
        for t in range(frames):
            gap = gaps[b0 + b, t]
            decay = decay_row(rates, gap)
            gain = jnp.sqrt(1.0 - decay * decay)
            state = gain * total[t] if state is None else decay * state + gain * total[t]
            local[b, t] = state
            span = gap if span is None else span + gap
        spans.append(jnp.zeros((1, states), F32) + span)
        if which == OTHER:
            message[pl.ds(b * cells, cells), :] = state.astype(BF16)
        else:
            end[b] = state
    if which == OTHER:
        tile = span_tile(spans, states)
        message[pl.ds(half * cells, tile.shape[0]), :] = tile


def pair_kernel(sel, gaps, rates, end, message, low, total, outgoing, meta):
    half, cells, states = end.shape
    b0 = sel[OWN]
    partner = spans_of(message[half * cells :, :], half)
    spans = []
    high = sel[HIGH] > 0
    meta[...] = jnp.zeros_like(meta)
    for b in range(half):
        mine = gaps[b0 + b, 0]
        for t in range(1, gaps.shape[1]):
            mine = mine + gaps[b0 + b, t]
        mine = jnp.zeros((1, states), F32) + mine
        theirs = message[pl.ds(b * cells, cells), :].astype(F32)
        keep = jnp.where(high, 1.0, jnp.exp(-rates[...] * partner[b]))
        add = jnp.where(high, jnp.exp(-rates[...] * mine), 1.0)
        whole = keep * end[b] + add * theirs
        low[b] = jnp.where(high, theirs, end[b])
        total[b] = whole
        outgoing[pl.ds(b * cells, cells), :] = whole.astype(BF16)
        spans.append(mine + partner[b])
        meta[0, b : b + 1] = mine + partner[b]
        meta[2, b : b + 1] = jnp.where(high, partner[b], mine)
    tile = span_tile(spans, states)
    outgoing[pl.ds(half * cells, tile.shape[0]), :] = tile


def round_kernel(bit, first, last, sel, rates, *refs):
    if last:
        if first:
            message, low, total, meta, incoming, outgoing = refs
        else:
            message, low, total, meta, before, incoming, outgoing = refs
    else:
        if first:
            message, total, meta, new_before, new_total, outgoing, new_meta = refs
        else:
            message, total, meta, before, new_before, new_total, outgoing, new_meta = refs
    half, cells, states = total.shape
    upper = sel[BITS + bit] > 0
    high = sel[HIGH] > 0
    partner = spans_of(message[half * cells :, :], half)
    spans = []
    if not last:
        new_meta[...] = jnp.zeros_like(new_meta)
    for b in range(half):
        theirs = message[pl.ds(b * cells, cells), :].astype(F32)
        mine = meta[0, b : b + 1]
        prefix = meta[1, b : b + 1]
        scale = jnp.where(upper, jnp.exp(-rates[...] * prefix), 0.0)
        now = scale * theirs
        if not first:
            now = now + before[b]
        if last:
            below = jnp.exp(-rates[...] * meta[2, b : b + 1]) * now + low[b]
            incoming[b] = jnp.where(high, below, now)
            outgoing[pl.ds(b * cells, cells), :] = jnp.where(high, now, below).astype(BF16)
        else:
            keep = jnp.where(upper, 1.0, jnp.exp(-rates[...] * partner[b]))
            add = jnp.where(upper, jnp.exp(-rates[...] * mine), 1.0)
            whole = keep * total[b] + add * theirs
            new_before[b] = now
            new_total[b] = whole
            outgoing[pl.ds(b * cells, cells), :] = whole.astype(BF16)
            spans.append(mine + partner[b])
            new_meta[0, b : b + 1] = mine + partner[b]
            new_meta[1, b : b + 1] = prefix + jnp.where(upper, partner[b], 0.0)
            new_meta[2, b : b + 1] = meta[2, b : b + 1]
    if not last:
        tile = span_tile(spans, states)
        outgoing[pl.ds(half * cells, tile.shape[0]), :] = tile


def conv_out_kernel(which, width, sel, gaps, rates, local, incoming, swap_local, ring_local, swap_in, ring_in, weight, mixed, framed):
    half, frames, cells, states = local.shape
    b0 = sel[which]
    for b in range(half):
        gone = None
        for t in range(frames):
            gap = gaps[b0 + b, t]
            gone = gap if gone is None else gone + gap
            product = decay_row(rates, gone)
            f = b * frames + t
            put(framed, f, width, local[b, t] + product * incoming[b].astype(F32), width)
            edge = swap_local[b0 + b, t].astype(F32) + product * swap_in[b0 + b].astype(F32)
            put(framed, f, pl.multiple_of(sel[SWAP_AT], width), edge, width)
            edge = ring_local[b0 + b, t].astype(F32) + product * ring_in[b0 + b].astype(F32)
            edge = jnp.where(sel[RING_OK] > 0, edge, 0.0)
            put(framed, f, pl.multiple_of(sel[RING_AT], width), edge, width)
    for b in range(half):
        block = framed.at[pl.ds(b * frames, frames)]
        total = None
        for d in range(3):
            lhs = block[:, d * width : d * width + cells, :].reshape(frames * cells, -1)
            term = jnp.dot(lhs, weight[d], preferred_element_type=F32)
            total = term if total is None else total + term
        mixed[b] = total.reshape(frames, cells, -1)


def on_device(video, weight_in, weight_out, rates, gaps):
    batch, frames, rows, width, channels = video.shape
    states = weight_in.shape[3]
    half = batch // 2
    cells = rows * width
    blocks = lax.axis_size("tm")
    strips = lax.axis_size("rows")
    me = lax.axis_index("tm")
    strip = lax.axis_index("rows")
    high = me % 2
    place = me // 2
    rounds = (blocks // 2).bit_length() - 1
    even = strip % 2 == 0
    bottom = rows - 1
    swap_from = jnp.where(even, bottom, 0)
    ring_from = bottom - swap_from
    ring_ok = jnp.logical_not(jnp.logical_or(jnp.logical_and(even, strip == 0), strip == strips - 1))
    low_at, high_at = 0, (rows + 1) * width
    sel = jnp.stack(
        [high * half, (1 - high) * half, jnp.where(even, high_at, low_at), jnp.where(even, low_at, high_at), ring_ok.astype(jnp.int32), high]
        + [(place >> r) & 1 for r in range(rounds)]
    ).astype(jnp.int32)
    swap = [(i, i ^ 1) for i in range(strips)]
    ring = [(i, (i + 1 if i % 2 else i - 1) % strips) for i in range(strips)]
    pair = [(i, i ^ 1) for i in range(blocks)]

    def mirror(r):
        return [(i, ((i // 2) ^ (2 ** (r + 1) - 1)) * 2 + i % 2) for i in range(blocks)]

    def edge(x, start):
        return lax.dynamic_slice_in_dim(x, start * width, width, axis=x.ndim - 2)

    rates = rates[None, :]
    video = video.reshape(batch, frames, cells, channels)
    ring_video = lax.ppermute(edge(video, ring_from), "rows", ring)
    swap_video = lax.ppermute(edge(video, swap_from), "rows", swap)
    weight_in = weight_in.reshape(3, 3 * channels, states)
    weight_out = weight_out.reshape(3, 3 * states, channels)
    extra = -(-3 * half // 16) * 16
    message_shape = jax.ShapeDtypeStruct((half * cells + extra, states), BF16)
    local_shape = jax.ShapeDtypeStruct((half, frames, cells, states), F32)
    end_shape = jax.ShapeDtypeStruct((half, cells, states), F32)
    meta_shape = jax.ShapeDtypeStruct((3, 8, states), F32)
    flops = 2 * half * frames * cells * 9 * channels * states
    framed = [pltpu.VMEM((half * frames, cells + 2 * width, 3 * channels), BF16)]

    common = (sel, gaps, rates, video, swap_video, ring_video, weight_in)
    local_other, message = call(
        functools.partial(conv_in_kernel, OTHER, width), [local_shape, message_shape], framed, 16, flops, *common
    )
    message = lax.ppermute(message, "tm", pair)
    local_own, end = call(functools.partial(conv_in_kernel, OWN, width), [local_shape, end_shape], framed, 16, flops, *common)

    low, total, outgoing, meta = call(
        pair_kernel, [end_shape, end_shape, message_shape, meta_shape], [], 8, 1 << 20, sel, gaps, rates, end, message
    )
    local = jnp.where(high == 0, jnp.concatenate([local_own, local_other]), jnp.concatenate([local_other, local_own]))
    swap_local = lax.ppermute(edge(local, swap_from).astype(BF16), "rows", swap)
    ring_local = lax.ppermute(edge(local, ring_from).astype(BF16), "rows", ring)
    before = None
    for r in range(rounds):
        message = lax.ppermute(outgoing, "tm", mirror(r))
        first, last = r == 0, r == rounds - 1
        kernel = functools.partial(round_kernel, r, first, last)
        extra_in = [] if first else [before]
        if last:
            incoming_own, outgoing = call(
                kernel,
                [end_shape, jax.ShapeDtypeStruct((half * cells, states), BF16)],
                [], 8, 1 << 20, sel, rates, message, low, total, meta, *extra_in,
            )
        else:
            before, total, outgoing, meta = call(
                kernel, [end_shape, end_shape, message_shape, meta_shape], [], 8, 1 << 20, sel, rates, message, total, meta, *extra_in
            )
    incoming_other = lax.ppermute(outgoing, "tm", pair).reshape(half, cells, states)
    own_low = incoming_own.astype(BF16)
    incoming = jnp.where(high == 0, jnp.concatenate([own_low, incoming_other]), jnp.concatenate([incoming_other, own_low]))
    swap_in = lax.ppermute(edge(incoming, swap_from), "rows", swap)
    ring_in = lax.ppermute(edge(incoming, ring_from), "rows", ring)

    framed = [pltpu.VMEM((half * frames, cells + 2 * width, 3 * states), BF16)]
    mixed_shape = jax.ShapeDtypeStruct((half, frames, cells, channels), F32)
    common = (swap_local, ring_local, swap_in, ring_in, weight_out)
    mixed_own, = call(functools.partial(conv_out_kernel, OWN, width), [mixed_shape], framed, 20, flops, sel, gaps, rates, local_own, incoming_own, *common)
    mixed_other, = call(functools.partial(conv_out_kernel, OTHER, width), [mixed_shape], framed, 20, flops, sel, gaps, rates, local_other, incoming_other, *common)
    mixed = jnp.where(high == 0, jnp.concatenate([mixed_own, mixed_other]), jnp.concatenate([mixed_other, mixed_own]))
    out = (video.astype(F32) + jax.nn.gelu(mixed, approximate=False)).astype(BF16)
    return out.reshape(batch, frames, rows, width, channels)


def solution(mesh):
    in_specs = (P(None, "tm", "rows", None, None), P(), P(), P(), P(None, "tm"))
    out_specs = P(None, "tm", "rows", None, None)
    return jax.shard_map(on_device, mesh=mesh, in_specs=in_specs, out_specs=out_specs, check_vma=False)
```

```python
import functools

import jax
import jax.numpy as jnp
from jax import lax
from jax.experimental import pallas as pl
from jax.experimental.pallas import tpu as pltpu
from jax.sharding import PartitionSpec as P

F32 = jnp.float32
BF16 = jnp.bfloat16
SMEM = pl.BlockSpec(memory_space=pltpu.SMEM)
VMEM = pl.BlockSpec(memory_space=pltpu.VMEM)
HBM = pl.BlockSpec(memory_space=pltpu.HBM)


def call(kernel, name, args, outs, scratch=(), specs=None, mib=8, flops=1 << 20, bytes_accessed=1 << 20):
    return pl.pallas_call(
        kernel,
        out_shape=outs,
        in_specs=specs or [VMEM] * len(args),
        out_specs=[VMEM] * len(outs),
        scratch_shapes=list(scratch),
        name=name,
        compiler_params=pltpu.CompilerParams(vmem_limit_bytes=mib << 20),
        cost_estimate=pl.CostEstimate(flops=flops, bytes_accessed=bytes_accessed, transcendentals=0),
    )(*args)


def like(*shape, dtype=F32):
    return jax.ShapeDtypeStruct(shape, dtype)


def even_strip():
    return lax.axis_index("rows") % 2 == 0


def aligned(start, step):
    return pl.multiple_of(start, step)


def with_shifts(x, width):
    rows = x.shape[0]
    x = x.astype(F32)
    column = lax.broadcasted_iota(jnp.int32, (rows, 1), 0) % width
    left = jnp.where(column == 0, 0.0, pltpu.roll(x, 1, 0))
    right = jnp.where(column == width - 1, 0.0, pltpu.roll(x, rows - 1, 0))
    return left.astype(BF16), x.astype(BF16), right.astype(BF16)


def put(dest, index, x, width):
    c = x.shape[1]
    for i, part in enumerate(with_shifts(x, width)):
        dest[index + (slice(i * c, (i + 1) * c),)] = part


def span_tile(spans):
    rows = []
    for span in spans:
        high = span.astype(BF16).astype(F32)
        rest = span - high
        middle = rest.astype(BF16).astype(F32)
        rows += [high, middle, rest - middle]
    total = -(-len(rows) // 16) * 16
    index = lax.broadcasted_iota(jnp.int32, (total, rows[0].shape[1]), 0)
    tile = jnp.zeros(index.shape, F32)
    for i, row in enumerate(rows):
        tile = jnp.where(index == i, row, tile)
    return tile.astype(BF16)


def spans_of(tile, half):
    tile = tile.astype(F32)
    return [tile[3 * b : 3 * b + 1] + tile[3 * b + 1 : 3 * b + 2] + tile[3 * b + 2 : 3 * b + 3] for b in range(half)]


def edges_kernel(width, video, ring, swap, sems):
    last = video.shape[2] - width
    even = even_strip()
    copies = []
    for i, (start, dest) in enumerate([(jnp.where(even, 0, last), ring), (jnp.where(even, last, 0), swap)]):
        copy = pltpu.make_async_copy(video.at[:, :, pl.ds(aligned(start, width), width), :], dest, sems.at[i])
        copy.start()
        copies.append(copy)
    for copy in copies:
        copy.wait()


def own_kernel(width, gaps, rates, video_hbm, weight_hbm, driven, table, weight, video, framed, sems):
    batch, frames, cells, states = driven.shape
    channels = video.shape[3]
    copies = [pltpu.make_async_copy(video_hbm, video, sems.at[3])]
    copies += [pltpu.make_async_copy(weight_hbm.at[d], weight.at[d], sems.at[d]) for d in (1, 0, 2)]
    for copy in copies:
        copy.start()
    for b in range(batch):
        span = None
        for t in range(frames):
            gap = gaps[b, t]
            span = gap if span is None else span + gap
            decay = jnp.exp(-rates[...] * gap)
            table[b, t : t + 1] = decay
            table[b, frames + t : frames + t + 1] = jnp.sqrt(1.0 - decay * decay)
            table[b, 2 * frames + t : 2 * frames + t + 1] = jnp.exp(-rates[...] * span)
        table[b, 3 * frames : 3 * frames + 1] = jnp.zeros((1, states), F32) + span
    copies[0].wait()
    for b in range(batch):
        put(framed, (pl.ds(b * frames * cells, frames * cells),), video[b].reshape(frames * cells, channels), width)
    less = cells - width
    half = batch // 2
    rows = half * frames * cells
    for copy in copies[1:]:
        copy.wait()
    for h in range(2):
        block = framed[pl.ds(h * rows, rows), :]
        frame = block.reshape(half * frames, cells, 3 * channels)
        total = jnp.dot(block, weight[1], preferred_element_type=F32)
        at = pl.ds(h * half, half)
        driven[at] = total.reshape(half, frames, cells, states)
        above = jnp.dot(frame[:, :less].reshape(-1, 3 * channels), weight[0], preferred_element_type=F32)
        driven[at, :, width:, :] += above.reshape(half, frames, less, states)
        below = jnp.dot(frame[:, width:].reshape(-1, 3 * channels), weight[2], preferred_element_type=F32)
        driven[at, :, :less, :] += below.reshape(half, frames, less, states)


def halo_rows(framed, first, half, width, swap, ring, product=None, more=None):
    even = even_strip().astype(jnp.int32)
    frames = swap.shape[1]
    rows = half * frames * width

    def block(ref, states):
        x = ref[first : first + half]
        if product is None:
            return x.reshape(rows, x.shape[3])
        pieces = []
        for b in range(half):
            incoming = states[first + b].astype(F32)
            pieces += [x[b, t].astype(F32) + product(b, t) * incoming for t in range(frames)]
        return jnp.concatenate(pieces, axis=0)

    x = block(swap, more and more[0])
    put(framed, (even, slice(None)), x, width)
    x = block(ring, more and more[1])
    put(framed, (1 - even, slice(None)), jnp.where(ring_open(), x, jnp.zeros_like(x)), width)


def ring_open():
    strip = lax.axis_index("rows")
    return jnp.logical_and(strip != 0, strip != lax.axis_size("rows") - 1)


def scan_kernel(part, width, driven, table, weight, swap, ring, *refs):
    if part == 0:
        local, message, framed = refs
    else:
        before, local, message, ring_out, swap_out, framed = refs
    half, frames, cells, states = local.shape
    first = part * half
    halo_rows(framed, first, half, width, swap, ring)
    top = jnp.dot(framed[0], weight[0], preferred_element_type=F32)
    bottom = jnp.dot(framed[1], weight[2], preferred_element_type=F32)
    spans = []
    for b in range(half):
        for r in range(0, cells, width):
            state = None
            for t in range(frames):
                value = driven[first + b, t, r : r + width]
                at = (b * frames + t) * width
                if r == 0:
                    value = value + top[at : at + width]
                if r == cells - width:
                    value = value + bottom[at : at + width]
                value = table[first + b, frames + t : frames + t + 1] * value
                state = value if state is None else table[first + b, t : t + 1] * state + value
                local[b, t, r : r + width] = state
            message[b * cells + r : b * cells + r + width] = state.astype(BF16)
        spans.append(table[first + b, 3 * frames : 3 * frames + 1])
    tile = span_tile(spans)
    message[half * cells : half * cells + tile.shape[0]] = tile
    if part == 1:
        even = even_strip()
        last = cells - width
        for source, at in ((before, 0), (local, half)):
            for dest, start in ((ring_out, jnp.where(even, 0, last)), (swap_out, jnp.where(even, last, 0))):
                for b in range(half):
                    dest[at + b] = source[b, :, pl.ds(aligned(start, width), width), :].astype(BF16)


def round_kernel(part, bit, *refs):
    if bit == 0:
        rates, message, local, table, before, total, outgoing, meta = refs
        half, frames, cells, states = local.shape
    else:
        rates, message, old_before, old_total, old_meta, before, total, outgoing, meta = refs
        half, cells, states = old_total.shape
    upper = (lax.axis_index("tm") >> bit) % 2 == 1
    partner = spans_of(message[half * cells :, :], half)
    spans = []
    meta[...] = jnp.zeros_like(meta)
    for b in range(half):
        theirs = message[b * cells : (b + 1) * cells].astype(F32)
        if bit == 0:
            mine = table[part * half + b, 3 * frames : 3 * frames + 1]
            own = local[b, frames - 1]
            before[b] = jnp.where(upper, theirs, 0.0)
            meta[1, b : b + 1] = jnp.where(upper, partner[b], 0.0)
        else:
            mine = old_meta[0, b : b + 1]
            prefix = old_meta[1, b : b + 1]
            own = old_total[b]
            before[b] = old_before[b] + jnp.where(upper, jnp.exp(-rates[...] * prefix), 0.0) * theirs
            meta[1, b : b + 1] = prefix + jnp.where(upper, partner[b], 0.0)
        keep = jnp.where(upper, 1.0, jnp.exp(-rates[...] * partner[b]))
        add = jnp.where(upper, jnp.exp(-rates[...] * mine), 1.0)
        whole = keep * own + add * theirs
        total[b] = whole
        outgoing[b * cells : (b + 1) * cells] = whole.astype(BF16)
        spans.append(mine + partner[b])
        meta[0, b : b + 1] = mine + partner[b]
    tile = span_tile(spans)
    outgoing[half * cells : half * cells + tile.shape[0]] = tile


def last_scale(bit, rates, meta, b):
    upper = (lax.axis_index("tm") >> bit) % 2 == 1
    return jnp.where(upper, jnp.exp(-rates[...] * meta[1, b : b + 1]), 0.0)


def incoming_edges_kernel(bit, width, rates, *refs):
    *halves, ring, swap = refs
    even = even_strip()
    for part in range(2):
        message, before, meta = halves[3 * part : 3 * part + 3]
        half, cells, states = before.shape
        last = cells - width
        for b in range(half):
            scale = last_scale(bit, rates, meta, b)
            for dest, start in ((ring, jnp.where(even, 0, last)), (swap, jnp.where(even, last, 0))):
                start = aligned(start, width)
                theirs = message[pl.ds(aligned(b * cells + start, width), width), :].astype(F32)
                dest[part * half + b] = (before[b, pl.ds(start, width), :] + scale * theirs).astype(BF16)


def gelu(x):
    return 0.5 * x * (1.0 + lax.erf(x * 0.7071067811865476))


def mix_kernel(part, bit, width, rates, message, before, meta, local, table, weight, video, inner, outer, framed):
    half, frames, cells, states = local.shape
    channels = video.shape[3]
    first = part * half
    for b in range(half):
        scale = last_scale(bit, rates, meta, b)
        incoming = before[b] + scale * message[b * cells : (b + 1) * cells].astype(F32)
        for t in range(frames):
            product = table[first + b, 2 * frames + t : 2 * frames + t + 1]
            put(framed, (pl.ds((b * frames + t) * cells, cells),), local[b, t] + product * incoming, width)
    less = cells - width
    for b in range(half):
        block = framed[pl.ds(b * frames * cells, frames * cells), :]
        frame = block.reshape(frames, cells, 3 * states)
        total = jnp.dot(block, weight[1], preferred_element_type=F32).reshape(frames, cells, channels)
        above = jnp.dot(frame[:, :less].reshape(-1, 3 * states), weight[0], preferred_element_type=F32).reshape(frames, less, channels)
        below = jnp.dot(frame[:, width:].reshape(-1, 3 * states), weight[2], preferred_element_type=F32).reshape(frames, less, channels)
        outer[b, :, :width] = total[:, :width] + below[:, :width]
        outer[b, :, width:] = total[:, less:] + above[:, less - width :]
        middle = total[:, width:less] + above[:, : less - width] + below[:, width:]
        inner[b] = (video[first + b, :, width:less].astype(F32) + gelu(middle)).astype(BF16)


def finish_kernel(width, inner_a, inner_b, outer_a, outer_b, swap_local, ring_local, swap_in, ring_in, table, weight, video, out, framed):
    batch, frames, cells, channels = out.shape
    half = batch // 2
    less = cells - width

    def product(b, t):
        return table[b, 2 * frames + t : 2 * frames + t + 1]

    halo_rows(framed, 0, batch, width, swap_local, ring_local, product, (swap_in, ring_in))
    top = jnp.dot(framed[0], weight[0], preferred_element_type=F32).reshape(batch, frames, width, channels)
    bottom = jnp.dot(framed[1], weight[2], preferred_element_type=F32).reshape(batch, frames, width, channels)
    for part, (inner, outer) in enumerate(((inner_a, outer_a), (inner_b, outer_b))):
        at = pl.ds(part * half, half)
        out[at, :, width:less] = inner[...]
        mixed = outer[:, :, :width] + top[part * half : (part + 1) * half]
        out[at, :, :width] = (video[at, :, :width].astype(F32) + gelu(mixed)).astype(BF16)
        mixed = outer[:, :, width:] + bottom[part * half : (part + 1) * half]
        out[at, :, less:] = (video[at, :, less:].astype(F32) + gelu(mixed)).astype(BF16)


def on_device(video, weight_in, weight_out, rates, gaps):
    batch, frames, rows, width, channels = video.shape
    states = weight_in.shape[3]
    half = batch // 2
    cells = rows * width
    blocks = lax.axis_size("tm")
    strips = lax.axis_size("rows")
    rounds = blocks.bit_length() - 1
    swap = [(i, i ^ 1) for i in range(strips)]
    ring = [(i, (i + 1 if i % 2 else i - 1) % strips) for i in range(strips)]

    def across(bit):
        mask = 1 if bit == 0 else 2 ** (bit + 1) - 2
        return [(i, i ^ mask) for i in range(blocks)]

    def permute(name, x, axis, pairs):
        with jax.named_scope(name):
            return lax.ppermute(x, axis, pairs)

    rates = rates[None, :]
    video = video.reshape(batch, frames, cells, channels)
    weight_in = weight_in.reshape(3, 3 * channels, states)
    weight_out = weight_out.reshape(3, 3 * states, channels)
    edge_flops = 2 * batch * frames * width * 6 * channels * states
    own_flops = 5 * edge_flops

    edge = like(batch, frames, width, channels, dtype=BF16)
    ring_video, swap_video = call(
        functools.partial(edges_kernel, width), "edges", [video], [edge, edge], [pltpu.SemaphoreType.DMA((2,))], [HBM]
    )
    ring_video = permute("ring_video", ring_video, "rows", ring)
    swap_video = permute("swap_video", swap_video, "rows", swap)

    table_rows = -(-(3 * frames + 1) // 8) * 8
    driven, table, weight, video = call(
        functools.partial(own_kernel, width), "own", [gaps, rates, video, weight_in],
        [like(batch, frames, cells, states), like(batch, table_rows, states), like(*weight_in.shape, dtype=BF16), like(*video.shape, dtype=BF16)],
        [pltpu.VMEM((batch * frames * cells, 3 * channels), BF16), pltpu.SemaphoreType.DMA((4,))],
        [SMEM, VMEM, HBM, HBM], mib=24, flops=own_flops,
    )
    extra = -(-3 * half // 16) * 16
    message = like(half * cells + extra, states, dtype=BF16)
    local = like(half, frames, cells, states)
    end = like(half, cells, states)
    meta = like(2, 8, states)
    halo = like(batch, frames, width, states, dtype=BF16)
    framed = [pltpu.VMEM((2, half * frames * width, 3 * channels), BF16)]
    common = [driven, table, weight, swap_video, ring_video]
    local_a, message_a = call(
        functools.partial(scan_kernel, 0, width), "scan_a", common, [local, message], framed, flops=edge_flops // 2
    )
    message_a = permute("r0a", message_a, "tm", across(0))
    local_b, message_b, ring_local, swap_local = call(
        functools.partial(scan_kernel, 1, width), "scan_b", common + [local_a], [local, message, halo, halo], framed, flops=edge_flops // 2
    )
    message_b = permute("r0b", message_b, "tm", across(0))
    ring_local = permute("ring_local", ring_local, "rows", ring)
    swap_local = permute("swap_local", swap_local, "rows", swap)

    parts = [[message_a, local_a, table], [message_b, local_b, table]]
    for bit in range(rounds - 1):
        for part in range(2):
            before, total, outgoing, state_meta = call(
                functools.partial(round_kernel, part, bit), f"join_{bit}{'ab'[part]}", [rates] + parts[part], [end, end, message, meta]
            )
            outgoing = permute(f"r{bit + 1}{'ab'[part]}", outgoing, "tm", across(bit + 1))
            parts[part] = [outgoing, before, total, state_meta]
    last = rounds - 1
    ends = [[p[0], p[1], p[3]] for p in parts]
    edge = like(batch, width, states, dtype=BF16)

    def mix(part, flops):
        return call(
            functools.partial(mix_kernel, part, last, width), f"mix_{'ab'[part]}",
            [rates] + ends[part] + [(local_a, local_b)[part], table, weight_out, video],
            [like(half, frames, cells - 2 * width, channels, dtype=BF16), like(half, frames, 2 * width, channels)],
            [pltpu.VMEM((half * frames * cells, 3 * states), BF16)], mib=16, flops=flops,
        )

    inner_a, outer_a = mix(0, own_flops // 2)
    ring_in, swap_in = call(
        functools.partial(incoming_edges_kernel, last, width), "incoming_edges", [rates] + ends[0] + ends[1], [edge, edge]
    )
    ring_in = permute("ring_in", ring_in, "rows", ring)
    swap_in = permute("swap_in", swap_in, "rows", swap)
    inner_b, outer_b = mix(1, own_flops // 2)
    out, = call(
        functools.partial(finish_kernel, width), "finish",
        [inner_a, inner_b, outer_a, outer_b, swap_local, ring_local, swap_in, ring_in, table, weight_out, video],
        [like(batch, frames, cells, channels, dtype=BF16)],
        [pltpu.VMEM((2, batch * frames * width, 3 * states), BF16)], mib=16, flops=edge_flops,
    )
    return out.reshape(batch, frames, rows, width, channels)


def solution(mesh):
    in_specs = (P(None, "tm", "rows", None, None), P(), P(), P(), P(None, "tm"))
    out_specs = P(None, "tm", "rows", None, None)
    return jax.shard_map(on_device, mesh=mesh, in_specs=in_specs, out_specs=out_specs, check_vma=False)
```

```python
import functools

import jax
import jax.numpy as jnp
from jax import lax
from jax.experimental import pallas as pl
from jax.experimental.pallas import tpu as pltpu
from jax.sharding import PartitionSpec as P


F32 = jnp.float32
BF16 = jnp.bfloat16
SMEM = pl.BlockSpec(memory_space=pltpu.SMEM)
VMEM = pl.BlockSpec(memory_space=pltpu.VMEM)
HBM = pl.BlockSpec(memory_space=pltpu.HBM)


def call(kernel, args, outs, scratch=(), specs=None, mib=8, flops=1 << 20, bytes_accessed=1 << 20):
    return pl.pallas_call(
        kernel,
        out_shape=outs,
        in_specs=specs or [VMEM] * len(args),
        out_specs=[VMEM] * len(outs),
        scratch_shapes=list(scratch),
        compiler_params=pltpu.CompilerParams(vmem_limit_bytes=mib << 20),
        cost_estimate=pl.CostEstimate(flops=flops, bytes_accessed=bytes_accessed, transcendentals=0),
    )(*args)


def like(*shape, dtype=F32):
    return jax.ShapeDtypeStruct(shape, dtype)


def even_strip():
    return lax.axis_index("rows") % 2 == 0


def aligned(start, step):
    return pl.multiple_of(start, step)


def with_shifts(x, width):
    rows = x.shape[0]
    x = x.astype(F32)
    column = lax.broadcasted_iota(jnp.int32, (rows, 1), 0) % width
    left = jnp.where(column == 0, 0.0, pltpu.roll(x, 1, 0))
    right = jnp.where(column == width - 1, 0.0, pltpu.roll(x, rows - 1, 0))
    return left.astype(BF16), x.astype(BF16), right.astype(BF16)


def put(dest, index, x, width):
    c = x.shape[1]
    for i, part in enumerate(with_shifts(x, width)):
        dest[index + (slice(i * c, (i + 1) * c),)] = part


def span_tile(spans):
    rows = []
    for span in spans:
        high = span.astype(BF16).astype(F32)
        rest = span - high
        middle = rest.astype(BF16).astype(F32)
        rows += [high, middle, rest - middle]
    total = -(-len(rows) // 16) * 16
    index = lax.broadcasted_iota(jnp.int32, (total, rows[0].shape[1]), 0)
    tile = jnp.zeros(index.shape, F32)
    for i, row in enumerate(rows):
        tile = jnp.where(index == i, row, tile)
    return tile.astype(BF16)


def spans_of(tile, half):
    tile = tile.astype(F32)
    return [tile[3 * b : 3 * b + 1] + tile[3 * b + 1 : 3 * b + 2] + tile[3 * b + 2 : 3 * b + 3] for b in range(half)]


def lanes(half):
    high = lax.axis_index("tm") % 2
    return high * half, (1 - high) * half


def edges_kernel(width, video, ring, swap, sems):
    batch = video.shape[0]
    half = batch // 2
    last = video.shape[2] - width
    even = even_strip()
    copies = []
    for i, (start, dest) in enumerate([(jnp.where(even, 0, last), ring), (jnp.where(even, last, 0), swap)]):
        for lane, first in enumerate(lanes(half)):
            source = video.at[pl.ds(first, half), :, pl.ds(aligned(start, width), width), :]
            copy = pltpu.make_async_copy(source, dest.at[pl.ds(lane * half, half)], sems.at[i, lane])
            copy.start()
            copies.append(copy)
    for copy in copies:
        copy.wait()


def own_kernel(width, gaps_hbm, rates_hbm, video_hbm, weight_hbm, driven, table, weight, video, framed, gaps, rates, sems):
    batch, frames, cells, states = driven.shape
    channels = video.shape[3]
    half = batch // 2
    first = lanes(half)
    copies = [pltpu.make_async_copy(video_hbm.at[pl.ds(first[i], half)], video.at[pl.ds(i * half, half)], sems.at[i]) for i in range(2)]
    copies += [pltpu.make_async_copy(gaps_hbm, gaps, sems.at[2]), pltpu.make_async_copy(rates_hbm, rates, sems.at[3])]
    weights = [pltpu.make_async_copy(weight_hbm.at[d], weight.at[d], sems.at[4 + d]) for d in (1, 0, 2)]
    for copy in copies + weights:
        copy.start()
    for copy in copies[:2]:
        copy.wait()
    for b in range(batch):
        put(framed, (pl.ds(b * frames * cells, frames * cells),), video[b].reshape(frames * cells, channels), width)
    less = cells - width
    rows = half * frames * cells
    for h in range(2):
        block = framed[pl.ds(h * rows, rows), :]
        frame = block.reshape(half * frames, cells, 3 * channels)
        at = pl.ds(h * half, half)
        if h == 0:
            weights[0].wait()
        total = jnp.dot(block, weight[1], preferred_element_type=F32)
        driven[at] = total.reshape(half, frames, cells, states)
        if h == 0:
            weights[1].wait()
        above = jnp.dot(frame[:, :less].reshape(-1, 3 * channels), weight[0], preferred_element_type=F32)
        driven[at, :, width:, :] += above.reshape(half, frames, less, states)
        if h == 0:
            weights[2].wait()
        below = jnp.dot(frame[:, width:].reshape(-1, 3 * channels), weight[2], preferred_element_type=F32)
        driven[at, :, :less, :] += below.reshape(half, frames, less, states)
    for copy in copies[2:]:
        copy.wait()
    rate = rates[...]
    for b in range(batch):
        span = None
        for t in range(frames):
            gap = gaps[first[b // half] + b % half, t]
            span = gap if span is None else span + gap
            decay = jnp.exp(-rate * gap)
            table[b, t : t + 1] = decay
            table[b, frames + t : frames + t + 1] = jnp.sqrt(1.0 - decay * decay)
            table[b, 2 * frames + t : 2 * frames + t + 1] = jnp.exp(-rate * span)
        table[b, 3 * frames : 3 * frames + 1] = jnp.zeros((1, states), F32) + span
        table[b, 3 * frames + 1 : 3 * frames + 2] = rate


def table_rows(frames):
    return -(-(3 * frames + 2) // 8) * 8


def ring_open():
    strip = lax.axis_index("rows")
    return jnp.logical_and(strip != 0, strip != lax.axis_size("rows") - 1)


def halo_block(first, half, halo, product=None, incoming=None):
    frames, width, c = halo.shape[1:]
    x = halo[first : first + half]
    if product is None:
        return x.reshape(half * frames * width, c)
    pieces = []
    for b in range(half):
        more = incoming[first + b].astype(F32)
        pieces += [x[b, t].astype(F32) + product(b, t) * more for t in range(frames)]
    return jnp.concatenate(pieces, axis=0)


def scan_kernel(part, width, driven, table, weight, swap, ring, *refs):
    if part == 1:
        local, message, framed = refs
    else:
        other, local, end, ring_out, swap_out, framed = refs
    half, frames, cells, _ = local.shape
    first = part * half
    even = even_strip().astype(jnp.int32)
    put(framed, (even, slice(None)), halo_block(first, half, swap), width)
    x = halo_block(first, half, ring)
    put(framed, (1 - even, slice(None)), jnp.where(ring_open(), x, jnp.zeros_like(x)), width)
    top = jnp.dot(framed[0], weight[0], preferred_element_type=F32)
    bottom = jnp.dot(framed[1], weight[2], preferred_element_type=F32)
    for b in range(half):
        for r in range(0, cells, width):
            state = None
            for t in range(frames):
                value = driven[first + b, t, r : r + width]
                at = (b * frames + t) * width
                if r == 0:
                    value = value + top[at : at + width]
                if r == cells - width:
                    value = value + bottom[at : at + width]
                value = table[first + b, frames + t : frames + t + 1] * value
                state = value if state is None else table[first + b, t : t + 1] * state + value
                local[b, t, r : r + width] = state
            if part == 1:
                message[b * cells + r : b * cells + r + width] = state.astype(BF16)
            else:
                end[b, r : r + width] = state
    if part == 1:
        tile = span_tile([table[first + b, 3 * frames : 3 * frames + 1] for b in range(half)])
        message[half * cells : half * cells + tile.shape[0]] = tile
    else:
        last = cells - width
        for source, at in ((local, 0), (other, half)):
            for dest, start in ((ring_out, jnp.where(even == 1, 0, last)), (swap_out, jnp.where(even == 1, last, 0))):
                for b in range(half):
                    dest[at + b] = source[b, :, pl.ds(aligned(start, width), width), :].astype(BF16)


def send(outgoing, values, spans):
    for b, value in enumerate(values):
        cells = value.shape[0]
        outgoing[b * cells : (b + 1) * cells] = value.astype(BF16)
    if spans:
        tile = span_tile(spans)
        outgoing[len(values) * cells : len(values) * cells + tile.shape[0]] = tile


def pair_kernel(frames, message, end, table, low, total, outgoing, meta):
    half, cells, _ = end.shape
    high = lax.axis_index("tm") % 2 == 1
    partner = spans_of(message[half * cells :, :], half)
    meta[...] = jnp.zeros_like(meta)
    values, spans = [], []
    for b in range(half):
        rate = table[b, 3 * frames + 1 : 3 * frames + 2]
        mine = table[b, 3 * frames : 3 * frames + 1]
        theirs = message[b * cells : (b + 1) * cells].astype(F32)
        keep = jnp.where(high, 1.0, jnp.exp(-rate * partner[b]))
        add = jnp.where(high, jnp.exp(-rate * mine), 1.0)
        whole = keep * end[b] + add * theirs
        low[b] = jnp.where(high, theirs, end[b])
        total[b] = whole
        values.append(whole)
        spans.append(mine + partner[b])
        meta[0, b : b + 1] = mine + partner[b]
        meta[2, b : b + 1] = jnp.where(high, partner[b], mine)
    send(outgoing, values, spans)


def join_kernel(frames, bit, first, last, message, table, old_total, old_meta, *refs):
    half, cells, _ = old_total.shape
    refs = list(refs)
    old_before = None if first else refs.pop(0)
    if last:
        low, incoming, outgoing = refs
    else:
        before, total, outgoing, meta = refs
        meta[...] = jnp.zeros_like(meta)
    place = lax.axis_index("tm")
    upper = (place >> bit) % 2 == 1
    high = place % 2 == 1
    partner = spans_of(message[half * cells :, :], half)
    values, spans = [], []
    for b in range(half):
        rate = table[b, 3 * frames + 1 : 3 * frames + 2]
        theirs = message[b * cells : (b + 1) * cells].astype(F32)
        mine = old_meta[0, b : b + 1]
        prefix = old_meta[1, b : b + 1]
        now = jnp.where(upper, jnp.exp(-rate * prefix), 0.0) * theirs
        if not first:
            now = now + old_before[b]
        if last:
            below = jnp.exp(-rate * old_meta[2, b : b + 1]) * now + low[b]
            incoming[b] = jnp.where(high, below, now)
            values.append(jnp.where(high, now, below))
            continue
        keep = jnp.where(upper, 1.0, jnp.exp(-rate * partner[b]))
        add = jnp.where(upper, jnp.exp(-rate * mine), 1.0)
        whole = keep * old_total[b] + add * theirs
        before[b] = now
        total[b] = whole
        values.append(whole)
        spans.append(mine + partner[b])
        meta[0, b : b + 1] = mine + partner[b]
        meta[1, b : b + 1] = prefix + jnp.where(upper, partner[b], 0.0)
        meta[2, b : b + 1] = old_meta[2, b : b + 1]
    send(outgoing, values, spans)


def incoming_edges_kernel(width, incoming, other, ring, swap):
    half, cells, _ = incoming.shape
    even = even_strip()
    last = cells - width
    for dest, start in ((ring, jnp.where(even, 0, last)), (swap, jnp.where(even, last, 0))):
        at = pl.ds(aligned(start, width), width)
        for b in range(half):
            dest[b] = incoming[b, at, :].astype(BF16)
            dest[half + b] = other[b, at, :]


def gelu(x):
    return 0.5 * x * (1.0 + lax.erf(x * 0.7071067811865476))


def mix_kernel(part, width, incoming, local, table, weight, video, inner, outer, framed):
    half, frames, cells, states = local.shape
    channels = video.shape[3]
    first = part * half
    for b in range(half):
        more = incoming[b].astype(F32)
        for t in range(frames):
            product = table[first + b, 2 * frames + t : 2 * frames + t + 1]
            put(framed, (pl.ds((b * frames + t) * cells, cells),), local[b, t] + product * more, width)
    less = cells - width
    for b in range(half):
        block = framed[pl.ds(b * frames * cells, frames * cells), :]
        frame = block.reshape(frames, cells, 3 * states)
        total = jnp.dot(block, weight[1], preferred_element_type=F32).reshape(frames, cells, channels)
        above = jnp.dot(frame[:, :less].reshape(-1, 3 * states), weight[0], preferred_element_type=F32).reshape(frames, less, channels)
        below = jnp.dot(frame[:, width:].reshape(-1, 3 * states), weight[2], preferred_element_type=F32).reshape(frames, less, channels)
        outer[0, b] = total[:, :width] + below[:, :width]
        outer[1, b] = total[:, less:] + above[:, less - width :]
        middle = total[:, width:less] + above[:, : less - width] + below[:, width:]
        inner[b] = (video[first + b, :, width:less].astype(F32) + gelu(middle)).astype(BF16)


def finish_kernel(side, width, *refs):
    if side == 0:
        outer_own, outer_other, halo_local, halo_in, table, weight, video, inner_own, inner_other, out, framed, edge, sems = refs
    else:
        outer_own, outer_other, halo_local, halo_in, table, weight, video, _, out, framed, edge, sems = refs
    batch, frames, cells, channels = out.shape
    half = batch // 2
    first = lanes(half)
    copies = []
    if side == 0:
        for lane, inner in enumerate((inner_own, inner_other)):
            dest = out.at[pl.ds(first[lane], half), :, pl.ds(width, cells - 2 * width), :]
            copies.append(pltpu.make_async_copy(inner, dest, sems.at[2 + lane]))
            copies[-1].start()

    def product(b, t):
        return table[b, 2 * frames + t : 2 * frames + t + 1]

    even = even_strip()
    below = even if side == 0 else jnp.logical_not(even)
    below = below.astype(jnp.int32)
    x = halo_block(0, batch, halo_local, product, halo_in)
    if side == 1:
        x = jnp.where(ring_open(), x, jnp.zeros_like(x))
    put(framed, (slice(None),), x, width)
    more = jnp.dot(framed[...], weight[2 * below], preferred_element_type=F32).reshape(batch, frames, width, channels)
    row = aligned(below * (cells - width), width)
    for lane, outer in enumerate((outer_own, outer_other)):
        at = slice(lane * half, (lane + 1) * half)
        mixed = outer[below] + more[at]
        edge[at] = (video[at, :, pl.ds(row, width), :].astype(F32) + gelu(mixed)).astype(BF16)
        copies.append(pltpu.make_async_copy(edge.at[at], out.at[pl.ds(first[lane], half), :, pl.ds(row, width), :], sems.at[lane]))
        copies[-1].start()
    for copy in copies:
        copy.wait()


def on_device(video, weight_in, weight_out, rates, gaps):
    batch, frames, rows, width, channels = video.shape
    states = weight_in.shape[3]
    half = batch // 2
    cells = rows * width
    blocks = lax.axis_size("tm")
    strips = lax.axis_size("rows")
    rounds = blocks.bit_length() - 1
    swap = [(i, i ^ 1) for i in range(strips)]
    ring = [(i, (i + 1 if i % 2 else i - 1) % strips) for i in range(strips)]

    def across(bit):
        mask = 1 if bit == 0 else 2 ** (bit + 1) - 2
        return [(i, i ^ mask) for i in range(blocks)]

    def in_hbm(x):
        return pltpu.with_memory_space_constraint(x, pltpu.HBM)

    video = in_hbm(video.reshape(batch, frames, cells, channels))
    weight_in = in_hbm(weight_in.reshape(3, 3 * channels, states))
    weight_out = weight_out.reshape(3, 3 * states, channels)
    edge_flops = 2 * batch * frames * width * 6 * channels * states
    own_flops = 5 * edge_flops

    edge = like(batch, frames, width, channels, dtype=BF16)
    ring_video, swap_video = call(
        functools.partial(edges_kernel, width), [video], [edge, edge], [pltpu.SemaphoreType.DMA((2, 2))], [HBM]
    )
    ring_video = lax.ppermute(ring_video, "rows", ring)
    swap_video = lax.ppermute(swap_video, "rows", swap)

    driven, table, weight, video = call(
        functools.partial(own_kernel, width), [in_hbm(gaps), in_hbm(rates[None, :]), video, weight_in],
        [like(batch, frames, cells, states), like(batch, table_rows(frames), states), like(*weight_in.shape, dtype=BF16), like(*video.shape, dtype=BF16)],
        [
            pltpu.VMEM((batch * frames * cells, 3 * channels), BF16),
            pltpu.SMEM(gaps.shape, F32),
            pltpu.VMEM((1, states), F32),
            pltpu.SemaphoreType.DMA((7,)),
        ],
        [HBM] * 4, mib=24, flops=own_flops,
    )
    extra = -(-3 * half // 16) * 16
    message = like(half * cells + extra, states, dtype=BF16)
    local = like(half, frames, cells, states)
    end = like(half, cells, states)
    meta = like(3, 8, states)
    halo = like(batch, frames, width, states, dtype=BF16)
    framed = [pltpu.VMEM((2, half * frames * width, 3 * channels), BF16)]
    common = [driven, table, weight, swap_video, ring_video]
    local_other, outgoing = call(
        functools.partial(scan_kernel, 1, width), common, [local, message], framed, flops=edge_flops // 2
    )
    incoming = lax.ppermute(outgoing, "tm", across(0))
    local_own, own_end, ring_local, swap_local = call(
        functools.partial(scan_kernel, 0, width), common + [local_other], [local, end, halo, halo], framed, flops=edge_flops // 2
    )
    ring_local = lax.ppermute(ring_local, "rows", ring)
    swap_local = lax.ppermute(swap_local, "rows", swap)

    low, total, outgoing, spans = call(
        functools.partial(pair_kernel, frames), [incoming, own_end, table], [end, end, message, meta]
    )
    before = []
    for bit in range(1, rounds):
        incoming = lax.ppermute(outgoing, "tm", across(bit))
        last = bit == rounds - 1
        kernel = functools.partial(join_kernel, frames, bit, bit == 1, last)
        args = [incoming, table, total, spans] + before
        if last:
            incoming_own, outgoing = call(kernel, args + [low], [end, like(half * cells, states, dtype=BF16)])
        else:
            now, total, outgoing, spans = call(kernel, args, [end, end, message, meta])
            before = [now]
    incoming_other = lax.ppermute(outgoing, "tm", across(0)).reshape(half, cells, states)

    def mix(part, incoming, local, flops):
        return call(
            functools.partial(mix_kernel, part, width), [incoming, local, table, weight_out, video],
            [like(half, frames, cells - 2 * width, channels, dtype=BF16), like(2, half, frames, width, channels)],
            [pltpu.VMEM((half * frames * cells, 3 * states), BF16)], mib=16, flops=flops,
        )

    inner_own, outer_own = mix(0, incoming_own, local_own, own_flops // 2)
    edge = like(batch, width, states, dtype=BF16)
    ring_in, swap_in = call(
        functools.partial(incoming_edges_kernel, width), [incoming_own, incoming_other], [edge, edge]
    )
    ring_in = lax.ppermute(ring_in, "rows", ring)
    swap_in = lax.ppermute(swap_in, "rows", swap)
    inner_other, outer_other = mix(1, incoming_other, local_other, own_flops // 2)

    def finish(side, halo_local, halo_in, more, specs, aliases):
        return pl.pallas_call(
            functools.partial(finish_kernel, side, width),
            out_shape=like(batch, frames, cells, channels, dtype=BF16),
            in_specs=[VMEM] * 7 + specs,
            out_specs=HBM,
            scratch_shapes=[
                pltpu.VMEM((batch * frames * width, 3 * states), BF16),
                pltpu.VMEM((batch, frames, width, channels), BF16),
                pltpu.SemaphoreType.DMA((4,)),
            ],
            input_output_aliases=aliases,
            compiler_params=pltpu.CompilerParams(vmem_limit_bytes=16 << 20),
            cost_estimate=pl.CostEstimate(flops=edge_flops // 2, bytes_accessed=1 << 20, transcendentals=0),
        )(outer_own, outer_other, halo_local, halo_in, table, weight_out, video, *more)

    out = finish(0, swap_local, swap_in, [inner_own, inner_other], [VMEM, VMEM], {})
    out = finish(1, ring_local, ring_in, [out], [HBM], {7: 0})
    return out.reshape(batch, frames, rows, width, channels)


def solution(mesh):
    in_specs = (P(None, "tm", "rows", None, None), P(), P(), P(), P(None, "tm"))
    out_specs = P(None, "tm", "rows", None, None)

    return jax.shard_map(on_device, mesh=mesh, in_specs=in_specs, out_specs=out_specs, check_vma=False)
```

```python
import functools

import jax
import jax.numpy as jnp
from jax import lax
from jax.experimental import pallas as pl
from jax.experimental.pallas import tpu as pltpu
from jax.sharding import PartitionSpec as P


F32 = jnp.float32
BF16 = jnp.bfloat16
SMEM = pl.BlockSpec(memory_space=pltpu.SMEM)
VMEM = pl.BlockSpec(memory_space=pltpu.VMEM)
HBM = pl.BlockSpec(memory_space=pltpu.HBM)


def call(kernel, args, outs, scratch=(), specs=None, mib=8, flops=1 << 20, bytes_accessed=1 << 20):
    return pl.pallas_call(
        kernel,
        out_shape=outs,
        in_specs=specs or [VMEM] * len(args),
        out_specs=[VMEM] * len(outs),
        scratch_shapes=list(scratch),
        compiler_params=pltpu.CompilerParams(vmem_limit_bytes=mib << 20),
        cost_estimate=pl.CostEstimate(flops=flops, bytes_accessed=bytes_accessed, transcendentals=0),
    )(*args)


def like(*shape, dtype=F32):
    return jax.ShapeDtypeStruct(shape, dtype)


def even_strip():
    return lax.axis_index("rows") % 2 == 0


def aligned(start, step):
    return pl.multiple_of(start, step)


def with_shifts(x, width):
    rows = x.shape[0]
    x = x.astype(F32)
    column = lax.broadcasted_iota(jnp.int32, (rows, 1), 0) % width
    left = jnp.where(column == 0, 0.0, pltpu.roll(x, 1, 0))
    right = jnp.where(column == width - 1, 0.0, pltpu.roll(x, rows - 1, 0))
    return left.astype(BF16), x.astype(BF16), right.astype(BF16)


def put(dest, index, x, width):
    c = x.shape[1]
    for i, part in enumerate(with_shifts(x, width)):
        dest[index + (slice(i * c, (i + 1) * c),)] = part


def span_tile(spans):
    rows = []
    for span in spans:
        high = span.astype(BF16).astype(F32)
        rest = span - high
        middle = rest.astype(BF16).astype(F32)
        rows += [high, middle, rest - middle]
    total = -(-len(rows) // 16) * 16
    index = lax.broadcasted_iota(jnp.int32, (total, rows[0].shape[1]), 0)
    tile = jnp.zeros(index.shape, F32)
    for i, row in enumerate(rows):
        tile = jnp.where(index == i, row, tile)
    return tile.astype(BF16)


def spans_of(tile, half):
    tile = tile.astype(F32)
    return [tile[3 * b : 3 * b + 1] + tile[3 * b + 1 : 3 * b + 2] + tile[3 * b + 2 : 3 * b + 3] for b in range(half)]


def lanes(half):
    high = lax.axis_index("tm") % 2
    return high * half, (1 - high) * half


def edges_kernel(width, video_hbm, weight_hbm, ring, swap, video, middle, sems):
    half = video.shape[0] // 2
    last = video.shape[2] - width
    even = even_strip()
    copies = [
        pltpu.make_async_copy(video_hbm.at[pl.ds(first, half)], video.at[pl.ds(lane * half, half)], sems.at[lane])
        for lane, first in enumerate(lanes(half))
    ]
    copies.append(pltpu.make_async_copy(weight_hbm.at[1], middle, sems.at[2]))
    for copy in copies:
        copy.start()
    for copy in copies[:2]:
        copy.wait()
    for start, dest in ((jnp.where(even, 0, last), ring), (jnp.where(even, last, 0), swap)):
        dest[...] = video[:, :, pl.ds(aligned(start, width), width), :]
    copies[2].wait()


def own_kernel(width, gaps_hbm, rates_hbm, weight_hbm, video, middle, driven, table, outer, framed, gaps, rates, sems):
    half, frames, cells, states = driven.shape
    batch, channels = video.shape[0], video.shape[3]
    first = lanes(half)
    copies = [pltpu.make_async_copy(weight_hbm.at[2 * d], outer.at[d], sems.at[d]) for d in range(2)]
    copies += [pltpu.make_async_copy(gaps_hbm, gaps, sems.at[2]), pltpu.make_async_copy(rates_hbm, rates, sems.at[3])]
    for copy in copies:
        copy.start()
    for b in range(half):
        put(framed, (pl.ds(b * frames * cells, frames * cells),), video[half + b].reshape(frames * cells, channels), width)
    less = cells - width
    block = framed[...]
    frame = block.reshape(half * frames, cells, 3 * channels)
    total = jnp.dot(block, middle[...], preferred_element_type=F32)
    driven[...] = total.reshape(half, frames, cells, states)
    copies[0].wait()
    above = jnp.dot(frame[:, :less].reshape(-1, 3 * channels), outer[0], preferred_element_type=F32)
    driven[:, :, width:, :] += above.reshape(half, frames, less, states)
    copies[1].wait()
    below = jnp.dot(frame[:, width:].reshape(-1, 3 * channels), outer[1], preferred_element_type=F32)
    driven[:, :, :less, :] += below.reshape(half, frames, less, states)
    for copy in copies[2:]:
        copy.wait()
    rate = rates[...]
    for b in range(batch):
        span = None
        for t in range(frames):
            gap = gaps[first[b // half] + b % half, t]
            span = gap if span is None else span + gap
            decay = jnp.exp(-rate * gap)
            table[b, t : t + 1] = decay
            table[b, frames + t : frames + t + 1] = jnp.sqrt(1.0 - decay * decay)
            table[b, 2 * frames + t : 2 * frames + t + 1] = jnp.exp(-rate * span)
        table[b, 3 * frames : 3 * frames + 1] = jnp.zeros((1, states), F32) + span
        table[b, 3 * frames + 1 : 3 * frames + 2] = rate


def table_rows(frames):
    return -(-(3 * frames + 2) // 8) * 8


def ring_open():
    strip = lax.axis_index("rows")
    return jnp.logical_and(strip != 0, strip != lax.axis_size("rows") - 1)


def halo_block(first, half, halo, product=None, incoming=None):
    frames, width, c = halo.shape[1:]
    x = halo[first : first + half]
    if product is None:
        return x.reshape(half * frames * width, c)
    pieces = []
    for b in range(half):
        more = incoming[first + b].astype(F32)
        pieces += [x[b, t].astype(F32) + product(b, t) * more for t in range(frames)]
    return jnp.concatenate(pieces, axis=0)


def recurrence(width, b, at, table, local, value_of, done):
    frames, cells = local.shape[1:3]
    for r in range(0, cells, width):
        state = None
        for t in range(frames):
            value = table[at, frames + t : frames + t + 1] * value_of(t, r)
            state = value if state is None else table[at, t : t + 1] * state + value
            local[b, t, r : r + width] = state
        done(r, state)


def scan_other_kernel(width, driven, table, outer, swap, ring, local, message, framed):
    half, frames, cells, _ = local.shape
    even = even_strip().astype(jnp.int32)
    put(framed, (even, slice(None)), halo_block(half, half, swap), width)
    x = halo_block(half, half, ring)
    put(framed, (1 - even, slice(None)), jnp.where(ring_open(), x, jnp.zeros_like(x)), width)
    top = jnp.dot(framed[0], outer[0], preferred_element_type=F32)
    bottom = jnp.dot(framed[1], outer[1], preferred_element_type=F32)
    for b in range(half):

        def value_of(t, r):
            value = driven[b, t, r : r + width]
            at = (b * frames + t) * width
            if r == 0:
                value = value + top[at : at + width]
            if r == cells - width:
                value = value + bottom[at : at + width]
            return value

        def done(r, state):
            message[b * cells + r : b * cells + r + width] = state.astype(BF16)

        recurrence(width, b, half + b, table, local, value_of, done)
    tile = span_tile([table[half + b, 3 * frames : 3 * frames + 1] for b in range(half)])
    message[half * cells : half * cells + tile.shape[0]] = tile


def scan_own_kernel(width, video, middle, outer, table, swap, ring, other, local, end, ring_out, swap_out, framed):
    half, frames, cells, states = local.shape
    channels = video.shape[3]
    even = even_strip()
    last = cells - width
    swap_at = aligned(jnp.where(even, cells + width, 0), width)
    ring_at = aligned(jnp.where(even, 0, cells + width), width)
    open_ring = ring_open()
    for b in range(half):
        for t in range(frames):
            f = b * frames + t
            put(framed, (f, pl.ds(width, cells)), video[b, t], width)
            put(framed, (f, pl.ds(swap_at, width)), swap[b, t], width)
            x = ring[b, t]
            put(framed, (f, pl.ds(ring_at, width)), jnp.where(open_ring, x, jnp.zeros_like(x)), width)
    for b in range(half):
        total = None
        for d, weight in enumerate((outer[0], middle[...], outer[1])):
            lhs = framed[b * frames : (b + 1) * frames, d * width : d * width + cells].reshape(frames * cells, 3 * channels)
            term = jnp.dot(lhs, weight, preferred_element_type=F32)
            total = term if total is None else total + term
        total = total.reshape(frames, cells, states)

        def value_of(t, r):
            return total[t, r : r + width]

        def done(r, state):
            end[b, r : r + width] = state

        recurrence(width, b, b, table, local, value_of, done)
    for source, at in ((local, 0), (other, half)):
        for dest, start in ((ring_out, jnp.where(even, 0, last)), (swap_out, jnp.where(even, last, 0))):
            for b in range(half):
                dest[at + b] = source[b, :, pl.ds(aligned(start, width), width), :].astype(BF16)


def send(outgoing, values, spans):
    for b, value in enumerate(values):
        cells = value.shape[0]
        outgoing[b * cells : (b + 1) * cells] = value.astype(BF16)
    if spans:
        tile = span_tile(spans)
        outgoing[len(values) * cells : len(values) * cells + tile.shape[0]] = tile


def pair_kernel(frames, message, end, table, low, total, outgoing, meta):
    half, cells, _ = end.shape
    high = lax.axis_index("tm") % 2 == 1
    partner = spans_of(message[half * cells :, :], half)
    meta[...] = jnp.zeros_like(meta)
    values, spans = [], []
    for b in range(half):
        rate = table[b, 3 * frames + 1 : 3 * frames + 2]
        mine = table[b, 3 * frames : 3 * frames + 1]
        theirs = message[b * cells : (b + 1) * cells].astype(F32)
        keep = jnp.where(high, 1.0, jnp.exp(-rate * partner[b]))
        add = jnp.where(high, jnp.exp(-rate * mine), 1.0)
        whole = keep * end[b] + add * theirs
        low[b] = jnp.where(high, theirs, end[b])
        total[b] = whole
        values.append(whole)
        spans.append(mine + partner[b])
        meta[0, b : b + 1] = mine + partner[b]
        meta[2, b : b + 1] = jnp.where(high, partner[b], mine)
    send(outgoing, values, spans)


def join_kernel(frames, bit, first, last, message, table, old_total, old_meta, *refs):
    half, cells, _ = old_total.shape
    refs = list(refs)
    old_before = None if first else refs.pop(0)
    if last:
        low, incoming, outgoing = refs
    else:
        before, total, outgoing, meta = refs
        meta[...] = jnp.zeros_like(meta)
    place = lax.axis_index("tm")
    upper = (place >> bit) % 2 == 1
    high = place % 2 == 1
    partner = spans_of(message[half * cells :, :], half)
    values, spans = [], []
    for b in range(half):
        rate = table[b, 3 * frames + 1 : 3 * frames + 2]
        theirs = message[b * cells : (b + 1) * cells].astype(F32)
        mine = old_meta[0, b : b + 1]
        prefix = old_meta[1, b : b + 1]
        now = jnp.where(upper, jnp.exp(-rate * prefix), 0.0) * theirs
        if not first:
            now = now + old_before[b]
        if last:
            below = jnp.exp(-rate * old_meta[2, b : b + 1]) * now + low[b]
            incoming[b] = jnp.where(high, below, now)
            values.append(jnp.where(high, now, below))
            continue
        keep = jnp.where(upper, 1.0, jnp.exp(-rate * partner[b]))
        add = jnp.where(upper, jnp.exp(-rate * mine), 1.0)
        whole = keep * old_total[b] + add * theirs
        before[b] = now
        total[b] = whole
        values.append(whole)
        spans.append(mine + partner[b])
        meta[0, b : b + 1] = mine + partner[b]
        meta[1, b : b + 1] = prefix + jnp.where(upper, partner[b], 0.0)
        meta[2, b : b + 1] = old_meta[2, b : b + 1]
    send(outgoing, values, spans)


def incoming_edges_kernel(width, incoming, other, ring, swap):
    half, cells, _ = incoming.shape
    even = even_strip()
    last = cells - width
    for dest, start in ((ring, jnp.where(even, 0, last)), (swap, jnp.where(even, last, 0))):
        at = pl.ds(aligned(start, width), width)
        for b in range(half):
            dest[b] = incoming[b, at, :].astype(BF16)
            dest[half + b] = other[b, at, :]


def gelu(x):
    return 0.5 * x * (1.0 + lax.erf(x * 0.7071067811865476))


def mix_kernel(part, width, incoming, local, table, weight, video, inner, outer, framed):
    half, frames, cells, states = local.shape
    channels = video.shape[3]
    first = part * half
    for b in range(half):
        more = incoming[b].astype(F32)
        for t in range(frames):
            product = table[first + b, 2 * frames + t : 2 * frames + t + 1]
            put(framed, (pl.ds((b * frames + t) * cells, cells),), local[b, t] + product * more, width)
    less = cells - width
    for b in range(half):
        block = framed[pl.ds(b * frames * cells, frames * cells), :]
        frame = block.reshape(frames, cells, 3 * states)
        total = jnp.dot(block, weight[1], preferred_element_type=F32).reshape(frames, cells, channels)
        above = jnp.dot(frame[:, :less].reshape(-1, 3 * states), weight[0], preferred_element_type=F32).reshape(frames, less, channels)
        below = jnp.dot(frame[:, width:].reshape(-1, 3 * states), weight[2], preferred_element_type=F32).reshape(frames, less, channels)
        outer[0, b] = total[:, :width] + below[:, :width]
        outer[1, b] = total[:, less:] + above[:, less - width :]
        middle = total[:, width:less] + above[:, : less - width] + below[:, width:]
        inner[b] = (video[first + b, :, width:less].astype(F32) + gelu(middle)).astype(BF16)


def edge_rows(side, width, outer_own, outer_other, halo_local, halo_in, table, weight, video, framed, edge, then):
    batch, frames, cells, channels = video.shape
    half = batch // 2

    def product(b, t):
        return table[b, 2 * frames + t : 2 * frames + t + 1]

    even = even_strip()
    below = even if side == 0 else jnp.logical_not(even)
    below = below.astype(jnp.int32)
    x = halo_block(0, batch, halo_local, product, halo_in)
    if side == 1:
        x = jnp.where(ring_open(), x, jnp.zeros_like(x))
    put(framed, (slice(None),), x, width)
    more = jnp.dot(framed[...], weight[2 * below], preferred_element_type=F32).reshape(batch, frames, width, channels)
    row = aligned(below * (cells - width), width)
    for lane, outer in enumerate((outer_own, outer_other)):
        at = slice(lane * half, (lane + 1) * half)
        mixed = outer[below] + more[at]
        edge[at] = (video[at, :, pl.ds(row, width), :].astype(F32) + gelu(mixed)).astype(BF16)
        then(lane, row)


def finish_swap_kernel(width, outer_own, outer_other, halo_local, halo_in, table, weight, video, edge, framed):
    edge_rows(0, width, outer_own, outer_other, halo_local, halo_in, table, weight, video, framed, edge, lambda lane, row: None)


def finish_ring_kernel(
    width, outer_own, outer_other, halo_local, halo_in, table, weight, video, inner_own, inner_other, done, out, framed, edge, sems
):
    batch, _, cells, _ = video.shape
    half = batch // 2
    first = lanes(half)
    copies = []

    def write(source, lane, row, count, kind):
        dest = out.at[pl.ds(first[lane], half), :, pl.ds(row, count), :]
        copies.append(pltpu.make_async_copy(source, dest, sems.at[kind, lane]))
        copies[-1].start()

    swap_row = aligned(even_strip().astype(jnp.int32) * (cells - width), width)
    for lane, inner in enumerate((inner_own, inner_other)):
        write(inner, lane, width, cells - 2 * width, 0)
        write(done.at[pl.ds(lane * half, half)], lane, swap_row, width, 1)

    def then(lane, row):
        write(edge.at[pl.ds(lane * half, half)], lane, row, width, 2)

    edge_rows(1, width, outer_own, outer_other, halo_local, halo_in, table, weight, video, framed, edge, then)
    for copy in copies:
        copy.wait()


def on_device(video, weight_in, weight_out, rates, gaps):
    batch, frames, rows, width, channels = video.shape
    states = weight_in.shape[3]
    half = batch // 2
    cells = rows * width
    blocks = lax.axis_size("tm")
    strips = lax.axis_size("rows")
    rounds = blocks.bit_length() - 1
    swap = [(i, i ^ 1) for i in range(strips)]

    def ring_partner(block, strip):
        if strip in (0, strips - 1):
            return block ^ 1, strip
        return block, strip + 1 if strip % 2 else strip - 1

    places = [(block, strip) for block in range(blocks) for strip in range(strips)]
    ring = [(place[0] * strips + place[1], partner[0] * strips + partner[1]) for place in places for partner in [ring_partner(*place)]]

    def across(bit):
        mask = 1 if bit == 0 else 2 ** (bit + 1) - 2
        return [(i, i ^ mask) for i in range(blocks)]

    def in_hbm(x):
        return pltpu.with_memory_space_constraint(x, pltpu.HBM)

    video = in_hbm(video.reshape(batch, frames, cells, channels))
    weight_in = in_hbm(weight_in.reshape(3, 3 * channels, states))
    weight_out = weight_out.reshape(3, 3 * states, channels)
    edge_flops = 2 * batch * frames * width * 6 * channels * states
    own_flops = 5 * edge_flops

    edge = like(batch, frames, width, channels, dtype=BF16)
    ring_video, swap_video, video, middle = call(
        functools.partial(edges_kernel, width), [video, weight_in],
        [edge, edge, like(*video.shape, dtype=BF16), like(*weight_in.shape[1:], dtype=BF16)],
        [pltpu.SemaphoreType.DMA((3,))], [HBM, HBM],
    )
    ring_video = lax.ppermute(ring_video, ("tm", "rows"), ring)
    swap_video = lax.ppermute(swap_video, "rows", swap)

    local = like(half, frames, cells, states)
    driven, table, outer = call(
        functools.partial(own_kernel, width), [in_hbm(gaps), in_hbm(rates[None, :]), weight_in, video, middle],
        [local, like(batch, table_rows(frames), states), like(2, *weight_in.shape[1:], dtype=BF16)],
        [
            pltpu.VMEM((half * frames * cells, 3 * channels), BF16),
            pltpu.SMEM(gaps.shape, F32),
            pltpu.VMEM((1, states), F32),
            pltpu.SemaphoreType.DMA((4,)),
        ],
        [HBM] * 3 + [VMEM] * 2, mib=16, flops=own_flops // 2,
    )
    extra = -(-3 * half // 16) * 16
    message = like(half * cells + extra, states, dtype=BF16)
    end = like(half, cells, states)
    meta = like(3, 8, states)
    halo = like(batch, frames, width, states, dtype=BF16)
    local_other, outgoing = call(
        functools.partial(scan_other_kernel, width), [driven, table, outer, swap_video, ring_video], [local, message],
        [pltpu.VMEM((2, half * frames * width, 3 * channels), BF16)], flops=edge_flops // 2,
    )
    incoming = lax.ppermute(outgoing, "tm", across(0))
    local_own, own_end, ring_local, swap_local = call(
        functools.partial(scan_own_kernel, width), [video, middle, outer, table, swap_video, ring_video, local_other],
        [local, end, halo, halo], [pltpu.VMEM((half * frames, cells + 2 * width, 3 * channels), BF16)], mib=16, flops=own_flops // 2,
    )
    ring_local = lax.ppermute(ring_local, ("tm", "rows"), ring)
    swap_local = lax.ppermute(swap_local, "rows", swap)

    low, total, outgoing, spans = call(
        functools.partial(pair_kernel, frames), [incoming, own_end, table], [end, end, message, meta]
    )
    before = []
    for bit in range(1, rounds):
        incoming = lax.ppermute(outgoing, "tm", across(bit))
        last = bit == rounds - 1
        kernel = functools.partial(join_kernel, frames, bit, bit == 1, last)
        args = [incoming, table, total, spans] + before
        if last:
            incoming_own, outgoing = call(kernel, args + [low], [end, like(half * cells, states, dtype=BF16)])
        else:
            now, total, outgoing, spans = call(kernel, args, [end, end, message, meta])
            before = [now]
    incoming_other = lax.ppermute(outgoing, "tm", across(0)).reshape(half, cells, states)

    def mix(part, incoming, local, flops):
        return call(
            functools.partial(mix_kernel, part, width), [incoming, local, table, weight_out, video],
            [like(half, frames, cells - 2 * width, channels, dtype=BF16), like(2, half, frames, width, channels)],
            [pltpu.VMEM((half * frames * cells, 3 * states), BF16)], mib=16, flops=flops,
        )

    inner_own, outer_own = mix(0, incoming_own, local_own, own_flops // 2)
    edge = like(batch, width, states, dtype=BF16)
    ring_in, swap_in = call(
        functools.partial(incoming_edges_kernel, width), [incoming_own, incoming_other], [edge, edge]
    )
    ring_in = lax.ppermute(ring_in, ("tm", "rows"), ring)
    swap_in = lax.ppermute(swap_in, "rows", swap)
    inner_other, outer_other = mix(1, incoming_other, local_other, own_flops // 2)

    common = [outer_own, outer_other]
    framed = pltpu.VMEM((batch * frames * width, 3 * states), BF16)
    edge = like(batch, frames, width, channels, dtype=BF16)
    done, = call(
        functools.partial(finish_swap_kernel, width), common + [swap_local, swap_in, table, weight_out, video],
        [edge], [framed], mib=16, flops=edge_flops // 2,
    )
    out = pl.pallas_call(
        functools.partial(finish_ring_kernel, width),
        out_shape=like(batch, frames, cells, channels, dtype=BF16),
        in_specs=[VMEM] * 10,
        out_specs=HBM,
        scratch_shapes=[framed, pltpu.VMEM(edge.shape, BF16), pltpu.SemaphoreType.DMA((3, 2))],
        name="finish_ring",
        compiler_params=pltpu.CompilerParams(vmem_limit_bytes=16 << 20),
        cost_estimate=pl.CostEstimate(flops=edge_flops // 2, bytes_accessed=1 << 20, transcendentals=0),
    )(*common, ring_local, ring_in, table, weight_out, video, inner_own, inner_other, done)
    return out.reshape(batch, frames, rows, width, channels)


def solution(mesh):
    in_specs = (P(None, "tm", "rows", None, None), P(), P(), P(), P(None, "tm"))
    out_specs = P(None, "tm", "rows", None, None)

    return jax.shard_map(on_device, mesh=mesh, in_specs=in_specs, out_specs=out_specs, check_vma=False)
```

```python
import functools

import jax
import jax.numpy as jnp
from jax import lax
from jax.experimental import pallas as pl
from jax.experimental.pallas import tpu as pltpu
from jax.sharding import PartitionSpec as P


F32 = jnp.float32
BF16 = jnp.bfloat16
SMEM = pl.BlockSpec(memory_space=pltpu.SMEM)
VMEM = pl.BlockSpec(memory_space=pltpu.VMEM)
HBM = pl.BlockSpec(memory_space=pltpu.HBM)


def call(kernel, args, outs, scratch=(), specs=None, mib=8, flops=1 << 20, bytes_accessed=1 << 20):
    return pl.pallas_call(
        kernel,
        out_shape=outs,
        in_specs=specs or [VMEM] * len(args),
        out_specs=[VMEM] * len(outs),
        scratch_shapes=list(scratch),
        compiler_params=pltpu.CompilerParams(vmem_limit_bytes=mib << 20),
        cost_estimate=pl.CostEstimate(flops=flops, bytes_accessed=bytes_accessed, transcendentals=0),
    )(*args)


def like(*shape, dtype=F32):
    return jax.ShapeDtypeStruct(shape, dtype)


def even_strip():
    return lax.axis_index("rows") % 2 == 0


def aligned(start, step):
    return pl.multiple_of(start, step)


def with_shifts(x, width):
    rows = x.shape[0]
    x = x.astype(F32)
    column = lax.broadcasted_iota(jnp.int32, (rows, 1), 0) % width
    left = jnp.where(column == 0, 0.0, pltpu.roll(x, 1, 0))
    right = jnp.where(column == width - 1, 0.0, pltpu.roll(x, rows - 1, 0))
    return left.astype(BF16), x.astype(BF16), right.astype(BF16)


def put(dest, index, x, width):
    c = x.shape[1]
    for i, part in enumerate(with_shifts(x, width)):
        dest[index + (slice(i * c, (i + 1) * c),)] = part


def tile_rows(half):
    return -(-3 * half // 8) * 8


def span_tile(spans):
    rows = []
    for span in spans:
        high = span.astype(BF16).astype(F32)
        rest = span - high
        middle = rest.astype(BF16).astype(F32)
        rows += [high, middle, rest - middle]
    index = lax.broadcasted_iota(jnp.int32, (tile_rows(len(spans)), rows[0].shape[1]), 0)
    tile = jnp.zeros(index.shape, F32)
    for i, row in enumerate(rows):
        tile = jnp.where(index == i, row, tile)
    return tile.astype(BF16)


def spans_of(tile, half):
    tile = tile.astype(F32)
    return [tile[3 * b : 3 * b + 1] + tile[3 * b + 1 : 3 * b + 2] + tile[3 * b + 2 : 3 * b + 3] for b in range(half)]


def lanes(half):
    high = lax.axis_index("tm") % 2
    return high * half, (1 - high) * half


def edges_kernel(width, video_hbm, weight_hbm, ring, swap, video, weight, sems):
    half = video.shape[0] // 2
    last = video.shape[2] - width
    even = even_strip()
    copies = [
        pltpu.make_async_copy(video_hbm.at[pl.ds(first, half)], video.at[pl.ds(lane * half, half)], sems.at[lane])
        for lane, first in enumerate(lanes(half))
    ]
    copies.append(pltpu.make_async_copy(weight_hbm, weight, sems.at[2]))
    for copy in copies:
        copy.start()
    for copy in copies[:2]:
        copy.wait()
    for start, dest in ((jnp.where(even, 0, last), ring), (jnp.where(even, last, 0), swap)):
        dest[...] = video[:, :, pl.ds(aligned(start, width), width), :]
    copies[2].wait()


def own_kernel(width, gaps_hbm, rates_hbm, weight, video, local, driven, message, table, framed, full, gaps, rates, sems):
    half, frames, inner, states = local.shape
    batch, cells, channels = video.shape[0], video.shape[2], video.shape[3]
    first = lanes(half)
    copies = [pltpu.make_async_copy(gaps_hbm, gaps, sems.at[0]), pltpu.make_async_copy(rates_hbm, rates, sems.at[1])]
    for copy in copies:
        copy.start()
    for b in range(half):
        put(framed, (pl.ds(b * frames * cells, frames * cells),), video[half + b].reshape(frames * cells, channels), width)
    less = cells - width
    block = framed[...]
    frame = block.reshape(half * frames, cells, 3 * channels)
    total = jnp.dot(block, weight[1], preferred_element_type=F32)
    full[...] = total.reshape(half, frames, cells, states)
    above = jnp.dot(frame[:, :less].reshape(-1, 3 * channels), weight[0], preferred_element_type=F32)
    full[:, :, width:, :] += above.reshape(half, frames, less, states)
    below = jnp.dot(frame[:, width:].reshape(-1, 3 * channels), weight[2], preferred_element_type=F32)
    full[:, :, :less, :] += below.reshape(half, frames, less, states)
    for copy in copies:
        copy.wait()
    rate = rates[...]
    for b in range(batch):
        span = None
        for t in range(frames):
            gap = gaps[first[b // half] + b % half, t]
            span = gap if span is None else span + gap
            decay = jnp.exp(-rate * gap)
            table[b, t : t + 1] = decay
            table[b, frames + t : frames + t + 1] = jnp.sqrt(1.0 - decay * decay)
            table[b, 2 * frames + t : 2 * frames + t + 1] = jnp.exp(-rate * span)
        table[b, 3 * frames : 3 * frames + 1] = jnp.zeros((1, states), F32) + span
        table[b, 3 * frames + 1 : 3 * frames + 2] = rate
    for b in range(half):
        driven[b, :, :width] = full[b, :, :width]
        driven[b, :, width:] = full[b, :, less:]
        for r in range(0, inner, width):

            def value_of(t):
                return full[b, t, width + r : 2 * width + r]

            state = recurrence(b, half + b, slice(r, r + width), table, local, value_of)
            message[b * inner + r : b * inner + r + width] = state.astype(BF16)
    message[half * inner : half * inner + tile_rows(half)] = span_tile([table[half + b, 3 * frames : 3 * frames + 1] for b in range(half)])


def table_rows(frames):
    return -(-(3 * frames + 2) // 8) * 8


def ring_open():
    strip = lax.axis_index("rows")
    return jnp.logical_and(strip != 0, strip != lax.axis_size("rows") - 1)


def halo_block(first, half, halo, product=None, incoming=None):
    frames, width, c = halo.shape[1:]
    x = halo[first : first + half]
    if product is None:
        return x.reshape(half * frames * width, c)
    pieces = []
    for b in range(half):
        more = incoming[first + b].astype(F32)
        pieces += [x[b, t].astype(F32) + product(b, t) * more for t in range(frames)]
    return jnp.concatenate(pieces, axis=0)


def recurrence(b, at, rows, table, local, value_of):
    frames = local.shape[1]
    state = None
    for t in range(frames):
        value = table[at, frames + t : frames + t + 1] * value_of(t)
        state = value if state is None else table[at, t : t + 1] * state + value
        local[b, t, rows] = state
    return state


def scan_other_kernel(width, driven, table, weight, swap, ring, local, message, framed):
    half, frames = local.shape[:2]
    even = even_strip().astype(jnp.int32)
    put(framed, (even, slice(None)), halo_block(half, half, swap), width)
    x = halo_block(half, half, ring)
    put(framed, (1 - even, slice(None)), jnp.where(ring_open(), x, jnp.zeros_like(x)), width)
    for side in range(2):
        more = jnp.dot(framed[side], weight[2 * side], preferred_element_type=F32)
        rows = slice(side * width, (side + 1) * width)
        for b in range(half):

            def value_of(t):
                at = (b * frames + t) * width
                return driven[b, t, rows] + more[at : at + width]

            state = recurrence(b, half + b, rows, table, local, value_of)
            message[(2 * b + side) * width : (2 * b + side + 1) * width] = state.astype(BF16)


def scan_own_kernel(width, video, weight, table, swap, ring, other_outer, inner, outer, ring_out, swap_out, framed):
    half, frames = inner.shape[:2]
    cells, channels = video.shape[2:]
    states = inner.shape[3]
    even = even_strip()
    swap_at = aligned(jnp.where(even, cells + width, 0), width)
    ring_at = aligned(jnp.where(even, 0, cells + width), width)
    open_ring = ring_open()
    for b in range(half):
        for t in range(frames):
            f = b * frames + t
            put(framed, (f, pl.ds(width, cells)), video[b, t], width)
            put(framed, (f, pl.ds(swap_at, width)), swap[b, t], width)
            x = ring[b, t]
            put(framed, (f, pl.ds(ring_at, width)), jnp.where(open_ring, x, jnp.zeros_like(x)), width)
    for b in range(half):
        total = None
        for d in range(3):
            lhs = framed[b * frames : (b + 1) * frames, d * width : d * width + cells].reshape(frames * cells, 3 * channels)
            term = jnp.dot(lhs, weight[d], preferred_element_type=F32)
            total = term if total is None else total + term
        total = total.reshape(frames, cells, states)
        for r in range(0, cells, width):
            if r == 0:
                dest, rows = outer, slice(0, width)
            elif r == cells - width:
                dest, rows = outer, slice(width, 2 * width)
            else:
                dest, rows = inner, slice(r - width, r)
            recurrence(b, b, rows, table, dest, lambda t: total[t, r : r + width])
    for source, at in ((outer, 0), (other_outer, half)):
        for dest, start in ((ring_out, jnp.where(even, 0, width)), (swap_out, jnp.where(even, width, 0))):
            for b in range(half):
                dest[at + b] = source[b, :, pl.ds(aligned(start, width), width), :].astype(BF16)


SPAN, PREFIX, LOW, THEIRS, MINE, BEFORE = range(6)


def join_kernel(frames, inner, bit, combine, last, names, *refs):
    ref = dict(zip(names, refs))
    table, message = ref["table"], ref["message"]
    place = lax.axis_index("tm")
    upper = (place >> bit) % 2 == 1
    high = place % 2 == 1
    if last:
        join_last(frames, ref, upper, high)
        return
    new = ref["new_total"]
    half, count = new.shape[:2]
    if inner:
        partner = spans_of(message[half * count :, :], half)
        ref["new_meta"][...] = jnp.zeros_like(ref["new_meta"])
    spans = []
    for b in range(half):
        row = slice(b, b + 1)
        rate = table[b, 3 * frames + 1 : 3 * frames + 2]
        if inner:
            meta = ref["new_meta"]
            mine = table[b, 3 * frames : 3 * frames + 1] if bit == 0 else ref["meta"][SPAN, row]
            prefix = jnp.zeros_like(mine) if bit == 0 else ref["meta"][PREFIX, row]
            meta[MINE, row] = mine
            meta[BEFORE, row] = prefix
            meta[THEIRS, row] = partner[b]
            meta[SPAN, row] = mine + partner[b]
            if bit == 0:
                meta[LOW, row] = jnp.where(high, partner[b], mine)
            else:
                meta[LOW, row] = ref["meta"][LOW, row]
                meta[PREFIX, row] = prefix + jnp.where(upper, partner[b], 0.0)
            theirs_span = partner[b]
        else:
            meta = ref["meta"]
            mine, prefix, theirs_span = meta[MINE, row], meta[BEFORE, row], meta[THEIRS, row]
        spans.append(mine + theirs_span)
        theirs = message[b * count : (b + 1) * count].astype(F32)
        own = ref["local"][b, frames - 1] if bit == 0 else ref["total"][b]
        keep = jnp.where(upper, 1.0, jnp.exp(-rate * theirs_span))
        add = jnp.where(upper, jnp.exp(-rate * mine), 1.0)
        whole = keep * own + add * theirs
        new[b] = whole
        if bit == 0:
            ref["low"][b] = jnp.where(high, theirs, own)
        else:
            now = jnp.where(upper, jnp.exp(-rate * prefix), 0.0) * theirs
            ref["new_before"][b] = now if bit == 1 else ref["before"][b] + now
        if not combine:
            ref["outgoing"][b * count : (b + 1) * count] = whole.astype(BF16)
        elif not inner:
            many = ref["inner_total"].shape[1]
            ref["outgoing"][b * many : (b + 1) * many] = ref["inner_total"][b].astype(BF16)
            at = half * many + b * count
            ref["outgoing"][at : at + count] = whole.astype(BF16)
    if inner != combine:
        rows = ref["outgoing"].shape[0]
        ref["outgoing"][rows - tile_rows(half) : rows] = span_tile(spans)


def join_last(frames, ref, upper, high):
    message, meta = ref["message"], ref["meta"]
    half, many = ref["low_inner"].shape[:2]
    for b in range(half):
        row = slice(b, b + 1)
        rate = ref["table"][b, 3 * frames + 1 : 3 * frames + 2]
        scale = jnp.where(upper, jnp.exp(-rate * meta[PREFIX, row]), 0.0)
        low_decay = jnp.exp(-rate * meta[LOW, row])
        for kind in ("inner", "outer"):
            low = ref["low_" + kind]
            count = low.shape[1]
            at = b * count + (half * many if kind == "outer" else 0)
            now = scale * message[at : at + count].astype(F32)
            if "before_" + kind in ref:
                now = now + ref["before_" + kind][b]
            below = low_decay * now + low[b]
            ref["incoming_" + kind][b] = jnp.where(high, below, now)
            ref["back_" + kind][b] = jnp.where(high, now, below).astype(BF16)


def incoming_edges_kernel(width, own, other, ring, swap):
    half = own.shape[0]
    even = even_strip()
    for dest, start in ((ring, jnp.where(even, 0, width)), (swap, jnp.where(even, width, 0))):
        at = pl.ds(aligned(start, width), width)
        for b in range(half):
            dest[b] = own[b, at, :].astype(BF16)
            dest[half + b] = other[b, at, :]


def gelu(x):
    return 0.5 * x * (1.0 + lax.erf(x * 0.7071067811865476))


def mix_kernel(part, width, in_inner, in_outer, local_inner, local_outer, table, weight, video, inner, outer, framed):
    half, frames, _, states = local_inner.shape
    cells, channels = video.shape[2:]
    first = part * half
    for b in range(half):
        for t in range(frames):
            product = table[first + b, 2 * frames + t : 2 * frames + t + 1]
            at = (b * frames + t) * cells
            x = local_inner[b, t] + product * in_inner[b].astype(F32)
            put(framed, (pl.ds(at + width, cells - 2 * width),), x, width)
            x = local_outer[b, t] + product * in_outer[b].astype(F32)
            put(framed, (pl.ds(at, width),), x[:width], width)
            put(framed, (pl.ds(at + cells - width, width),), x[width:], width)
    less = cells - width
    for b in range(half):
        block = framed[pl.ds(b * frames * cells, frames * cells), :]
        frame = block.reshape(frames, cells, 3 * states)
        total = jnp.dot(block, weight[1], preferred_element_type=F32).reshape(frames, cells, channels)
        above = jnp.dot(frame[:, :less].reshape(-1, 3 * states), weight[0], preferred_element_type=F32).reshape(frames, less, channels)
        below = jnp.dot(frame[:, width:].reshape(-1, 3 * states), weight[2], preferred_element_type=F32).reshape(frames, less, channels)
        outer[0, b] = total[:, :width] + below[:, :width]
        outer[1, b] = total[:, less:] + above[:, less - width :]
        middle = total[:, width:less] + above[:, : less - width] + below[:, width:]
        inner[b] = (video[first + b, :, width:less].astype(F32) + gelu(middle)).astype(BF16)


def edge_rows(side, width, outer_own, outer_other, halo_local, halo_in, table, weight, video, framed, edge, then):
    batch, frames, cells, channels = video.shape
    half = batch // 2

    def product(b, t):
        return table[b, 2 * frames + t : 2 * frames + t + 1]

    even = even_strip()
    below = even if side == 0 else jnp.logical_not(even)
    below = below.astype(jnp.int32)
    x = halo_block(0, batch, halo_local, product, halo_in)
    if side == 1:
        x = jnp.where(ring_open(), x, jnp.zeros_like(x))
    put(framed, (slice(None),), x, width)
    more = jnp.dot(framed[...], weight[2 * below], preferred_element_type=F32).reshape(batch, frames, width, channels)
    row = aligned(below * (cells - width), width)
    for lane, outer in enumerate((outer_own, outer_other)):
        at = slice(lane * half, (lane + 1) * half)
        mixed = outer[below] + more[at]
        edge[at] = (video[at, :, pl.ds(row, width), :].astype(F32) + gelu(mixed)).astype(BF16)
        then(lane, row)


def finish_swap_kernel(width, outer_own, outer_other, halo_local, halo_in, table, weight, video, edge, framed):
    edge_rows(0, width, outer_own, outer_other, halo_local, halo_in, table, weight, video, framed, edge, lambda lane, row: None)


def finish_ring_kernel(
    width, outer_own, outer_other, halo_local, halo_in, table, weight, video, inner_own, inner_other, done, out, framed, edge, sems
):
    batch, _, cells, _ = video.shape
    half = batch // 2
    first = lanes(half)
    copies = []

    def write(source, lane, row, count, kind):
        dest = out.at[pl.ds(first[lane], half), :, pl.ds(row, count), :]
        copies.append(pltpu.make_async_copy(source, dest, sems.at[kind, lane]))
        copies[-1].start()

    swap_row = aligned(even_strip().astype(jnp.int32) * (cells - width), width)
    for lane, inner in enumerate((inner_own, inner_other)):
        write(inner, lane, width, cells - 2 * width, 0)
        write(done.at[pl.ds(lane * half, half)], lane, swap_row, width, 1)

    def then(lane, row):
        write(edge.at[pl.ds(lane * half, half)], lane, row, width, 2)

    edge_rows(1, width, outer_own, outer_other, halo_local, halo_in, table, weight, video, framed, edge, then)
    for copy in copies:
        copy.wait()


def on_device(video, weight_in, weight_out, rates, gaps):
    batch, frames, rows, width, channels = video.shape
    states = weight_in.shape[3]
    half = batch // 2
    cells = rows * width
    blocks = lax.axis_size("tm")
    strips = lax.axis_size("rows")
    rounds = blocks.bit_length() - 1
    swap = [(i, i ^ 1) for i in range(strips)]

    def ring_partner(block, strip):
        if strip in (0, strips - 1):
            return block ^ 1, strip
        return block, strip + 1 if strip % 2 else strip - 1

    places = [(block, strip) for block in range(blocks) for strip in range(strips)]
    ring = [(place[0] * strips + place[1], partner[0] * strips + partner[1]) for place in places for partner in [ring_partner(*place)]]

    def across(bit):
        mask = 1 if bit == 0 else 2 ** (bit + 1) - 2
        return [(i, i ^ mask) for i in range(blocks)]

    def in_hbm(x):
        return pltpu.with_memory_space_constraint(x, pltpu.HBM)

    video = in_hbm(video.reshape(batch, frames, cells, channels))
    weight_in = in_hbm(weight_in.reshape(3, 3 * channels, states))
    weight_out = weight_out.reshape(3, 3 * states, channels)
    edge_flops = 2 * batch * frames * width * 6 * channels * states
    own_flops = 5 * edge_flops

    edge = like(batch, frames, width, channels, dtype=BF16)
    ring_video, swap_video, video, weight = call(
        functools.partial(edges_kernel, width), [video, weight_in],
        [edge, edge, like(*video.shape, dtype=BF16), like(*weight_in.shape, dtype=BF16)],
        [pltpu.SemaphoreType.DMA((3,))], [HBM, HBM],
    )
    ring_video = lax.ppermute(ring_video, ("tm", "rows"), ring)
    swap_video = lax.ppermute(swap_video, "rows", swap)

    count = {"inner": cells - 2 * width, "outer": 2 * width}
    local = {kind: like(half, frames, n, states) for kind, n in count.items()}
    end = {kind: like(half, n, states) for kind, n in count.items()}
    message = {"inner": like(half * count["inner"] + tile_rows(half), states, dtype=BF16), "outer": like(half * count["outer"], states, dtype=BF16)}
    both = like(half * cells + tile_rows(half), states, dtype=BF16)
    rows_in_table = table_rows(frames)
    other = {}
    outgoing = {}
    other["inner"], driven, outgoing["inner"], table = call(
        functools.partial(own_kernel, width), [in_hbm(gaps), in_hbm(rates[None, :]), weight, video],
        [local["inner"], local["outer"], message["inner"], like(batch, rows_in_table, states)],
        [
            pltpu.VMEM((half * frames * cells, 3 * channels), BF16),
            pltpu.VMEM((half, frames, cells, states), F32),
            pltpu.SMEM(gaps.shape, F32),
            pltpu.VMEM((1, states), F32),
            pltpu.SemaphoreType.DMA((2,)),
        ],
        [HBM] * 2 + [VMEM] * 2, mib=16, flops=own_flops // 2,
    )
    meta_shape = like(6, 8, states)
    halo = like(batch, frames, width, states, dtype=BF16)
    incoming = {"inner": lax.ppermute(outgoing["inner"], "tm", across(0))}
    other["outer"], outgoing["outer"] = call(
        functools.partial(scan_other_kernel, width), [driven, table, weight, swap_video, ring_video],
        [local["outer"], message["outer"]], [pltpu.VMEM((2, half * frames * width, 3 * channels), BF16)], flops=edge_flops // 2,
    )
    incoming["outer"] = lax.ppermute(outgoing["outer"], "tm", across(0))
    own = {}
    own["inner"], own["outer"], ring_local, swap_local = call(
        functools.partial(scan_own_kernel, width), [video, weight, table, swap_video, ring_video, other["outer"]],
        [local["inner"], local["outer"], halo, halo], [pltpu.VMEM((half * frames, cells + 2 * width, 3 * channels), BF16)],
        mib=16, flops=own_flops // 2,
    )
    ring_local = lax.ppermute(ring_local, ("tm", "rows"), ring)
    swap_local = lax.ppermute(swap_local, "rows", swap)

    def join(inner, bit, combine, last, ins, outs):
        results = call(
            functools.partial(join_kernel, frames, inner, bit, combine, last, tuple(ins) + tuple(outs)), list(ins.values()), list(outs.values())
        )
        return dict(zip(outs, results))

    final = rounds - 1
    constant = {"table": table}
    total, before, low, meta = {}, {}, {}, None
    for bit in range(final):
        combine = bit + 1 == final
        for kind in ("inner", "outer"):
            inner = kind == "inner"
            ins = {"message": incoming[kind], **constant}
            outs = {"new_total": end[kind]}
            if bit == 0:
                ins["local"] = own[kind]
                outs["low"] = end[kind]
            else:
                ins["total"] = total[kind]
                outs["new_before"] = end[kind]
            if bit > 1:
                ins["before"] = before[kind]
            if bit or not inner:
                ins["meta"] = meta
            if inner:
                outs["new_meta"] = meta_shape
            if not combine:
                outs["outgoing"] = message[kind]
            elif not inner:
                ins["inner_total"] = total["inner"]
                outs["outgoing"] = both
            got = join(inner, bit, combine, False, ins, outs)
            total[kind] = got["new_total"]
            low[kind] = got.get("low", low.get(kind))
            before[kind] = got.get("new_before")
            meta = got.get("new_meta", meta)
            if not combine:
                incoming[kind] = lax.ppermute(got["outgoing"], "tm", across(bit + 1))
            elif not inner:
                incoming["both"] = lax.ppermute(got["outgoing"], "tm", across(final))
    ins = {"message": incoming["both"], **constant, "meta": meta}
    outs = {}
    for kind in ("inner", "outer"):
        ins["low_" + kind] = low[kind]
        if before[kind] is not None:
            ins["before_" + kind] = before[kind]
        outs["incoming_" + kind] = end[kind]
        outs["back_" + kind] = like(*end[kind].shape, dtype=BF16)
    got = join(True, final, True, True, ins, outs)
    into_own = {kind: got["incoming_" + kind] for kind in end}
    into_other = {kind: lax.ppermute(got["back_" + kind], "tm", across(0)) for kind in ("outer", "inner")}

    def mix(part, into, local, flops):
        return call(
            functools.partial(mix_kernel, part, width),
            [into["inner"], into["outer"], local["inner"], local["outer"], table, weight_out, video],
            [like(half, frames, cells - 2 * width, channels, dtype=BF16), like(2, half, frames, width, channels)],
            [pltpu.VMEM((half * frames * cells, 3 * states), BF16)], mib=16, flops=flops,
        )

    inner_own, outer_own = mix(0, into_own, own, own_flops // 2)
    edge = like(batch, width, states, dtype=BF16)
    ring_in, swap_in = call(
        functools.partial(incoming_edges_kernel, width), [into_own["outer"], into_other["outer"]], [edge, edge]
    )
    ring_in = lax.ppermute(ring_in, ("tm", "rows"), ring)
    swap_in = lax.ppermute(swap_in, "rows", swap)
    inner_other, outer_other = mix(1, into_other, other, own_flops // 2)
    common = [outer_own, outer_other]
    framed = pltpu.VMEM((batch * frames * width, 3 * states), BF16)
    edge = like(batch, frames, width, channels, dtype=BF16)
    done, = call(
        functools.partial(finish_swap_kernel, width), common + [swap_local, swap_in, table, weight_out, video],
        [edge], [framed], mib=16, flops=edge_flops // 2,
    )
    out = pl.pallas_call(
        functools.partial(finish_ring_kernel, width),
        out_shape=like(batch, frames, cells, channels, dtype=BF16),
        in_specs=[VMEM] * 10,
        out_specs=HBM,
        scratch_shapes=[framed, pltpu.VMEM(edge.shape, BF16), pltpu.SemaphoreType.DMA((3, 2))],
        name="finish_ring",
        compiler_params=pltpu.CompilerParams(vmem_limit_bytes=16 << 20),
        cost_estimate=pl.CostEstimate(flops=edge_flops // 2, bytes_accessed=1 << 20, transcendentals=0),
    )(*common, ring_local, ring_in, table, weight_out, video, inner_own, inner_other, done)
    return out.reshape(batch, frames, rows, width, channels)


def solution(mesh):
    in_specs = (P(None, "tm", "rows", None, None), P(), P(), P(), P(None, "tm"))
    out_specs = P(None, "tm", "rows", None, None)

    return jax.shard_map(on_device, mesh=mesh, in_specs=in_specs, out_specs=out_specs, check_vma=False)
```

```python
import functools

import jax
import jax.numpy as jnp
from jax import lax
from jax.experimental import pallas as pl
from jax.experimental.pallas import tpu as pltpu
from jax.sharding import PartitionSpec as P


F32 = jnp.float32
BF16 = jnp.bfloat16
SMEM = pl.BlockSpec(memory_space=pltpu.SMEM)
VMEM = pl.BlockSpec(memory_space=pltpu.VMEM)
HBM = pl.BlockSpec(memory_space=pltpu.HBM)


def call(kernel, args, outs, scratch=(), specs=None, mib=8, flops=1 << 20, bytes_accessed=1 << 20):
    return pl.pallas_call(
        kernel,
        out_shape=outs,
        in_specs=specs or [VMEM] * len(args),
        out_specs=[VMEM] * len(outs),
        scratch_shapes=list(scratch),
        compiler_params=pltpu.CompilerParams(vmem_limit_bytes=mib << 20),
        cost_estimate=pl.CostEstimate(flops=flops, bytes_accessed=bytes_accessed, transcendentals=0),
    )(*args)


def like(*shape, dtype=F32):
    return jax.ShapeDtypeStruct(shape, dtype)


def even_strip():
    return lax.axis_index("rows") % 2 == 0


def aligned(start, step):
    return pl.multiple_of(start, step)


def with_shifts(x, width):
    rows = x.shape[0]
    x = x.astype(F32)
    column = lax.broadcasted_iota(jnp.int32, (rows, 1), 0) % width
    left = jnp.where(column == 0, 0.0, pltpu.roll(x, 1, 0))
    right = jnp.where(column == width - 1, 0.0, pltpu.roll(x, rows - 1, 0))
    return left.astype(BF16), x.astype(BF16), right.astype(BF16)


def put(dest, index, x, width):
    c = x.shape[1]
    for i, part in enumerate(with_shifts(x, width)):
        dest[index + (slice(i * c, (i + 1) * c),)] = part


def tile_rows(half):
    return -(-3 * half // 8) * 8


def span_tile(spans):
    rows = []
    for span in spans:
        high = span.astype(BF16).astype(F32)
        rest = span - high
        middle = rest.astype(BF16).astype(F32)
        rows += [high, middle, rest - middle]
    index = lax.broadcasted_iota(jnp.int32, (tile_rows(len(spans)), rows[0].shape[1]), 0)
    tile = jnp.zeros(index.shape, F32)
    for i, row in enumerate(rows):
        tile = jnp.where(index == i, row, tile)
    return tile.astype(BF16)


def spans_of(tile, half):
    tile = tile.astype(F32)
    return [tile[3 * b : 3 * b + 1] + tile[3 * b + 1 : 3 * b + 2] + tile[3 * b + 2 : 3 * b + 3] for b in range(half)]


def lanes(half):
    high = lax.axis_index("tm") % 2
    return high * half, (1 - high) * half


def edges_kernel(width, video_hbm, ring, swap, video, sems):
    half = video.shape[0] // 2
    last = video.shape[2] - width
    even = even_strip()
    copies = [
        pltpu.make_async_copy(video_hbm.at[pl.ds(first, half)], video.at[pl.ds(lane * half, half)], sems.at[lane])
        for lane, first in enumerate(lanes(half))
    ]
    for copy in copies:
        copy.start()
    for copy in copies:
        copy.wait()
    for start, dest in ((jnp.where(even, 0, last), ring), (jnp.where(even, last, 0), swap)):
        dest[...] = video[:, :, pl.ds(aligned(start, width), width), :]


def own_kernel(width, gaps_hbm, rates_hbm, weight_hbm, video, local, driven, message, table, weight, framed, full, gaps, rates, sems):
    half, frames, inner, states = local.shape
    batch, cells, channels = video.shape[0], video.shape[2], video.shape[3]
    first = lanes(half)
    weights = {d: pltpu.make_async_copy(weight_hbm.at[d], weight.at[d], sems.at[2 + d]) for d in (1, 0, 2)}
    copies = [pltpu.make_async_copy(gaps_hbm, gaps, sems.at[0]), pltpu.make_async_copy(rates_hbm, rates, sems.at[1])]
    for copy in list(weights.values()) + copies:
        copy.start()
    for b in range(half):
        put(framed, (pl.ds(b * frames * cells, frames * cells),), video[half + b].reshape(frames * cells, channels), width)
    less = cells - width
    block = framed[...]
    frame = block.reshape(half * frames, cells, 3 * channels)
    weights[1].wait()
    total = jnp.dot(block, weight[1], preferred_element_type=F32)
    full[...] = total.reshape(half, frames, cells, states)
    weights[0].wait()
    above = jnp.dot(frame[:, :less].reshape(-1, 3 * channels), weight[0], preferred_element_type=F32)
    full[:, :, width:, :] += above.reshape(half, frames, less, states)
    weights[2].wait()
    below = jnp.dot(frame[:, width:].reshape(-1, 3 * channels), weight[2], preferred_element_type=F32)
    full[:, :, :less, :] += below.reshape(half, frames, less, states)
    for copy in copies:
        copy.wait()
    rate = rates[...]
    for b in range(batch):
        span = None
        for t in range(frames):
            gap = gaps[first[b // half] + b % half, t]
            span = gap if span is None else span + gap
            decay = jnp.exp(-rate * gap)
            table[b, t : t + 1] = decay
            table[b, frames + t : frames + t + 1] = jnp.sqrt(1.0 - decay * decay)
            table[b, 2 * frames + t : 2 * frames + t + 1] = jnp.exp(-rate * span)
        table[b, 3 * frames : 3 * frames + 1] = jnp.zeros((1, states), F32) + span
        table[b, 3 * frames + 1 : 3 * frames + 2] = rate
    for b in range(half):
        driven[b, :, :width] = full[b, :, :width]
        driven[b, :, width:] = full[b, :, less:]
        for r in range(0, inner, width):

            def value_of(t):
                return full[b, t, width + r : 2 * width + r]

            state = recurrence(b, half + b, slice(r, r + width), table, local, value_of)
            message[b * inner + r : b * inner + r + width] = state.astype(BF16)
    message[half * inner : half * inner + tile_rows(half)] = span_tile([table[half + b, 3 * frames : 3 * frames + 1] for b in range(half)])


def table_rows(frames):
    return -(-(3 * frames + 2) // 8) * 8


def ring_open():
    strip = lax.axis_index("rows")
    return jnp.logical_and(strip != 0, strip != lax.axis_size("rows") - 1)


def halo_block(first, half, halo, product=None, incoming=None):
    frames, width, c = halo.shape[1:]
    x = halo[first : first + half]
    if product is None:
        return x.reshape(half * frames * width, c)
    pieces = []
    for b in range(half):
        more = incoming[first + b].astype(F32)
        pieces += [x[b, t].astype(F32) + product(b, t) * more for t in range(frames)]
    return jnp.concatenate(pieces, axis=0)


def recurrence(b, at, rows, table, local, value_of):
    frames = local.shape[1]
    state = None
    for t in range(frames):
        value = table[at, frames + t : frames + t + 1] * value_of(t)
        state = value if state is None else table[at, t : t + 1] * state + value
        local[b, t, rows] = state
    return state


def scan_other_kernel(width, driven, table, weight, swap, ring, local, message, framed):
    half, frames = local.shape[:2]
    even = even_strip().astype(jnp.int32)
    put(framed, (even, slice(None)), halo_block(half, half, swap), width)
    x = halo_block(half, half, ring)
    put(framed, (1 - even, slice(None)), jnp.where(ring_open(), x, jnp.zeros_like(x)), width)
    for side in range(2):
        more = jnp.dot(framed[side], weight[2 * side], preferred_element_type=F32)
        rows = slice(side * width, (side + 1) * width)
        for b in range(half):

            def value_of(t):
                at = (b * frames + t) * width
                return driven[b, t, rows] + more[at : at + width]

            state = recurrence(b, half + b, rows, table, local, value_of)
            message[(2 * b + side) * width : (2 * b + side + 1) * width] = state.astype(BF16)


def scan_own_kernel(width, video, weight, table, swap, ring, other_outer, inner, outer, ring_out, swap_out, framed):
    half, frames = inner.shape[:2]
    cells, channels = video.shape[2:]
    states = inner.shape[3]
    even = even_strip()
    swap_at = aligned(jnp.where(even, cells + width, 0), width)
    ring_at = aligned(jnp.where(even, 0, cells + width), width)
    open_ring = ring_open()
    for b in range(half):
        for t in range(frames):
            f = b * frames + t
            put(framed, (f, pl.ds(width, cells)), video[b, t], width)
            put(framed, (f, pl.ds(swap_at, width)), swap[b, t], width)
            x = ring[b, t]
            put(framed, (f, pl.ds(ring_at, width)), jnp.where(open_ring, x, jnp.zeros_like(x)), width)
    for b in range(half):
        total = None
        for d in range(3):
            lhs = framed[b * frames : (b + 1) * frames, d * width : d * width + cells].reshape(frames * cells, 3 * channels)
            term = jnp.dot(lhs, weight[d], preferred_element_type=F32)
            total = term if total is None else total + term
        total = total.reshape(frames, cells, states)
        for r in range(0, cells, width):
            if r == 0:
                dest, rows = outer, slice(0, width)
            elif r == cells - width:
                dest, rows = outer, slice(width, 2 * width)
            else:
                dest, rows = inner, slice(r - width, r)
            recurrence(b, b, rows, table, dest, lambda t: total[t, r : r + width])
    for source, at in ((outer, 0), (other_outer, half)):
        for dest, start in ((ring_out, jnp.where(even, 0, width)), (swap_out, jnp.where(even, width, 0))):
            for b in range(half):
                dest[at + b] = source[b, :, pl.ds(aligned(start, width), width), :].astype(BF16)


SPAN, PREFIX, LOW, THEIRS, MINE, BEFORE = range(6)


def join_kernel(frames, inner, bit, combine, last, names, *refs):
    ref = dict(zip(names, refs))
    table, message = ref["table"], ref["message"]
    place = lax.axis_index("tm")
    upper = (place >> bit) % 2 == 1
    high = place % 2 == 1
    if last:
        join_last(frames, ref, upper, high)
        return
    new = ref.get("new_total")
    half, count = ref["low" if bit == 0 else "new_before"].shape[:2]
    if inner:
        partner = spans_of(message[half * count :, :], half)
        ref["new_meta"][...] = jnp.zeros_like(ref["new_meta"])
    spans = []
    for b in range(half):
        row = slice(b, b + 1)
        rate = table[b, 3 * frames + 1 : 3 * frames + 2]
        if inner:
            meta = ref["new_meta"]
            mine = table[b, 3 * frames : 3 * frames + 1] if bit == 0 else ref["meta"][SPAN, row]
            prefix = jnp.zeros_like(mine) if bit == 0 else ref["meta"][PREFIX, row]
            meta[MINE, row] = mine
            meta[BEFORE, row] = prefix
            meta[THEIRS, row] = partner[b]
            meta[SPAN, row] = mine + partner[b]
            if bit == 0:
                meta[LOW, row] = jnp.where(high, partner[b], mine)
            else:
                meta[LOW, row] = ref["meta"][LOW, row]
                meta[PREFIX, row] = prefix + jnp.where(upper, partner[b], 0.0)
            theirs_span = partner[b]
        else:
            meta = ref["meta"]
            mine, prefix, theirs_span = meta[MINE, row], meta[BEFORE, row], meta[THEIRS, row]
        spans.append(mine + theirs_span)
        theirs = message[b * count : (b + 1) * count].astype(F32)
        own = ref["local"][b, frames - 1] if bit == 0 else ref["total"][b]
        keep = jnp.where(upper, 1.0, jnp.exp(-rate * theirs_span))
        add = jnp.where(upper, jnp.exp(-rate * mine), 1.0)
        whole = keep * own + add * theirs
        if new is not None:
            new[b] = whole
        if bit == 0:
            ref["low"][b] = jnp.where(high, theirs, own)
        else:
            now = jnp.where(upper, jnp.exp(-rate * prefix), 0.0) * theirs
            ref["new_before"][b] = now if bit == 1 else ref["before"][b] + now
        if not combine:
            ref["outgoing"][b * count : (b + 1) * count] = whole.astype(BF16)
        elif not inner:
            many = ref["inner_total"].shape[1]
            ref["outgoing"][b * many : (b + 1) * many] = ref["inner_total"][b].astype(BF16)
            at = half * many + b * count
            ref["outgoing"][at : at + count] = whole.astype(BF16)
    if inner != combine:
        rows = ref["outgoing"].shape[0]
        ref["outgoing"][rows - tile_rows(half) : rows] = span_tile(spans)


def join_last(frames, ref, upper, high):
    message, meta = ref["message"], ref["meta"]
    half, many = ref["low_inner"].shape[:2]
    for b in range(half):
        row = slice(b, b + 1)
        rate = ref["table"][b, 3 * frames + 1 : 3 * frames + 2]
        scale = jnp.where(upper, jnp.exp(-rate * meta[PREFIX, row]), 0.0)
        low_decay = jnp.exp(-rate * meta[LOW, row])
        for kind in ("inner", "outer"):
            low = ref["low_" + kind]
            count = low.shape[1]
            at = b * count + (half * many if kind == "outer" else 0)
            now = scale * message[at : at + count].astype(F32)
            if "before_" + kind in ref:
                now = now + ref["before_" + kind][b]
            below = low_decay * now + low[b]
            ref["incoming_" + kind][b] = jnp.where(high, below, now)
            ref["back_" + kind][b] = jnp.where(high, now, below).astype(BF16)


def incoming_edges_kernel(width, own, other, ring, swap):
    half = own.shape[0]
    even = even_strip()
    for dest, start in ((ring, jnp.where(even, 0, width)), (swap, jnp.where(even, width, 0))):
        at = pl.ds(aligned(start, width), width)
        for b in range(half):
            dest[b] = own[b, at, :].astype(BF16)
            dest[half + b] = other[b, at, :]


def gelu(x):
    return 0.5 * x * (1.0 + lax.erf(x * 0.7071067811865476))


def mix_kernel(part, width, in_inner, in_outer, local_inner, local_outer, table, weight, video, inner, outer, framed):
    half, frames, _, states = local_inner.shape
    cells, channels = video.shape[2:]
    first = part * half
    for b in range(half):
        for t in range(frames):
            product = table[first + b, 2 * frames + t : 2 * frames + t + 1]
            at = (b * frames + t) * cells
            x = local_inner[b, t] + product * in_inner[b].astype(F32)
            put(framed, (pl.ds(at + width, cells - 2 * width),), x, width)
            x = local_outer[b, t] + product * in_outer[b].astype(F32)
            put(framed, (pl.ds(at, width),), x[:width], width)
            put(framed, (pl.ds(at + cells - width, width),), x[width:], width)
    less = cells - width
    for b in range(half):
        block = framed[pl.ds(b * frames * cells, frames * cells), :]
        frame = block.reshape(frames, cells, 3 * states)
        total = jnp.dot(block, weight[1], preferred_element_type=F32).reshape(frames, cells, channels)
        above = jnp.dot(frame[:, :less].reshape(-1, 3 * states), weight[0], preferred_element_type=F32).reshape(frames, less, channels)
        below = jnp.dot(frame[:, width:].reshape(-1, 3 * states), weight[2], preferred_element_type=F32).reshape(frames, less, channels)
        outer[0, b] = total[:, :width] + below[:, :width]
        outer[1, b] = total[:, less:] + above[:, less - width :]
        middle = total[:, width:less] + above[:, : less - width] + below[:, width:]
        inner[b] = (video[first + b, :, width:less].astype(F32) + gelu(middle)).astype(BF16)


def edge_rows(side, width, outer_own, outer_other, halo_local, halo_in, table, weight, video, framed, edge, then):
    batch, frames, cells, channels = video.shape
    half = batch // 2

    def product(b, t):
        return table[b, 2 * frames + t : 2 * frames + t + 1]

    even = even_strip()
    below = even if side == 0 else jnp.logical_not(even)
    below = below.astype(jnp.int32)
    x = halo_block(0, batch, halo_local, product, halo_in)
    if side == 1:
        x = jnp.where(ring_open(), x, jnp.zeros_like(x))
    put(framed, (slice(None),), x, width)
    more = jnp.dot(framed[...], weight[2 * below], preferred_element_type=F32).reshape(batch, frames, width, channels)
    row = aligned(below * (cells - width), width)
    for lane, outer in enumerate((outer_own, outer_other)):
        at = slice(lane * half, (lane + 1) * half)
        mixed = outer[below] + more[at]
        edge[at] = (video[at, :, pl.ds(row, width), :].astype(F32) + gelu(mixed)).astype(BF16)
        then(lane, row)


def finish_swap_kernel(width, outer_own, outer_other, halo_local, halo_in, table, weight, video, edge, framed):
    edge_rows(0, width, outer_own, outer_other, halo_local, halo_in, table, weight, video, framed, edge, lambda lane, row: None)


def finish_ring_kernel(
    width, outer_own, outer_other, halo_local, halo_in, table, weight, video, inner_own, inner_other, done, out, framed, edge, sems
):
    batch, _, cells, _ = video.shape
    half = batch // 2
    first = lanes(half)
    copies = []

    def write(source, lane, row, count, kind):
        dest = out.at[pl.ds(first[lane], half), :, pl.ds(row, count), :]
        copies.append(pltpu.make_async_copy(source, dest, sems.at[kind, lane]))
        copies[-1].start()

    swap_row = aligned(even_strip().astype(jnp.int32) * (cells - width), width)
    for lane, inner in enumerate((inner_own, inner_other)):
        write(inner, lane, width, cells - 2 * width, 0)
        write(done.at[pl.ds(lane * half, half)], lane, swap_row, width, 1)

    def then(lane, row):
        write(edge.at[pl.ds(lane * half, half)], lane, row, width, 2)

    edge_rows(1, width, outer_own, outer_other, halo_local, halo_in, table, weight, video, framed, edge, then)
    for copy in copies:
        copy.wait()


def on_device(video, weight_in, weight_out, rates, gaps):
    batch, frames, rows, width, channels = video.shape
    states = weight_in.shape[3]
    half = batch // 2
    cells = rows * width
    blocks = lax.axis_size("tm")
    strips = lax.axis_size("rows")
    rounds = blocks.bit_length() - 1
    swap = [(i, i ^ 1) for i in range(strips)]

    def ring_partner(block, strip):
        if strip in (0, strips - 1):
            return block ^ 1, strip
        return block, strip + 1 if strip % 2 else strip - 1

    places = [(block, strip) for block in range(blocks) for strip in range(strips)]
    ring = [(place[0] * strips + place[1], partner[0] * strips + partner[1]) for place in places for partner in [ring_partner(*place)]]

    def across(bit):
        mask = 1 if bit == 0 else 2 ** (bit + 1) - 2
        return [(i, i ^ mask) for i in range(blocks)]

    def in_hbm(x):
        return pltpu.with_memory_space_constraint(x, pltpu.HBM)

    video = in_hbm(video.reshape(batch, frames, cells, channels))
    weight_in = in_hbm(weight_in.reshape(3, 3 * channels, states))
    weight_out = weight_out.reshape(3, 3 * states, channels)
    edge_flops = 2 * batch * frames * width * 6 * channels * states
    own_flops = 5 * edge_flops

    edge = like(batch, frames, width, channels, dtype=BF16)
    ring_video, swap_video, video = call(
        functools.partial(edges_kernel, width), [video], [edge, edge, like(*video.shape, dtype=BF16)],
        [pltpu.SemaphoreType.DMA((2,))], [HBM],
    )
    ring_video = lax.ppermute(ring_video, ("tm", "rows"), ring)
    swap_video = lax.ppermute(swap_video, "rows", swap)

    count = {"inner": cells - 2 * width, "outer": 2 * width}
    local = {kind: like(half, frames, n, states) for kind, n in count.items()}
    end = {kind: like(half, n, states) for kind, n in count.items()}
    message = {"inner": like(half * count["inner"] + tile_rows(half), states, dtype=BF16), "outer": like(half * count["outer"], states, dtype=BF16)}
    both = like(half * cells + tile_rows(half), states, dtype=BF16)
    rows_in_table = table_rows(frames)
    other = {}
    outgoing = {}
    other["inner"], driven, outgoing["inner"], table, weight = call(
        functools.partial(own_kernel, width), [in_hbm(gaps), in_hbm(rates[None, :]), weight_in, video],
        [local["inner"], local["outer"], message["inner"], like(batch, rows_in_table, states), like(*weight_in.shape, dtype=BF16)],
        [
            pltpu.VMEM((half * frames * cells, 3 * channels), BF16),
            pltpu.VMEM((half, frames, cells, states), F32),
            pltpu.SMEM(gaps.shape, F32),
            pltpu.VMEM((1, states), F32),
            pltpu.SemaphoreType.DMA((5,)),
        ],
        [HBM] * 3 + [VMEM], mib=16, flops=own_flops // 2,
    )
    meta_shape = like(6, 8, states)
    halo = like(batch, frames, width, states, dtype=BF16)
    incoming = {"inner": lax.ppermute(outgoing["inner"], "tm", across(0))}
    other["outer"], outgoing["outer"] = call(
        functools.partial(scan_other_kernel, width), [driven, table, weight, swap_video, ring_video],
        [local["outer"], message["outer"]], [pltpu.VMEM((2, half * frames * width, 3 * channels), BF16)], flops=edge_flops // 2,
    )
    incoming["outer"] = lax.ppermute(outgoing["outer"], "tm", across(0))
    own = {}
    own["inner"], own["outer"], ring_local, swap_local = call(
        functools.partial(scan_own_kernel, width), [video, weight, table, swap_video, ring_video, other["outer"]],
        [local["inner"], local["outer"], halo, halo], [pltpu.VMEM((half * frames, cells + 2 * width, 3 * channels), BF16)],
        mib=16, flops=own_flops // 2,
    )
    ring_local = lax.ppermute(ring_local, ("tm", "rows"), ring)
    swap_local = lax.ppermute(swap_local, "rows", swap)

    def join(inner, bit, combine, last, ins, outs):
        results = call(
            functools.partial(join_kernel, frames, inner, bit, combine, last, tuple(ins) + tuple(outs)), list(ins.values()), list(outs.values())
        )
        return dict(zip(outs, results))

    final = rounds - 1
    constant = {"table": table}
    total, before, low, meta = {}, {}, {}, None
    for bit in range(final):
        combine = bit + 1 == final
        for kind in ("inner", "outer"):
            inner = kind == "inner"
            ins = {"message": incoming[kind], **constant}
            outs = {"new_total": end[kind]} if inner or not combine else {}
            if bit == 0:
                ins["local"] = own[kind]
                outs["low"] = end[kind]
            else:
                ins["total"] = total[kind]
                outs["new_before"] = end[kind]
            if bit > 1:
                ins["before"] = before[kind]
            if bit or not inner:
                ins["meta"] = meta
            if inner:
                outs["new_meta"] = meta_shape
            if not combine:
                outs["outgoing"] = message[kind]
            elif not inner:
                ins["inner_total"] = total["inner"]
                outs["outgoing"] = both
            got = join(inner, bit, combine, False, ins, outs)
            total[kind] = got.get("new_total")
            low[kind] = got.get("low", low.get(kind))
            before[kind] = got.get("new_before")
            meta = got.get("new_meta", meta)
            if not combine:
                incoming[kind] = lax.ppermute(got["outgoing"], "tm", across(bit + 1))
            elif not inner:
                incoming["both"] = lax.ppermute(got["outgoing"], "tm", across(final))
    ins = {"message": incoming["both"], **constant, "meta": meta}
    outs = {}
    for kind in ("inner", "outer"):
        ins["low_" + kind] = low[kind]
        if before[kind] is not None:
            ins["before_" + kind] = before[kind]
        outs["incoming_" + kind] = end[kind]
        outs["back_" + kind] = like(*end[kind].shape, dtype=BF16)
    got = join(True, final, True, True, ins, outs)
    into_own = {kind: got["incoming_" + kind] for kind in end}
    into_other = {kind: lax.ppermute(got["back_" + kind], "tm", across(0)) for kind in ("outer", "inner")}

    def mix(part, into, local, flops):
        return call(
            functools.partial(mix_kernel, part, width),
            [into["inner"], into["outer"], local["inner"], local["outer"], table, weight_out, video],
            [like(half, frames, cells - 2 * width, channels, dtype=BF16), like(2, half, frames, width, channels)],
            [pltpu.VMEM((half * frames * cells, 3 * states), BF16)], mib=16, flops=flops,
        )

    inner_own, outer_own = mix(0, into_own, own, own_flops // 2)
    edge = like(batch, width, states, dtype=BF16)
    ring_in, swap_in = call(
        functools.partial(incoming_edges_kernel, width), [into_own["outer"], into_other["outer"]], [edge, edge]
    )
    ring_in = lax.ppermute(ring_in, ("tm", "rows"), ring)
    swap_in = lax.ppermute(swap_in, "rows", swap)
    inner_other, outer_other = mix(1, into_other, other, own_flops // 2)
    common = [outer_own, outer_other]
    framed = pltpu.VMEM((batch * frames * width, 3 * states), BF16)
    edge = like(batch, frames, width, channels, dtype=BF16)
    done, = call(
        functools.partial(finish_swap_kernel, width), common + [swap_local, swap_in, table, weight_out, video],
        [edge], [framed], mib=16, flops=edge_flops // 2,
    )
    out = pl.pallas_call(
        functools.partial(finish_ring_kernel, width),
        out_shape=like(batch, frames, cells, channels, dtype=BF16),
        in_specs=[VMEM] * 10,
        out_specs=HBM,
        scratch_shapes=[framed, pltpu.VMEM(edge.shape, BF16), pltpu.SemaphoreType.DMA((3, 2))],
        name="finish_ring",
        compiler_params=pltpu.CompilerParams(vmem_limit_bytes=16 << 20),
        cost_estimate=pl.CostEstimate(flops=edge_flops // 2, bytes_accessed=1 << 20, transcendentals=0),
    )(*common, ring_local, ring_in, table, weight_out, video, inner_own, inner_other, done)
    return out.reshape(batch, frames, rows, width, channels)


def solution(mesh):
    in_specs = (P(None, "tm", "rows", None, None), P(), P(), P(), P(None, "tm"))
    out_specs = P(None, "tm", "rows", None, None)

    return jax.shard_map(on_device, mesh=mesh, in_specs=in_specs, out_specs=out_specs, check_vma=False)
```

```python
import functools

import jax
import jax.numpy as jnp
from jax import lax
from jax.experimental import pallas as pl
from jax.experimental.pallas import tpu as pltpu
from jax.sharding import PartitionSpec as P


F32 = jnp.float32
BF16 = jnp.bfloat16
SMEM = pl.BlockSpec(memory_space=pltpu.SMEM)
VMEM = pl.BlockSpec(memory_space=pltpu.VMEM)
HBM = pl.BlockSpec(memory_space=pltpu.HBM)


def call(kernel, args, outs, scratch=(), specs=None, mib=8, flops=1 << 20, bytes_accessed=1 << 20):
    return pl.pallas_call(
        kernel,
        out_shape=outs,
        in_specs=specs or [VMEM] * len(args),
        out_specs=[VMEM] * len(outs),
        scratch_shapes=list(scratch),
        compiler_params=pltpu.CompilerParams(vmem_limit_bytes=mib << 20),
        cost_estimate=pl.CostEstimate(flops=flops, bytes_accessed=bytes_accessed, transcendentals=0),
    )(*args)


def like(*shape, dtype=F32):
    return jax.ShapeDtypeStruct(shape, dtype)


def even_strip():
    return lax.axis_index("rows") % 2 == 0


def aligned(start, step):
    return pl.multiple_of(start, step)


def with_shifts(x, width):
    rows = x.shape[0]
    x = x.astype(F32)
    column = lax.broadcasted_iota(jnp.int32, (rows, 1), 0) % width
    left = jnp.where(column == 0, 0.0, pltpu.roll(x, 1, 0))
    right = jnp.where(column == width - 1, 0.0, pltpu.roll(x, rows - 1, 0))
    return left.astype(BF16), x.astype(BF16), right.astype(BF16)


def put(dest, index, x, width):
    c = x.shape[1]
    for i, part in enumerate(with_shifts(x, width)):
        dest[index + (slice(i * c, (i + 1) * c),)] = part


def tile_rows(half):
    return -(-3 * half // 8) * 8


def span_tile(spans):
    rows = []
    for span in spans:
        high = span.astype(BF16).astype(F32)
        rest = span - high
        middle = rest.astype(BF16).astype(F32)
        rows += [high, middle, rest - middle]
    index = lax.broadcasted_iota(jnp.int32, (tile_rows(len(spans)), rows[0].shape[1]), 0)
    tile = jnp.zeros(index.shape, F32)
    for i, row in enumerate(rows):
        tile = jnp.where(index == i, row, tile)
    return tile.astype(BF16)


def spans_of(tile, half):
    tile = tile.astype(F32)
    return [tile[3 * b : 3 * b + 1] + tile[3 * b + 1 : 3 * b + 2] + tile[3 * b + 2 : 3 * b + 3] for b in range(half)]


def lanes(half):
    high = lax.axis_index("tm") % 2
    return high * half, (1 - high) * half


def edges_kernel(width, video_hbm, ring, swap, video, sems):
    half = video.shape[0] // 2
    last = video.shape[2] - width
    even = even_strip()
    copies = [
        pltpu.make_async_copy(video_hbm.at[pl.ds(first, half)], video.at[pl.ds(lane * half, half)], sems.at[lane])
        for lane, first in enumerate(lanes(half))
    ]
    for copy in copies:
        copy.start()
    for copy in copies:
        copy.wait()
    for start, dest in ((jnp.where(even, 0, last), ring), (jnp.where(even, last, 0), swap)):
        dest[...] = video[:, :, pl.ds(aligned(start, width), width), :]


def own_kernel(width, gaps_hbm, rates_hbm, weight, video, local, driven, message, table, framed, full, gaps, rates, sems):
    half, frames, inner, states = local.shape
    batch, cells, channels = video.shape[0], video.shape[2], video.shape[3]
    first = lanes(half)
    copies = [pltpu.make_async_copy(gaps_hbm, gaps, sems.at[0]), pltpu.make_async_copy(rates_hbm, rates, sems.at[1])]
    for copy in copies:
        copy.start()
    for b in range(half):
        put(framed, (pl.ds(b * frames * cells, frames * cells),), video[half + b].reshape(frames * cells, channels), width)
    less = cells - width
    block = framed[...]
    frame = block.reshape(half * frames, cells, 3 * channels)
    total = jnp.dot(block, weight[1], preferred_element_type=F32)
    full[...] = total.reshape(half, frames, cells, states)
    above = jnp.dot(frame[:, :less].reshape(-1, 3 * channels), weight[0], preferred_element_type=F32)
    full[:, :, width:, :] += above.reshape(half, frames, less, states)
    below = jnp.dot(frame[:, width:].reshape(-1, 3 * channels), weight[2], preferred_element_type=F32)
    full[:, :, :less, :] += below.reshape(half, frames, less, states)
    for copy in copies:
        copy.wait()
    rate = rates[...]
    for b in range(batch):
        span = None
        for t in range(frames):
            gap = gaps[first[b // half] + b % half, t]
            span = gap if span is None else span + gap
            decay = jnp.exp(-rate * gap)
            table[b, t : t + 1] = decay
            table[b, frames + t : frames + t + 1] = jnp.sqrt(1.0 - decay * decay)
            table[b, 2 * frames + t : 2 * frames + t + 1] = jnp.exp(-rate * span)
        table[b, 3 * frames : 3 * frames + 1] = jnp.zeros((1, states), F32) + span
        table[b, 3 * frames + 1 : 3 * frames + 2] = rate
    for b in range(half):
        driven[b, :, :width] = full[b, :, :width]
        driven[b, :, width:] = full[b, :, less:]
        for r in range(0, inner, width):

            def value_of(t):
                return full[b, t, width + r : 2 * width + r]

            state = recurrence(b, half + b, slice(r, r + width), table, local, value_of)
            message[b * inner + r : b * inner + r + width] = state.astype(BF16)
    message[half * inner : half * inner + tile_rows(half)] = span_tile([table[half + b, 3 * frames : 3 * frames + 1] for b in range(half)])


def table_rows(frames):
    return -(-(3 * frames + 2) // 8) * 8


def ring_open():
    strip = lax.axis_index("rows")
    return jnp.logical_and(strip != 0, strip != lax.axis_size("rows") - 1)


def halo_block(first, half, halo, product=None, incoming=None):
    frames, width, c = halo.shape[1:]
    x = halo[first : first + half]
    if product is None:
        return x.reshape(half * frames * width, c)
    pieces = []
    for b in range(half):
        more = incoming[first + b].astype(F32)
        pieces += [x[b, t].astype(F32) + product(b, t) * more for t in range(frames)]
    return jnp.concatenate(pieces, axis=0)


def recurrence(b, at, rows, table, local, value_of):
    frames = local.shape[1]
    state = None
    for t in range(frames):
        value = table[at, frames + t : frames + t + 1] * value_of(t)
        state = value if state is None else table[at, t : t + 1] * state + value
        local[b, t, rows] = state
    return state


def scan_other_kernel(width, driven, table, weight, swap, ring, local, message, framed):
    half, frames = local.shape[:2]
    even = even_strip().astype(jnp.int32)
    put(framed, (even, slice(None)), halo_block(half, half, swap), width)
    x = halo_block(half, half, ring)
    put(framed, (1 - even, slice(None)), jnp.where(ring_open(), x, jnp.zeros_like(x)), width)
    for side in range(2):
        more = jnp.dot(framed[side], weight[2 * side], preferred_element_type=F32)
        rows = slice(side * width, (side + 1) * width)
        for b in range(half):

            def value_of(t):
                at = (b * frames + t) * width
                return driven[b, t, rows] + more[at : at + width]

            state = recurrence(b, half + b, rows, table, local, value_of)
            message[(2 * b + side) * width : (2 * b + side + 1) * width] = state.astype(BF16)


def scan_own_kernel(width, video, weight, table, swap, ring, other_outer, inner, outer, ring_out, swap_out, framed):
    half, frames = inner.shape[:2]
    cells, channels = video.shape[2:]
    states = inner.shape[3]
    even = even_strip()
    swap_at = aligned(jnp.where(even, cells + width, 0), width)
    ring_at = aligned(jnp.where(even, 0, cells + width), width)
    open_ring = ring_open()
    for b in range(half):
        for t in range(frames):
            f = b * frames + t
            put(framed, (f, pl.ds(width, cells)), video[b, t], width)
            put(framed, (f, pl.ds(swap_at, width)), swap[b, t], width)
            x = ring[b, t]
            put(framed, (f, pl.ds(ring_at, width)), jnp.where(open_ring, x, jnp.zeros_like(x)), width)
    for b in range(half):
        total = None
        for d in range(3):
            lhs = framed[b * frames : (b + 1) * frames, d * width : d * width + cells].reshape(frames * cells, 3 * channels)
            term = jnp.dot(lhs, weight[d], preferred_element_type=F32)
            total = term if total is None else total + term
        total = total.reshape(frames, cells, states)
        for r in range(0, cells, width):
            if r == 0:
                dest, rows = outer, slice(0, width)
            elif r == cells - width:
                dest, rows = outer, slice(width, 2 * width)
            else:
                dest, rows = inner, slice(r - width, r)
            recurrence(b, b, rows, table, dest, lambda t: total[t, r : r + width])
    for source, at in ((outer, 0), (other_outer, half)):
        for dest, start in ((ring_out, jnp.where(even, 0, width)), (swap_out, jnp.where(even, width, 0))):
            for b in range(half):
                dest[at + b] = source[b, :, pl.ds(aligned(start, width), width), :].astype(BF16)


SPAN, PREFIX, LOW, THEIRS, MINE, BEFORE = range(6)


def join_kernel(frames, inner, bit, combine, last, names, *refs):
    ref = dict(zip(names, refs))
    table, message = ref["table"], ref["message"]
    place = lax.axis_index("tm")
    upper = (place >> bit) % 2 == 1
    high = place % 2 == 1
    if last:
        join_last(frames, ref, upper, high)
        return
    new = ref.get("new_total")
    half, count = ref["low" if bit == 0 else "new_before"].shape[:2]
    if inner:
        partner = spans_of(message[half * count :, :], half)
        ref["new_meta"][...] = jnp.zeros_like(ref["new_meta"])
    spans = []
    for b in range(half):
        row = slice(b, b + 1)
        rate = table[b, 3 * frames + 1 : 3 * frames + 2]
        if inner:
            meta = ref["new_meta"]
            mine = table[b, 3 * frames : 3 * frames + 1] if bit == 0 else ref["meta"][SPAN, row]
            prefix = jnp.zeros_like(mine) if bit == 0 else ref["meta"][PREFIX, row]
            meta[MINE, row] = mine
            meta[BEFORE, row] = prefix
            meta[THEIRS, row] = partner[b]
            meta[SPAN, row] = mine + partner[b]
            if bit == 0:
                meta[LOW, row] = jnp.where(high, partner[b], mine)
            else:
                meta[LOW, row] = ref["meta"][LOW, row]
                meta[PREFIX, row] = prefix + jnp.where(upper, partner[b], 0.0)
            theirs_span = partner[b]
        else:
            meta = ref["meta"]
            mine, prefix, theirs_span = meta[MINE, row], meta[BEFORE, row], meta[THEIRS, row]
        spans.append(mine + theirs_span)
        theirs = message[b * count : (b + 1) * count].astype(F32)
        own = ref["local"][b, frames - 1] if bit == 0 else ref["total"][b]
        keep = jnp.where(upper, 1.0, jnp.exp(-rate * theirs_span))
        add = jnp.where(upper, jnp.exp(-rate * mine), 1.0)
        whole = keep * own + add * theirs
        if new is not None:
            new[b] = whole
        if bit == 0:
            ref["low"][b] = jnp.where(high, theirs, own)
        else:
            now = jnp.where(upper, jnp.exp(-rate * prefix), 0.0) * theirs
            ref["new_before"][b] = now if bit == 1 else ref["before"][b] + now
        if not combine:
            ref["outgoing"][b * count : (b + 1) * count] = whole.astype(BF16)
        elif not inner:
            many = ref["inner_total"].shape[1]
            ref["outgoing"][b * many : (b + 1) * many] = ref["inner_total"][b].astype(BF16)
            at = half * many + b * count
            ref["outgoing"][at : at + count] = whole.astype(BF16)
    if inner != combine:
        rows = ref["outgoing"].shape[0]
        ref["outgoing"][rows - tile_rows(half) : rows] = span_tile(spans)


def join_last(frames, ref, upper, high):
    message, meta = ref["message"], ref["meta"]
    half, many = ref["low_inner"].shape[:2]
    for b in range(half):
        row = slice(b, b + 1)
        rate = ref["table"][b, 3 * frames + 1 : 3 * frames + 2]
        scale = jnp.where(upper, jnp.exp(-rate * meta[PREFIX, row]), 0.0)
        low_decay = jnp.exp(-rate * meta[LOW, row])
        for kind in ("inner", "outer"):
            low = ref["low_" + kind]
            count = low.shape[1]
            at = b * count + (half * many if kind == "outer" else 0)
            now = scale * message[at : at + count].astype(F32)
            if "before_" + kind in ref:
                now = now + ref["before_" + kind][b]
            below = low_decay * now + low[b]
            ref["incoming_" + kind][b] = jnp.where(high, below, now)
            ref["back_" + kind][b] = jnp.where(high, now, below).astype(BF16)


def incoming_edges_kernel(width, own, other, ring, swap):
    half = own.shape[0]
    even = even_strip()
    for dest, start in ((ring, jnp.where(even, 0, width)), (swap, jnp.where(even, width, 0))):
        at = pl.ds(aligned(start, width), width)
        for b in range(half):
            dest[b] = own[b, at, :].astype(BF16)
            dest[half + b] = other[b, at, :]


def gelu(x):
    return 0.5 * x * (1.0 + lax.erf(x * 0.7071067811865476))


def mix_kernel(part, width, in_inner, in_outer, local_inner, local_outer, table, weight, video, inner, outer, framed):
    half, frames, _, states = local_inner.shape
    cells, channels = video.shape[2:]
    first = part * half
    for b in range(half):
        for t in range(frames):
            product = table[first + b, 2 * frames + t : 2 * frames + t + 1]
            at = (b * frames + t) * cells
            x = local_inner[b, t] + product * in_inner[b].astype(F32)
            put(framed, (pl.ds(at + width, cells - 2 * width),), x, width)
            x = local_outer[b, t] + product * in_outer[b].astype(F32)
            put(framed, (pl.ds(at, width),), x[:width], width)
            put(framed, (pl.ds(at + cells - width, width),), x[width:], width)
    less = cells - width
    for b in range(half):
        block = framed[pl.ds(b * frames * cells, frames * cells), :]
        frame = block.reshape(frames, cells, 3 * states)
        total = jnp.dot(block, weight[1], preferred_element_type=F32).reshape(frames, cells, channels)
        above = jnp.dot(frame[:, :less].reshape(-1, 3 * states), weight[0], preferred_element_type=F32).reshape(frames, less, channels)
        below = jnp.dot(frame[:, width:].reshape(-1, 3 * states), weight[2], preferred_element_type=F32).reshape(frames, less, channels)
        outer[0, b] = total[:, :width] + below[:, :width]
        outer[1, b] = total[:, less:] + above[:, less - width :]
        middle = total[:, width:less] + above[:, : less - width] + below[:, width:]
        inner[b] = (video[first + b, :, width:less].astype(F32) + gelu(middle)).astype(BF16)


def edge_rows(side, width, outer_own, outer_other, halo_local, halo_in, table, weight, video, framed, edge, then):
    batch, frames, cells, channels = video.shape
    half = batch // 2

    def product(b, t):
        return table[b, 2 * frames + t : 2 * frames + t + 1]

    even = even_strip()
    below = even if side == 0 else jnp.logical_not(even)
    below = below.astype(jnp.int32)
    x = halo_block(0, batch, halo_local, product, halo_in)
    if side == 1:
        x = jnp.where(ring_open(), x, jnp.zeros_like(x))
    put(framed, (slice(None),), x, width)
    more = jnp.dot(framed[...], weight[2 * below], preferred_element_type=F32).reshape(batch, frames, width, channels)
    row = aligned(below * (cells - width), width)
    for lane, outer in enumerate((outer_own, outer_other)):
        at = slice(lane * half, (lane + 1) * half)
        mixed = outer[below] + more[at]
        edge[at] = (video[at, :, pl.ds(row, width), :].astype(F32) + gelu(mixed)).astype(BF16)
        then(lane, row)


def finish_swap_kernel(width, outer_own, outer_other, halo_local, halo_in, table, weight, video, edge, framed):
    edge_rows(0, width, outer_own, outer_other, halo_local, halo_in, table, weight, video, framed, edge, lambda lane, row: None)


def finish_ring_kernel(
    width, outer_own, outer_other, halo_local, halo_in, table, weight, video, inner_own, inner_other, done, out, framed, edge, sems
):
    batch, _, cells, _ = video.shape
    half = batch // 2
    first = lanes(half)
    copies = []

    def write(source, lane, row, count, kind):
        dest = out.at[pl.ds(first[lane], half), :, pl.ds(row, count), :]
        copies.append(pltpu.make_async_copy(source, dest, sems.at[kind, lane]))
        copies[-1].start()

    swap_row = aligned(even_strip().astype(jnp.int32) * (cells - width), width)
    for lane, inner in enumerate((inner_own, inner_other)):
        write(inner, lane, width, cells - 2 * width, 0)
        write(done.at[pl.ds(lane * half, half)], lane, swap_row, width, 1)

    def then(lane, row):
        write(edge.at[pl.ds(lane * half, half)], lane, row, width, 2)

    edge_rows(1, width, outer_own, outer_other, halo_local, halo_in, table, weight, video, framed, edge, then)
    for copy in copies:
        copy.wait()


def on_device(video, weight_in, weight_out, rates, gaps):
    batch, frames, rows, width, channels = video.shape
    states = weight_in.shape[3]
    half = batch // 2
    cells = rows * width
    blocks = lax.axis_size("tm")
    strips = lax.axis_size("rows")
    rounds = blocks.bit_length() - 1
    swap = [(i, i ^ 1) for i in range(strips)]

    def ring_partner(block, strip):
        if strip in (0, strips - 1):
            return block ^ 1, strip
        return block, strip + 1 if strip % 2 else strip - 1

    places = [(block, strip) for block in range(blocks) for strip in range(strips)]
    ring = [(place[0] * strips + place[1], partner[0] * strips + partner[1]) for place in places for partner in [ring_partner(*place)]]

    def across(bit):
        mask = 1 if bit == 0 else 2 ** (bit + 1) - 2
        return [(i, i ^ mask) for i in range(blocks)]

    def in_hbm(x):
        return pltpu.with_memory_space_constraint(x, pltpu.HBM)

    video = in_hbm(video.reshape(batch, frames, cells, channels))
    weight_in = weight_in.reshape(3, 3 * channels, states)
    weight_out = weight_out.reshape(3, 3 * states, channels)
    edge_flops = 2 * batch * frames * width * 6 * channels * states
    own_flops = 5 * edge_flops

    edge = like(batch, frames, width, channels, dtype=BF16)
    ring_video, swap_video, video = call(
        functools.partial(edges_kernel, width), [video], [edge, edge, like(*video.shape, dtype=BF16)],
        [pltpu.SemaphoreType.DMA((2,))], [HBM], flops=1 << 31, bytes_accessed=1 << 26,
    )
    ring_video = lax.ppermute(ring_video, ("tm", "rows"), ring)
    swap_video = lax.ppermute(swap_video, "rows", swap)

    count = {"inner": cells - 2 * width, "outer": 2 * width}
    local = {kind: like(half, frames, n, states) for kind, n in count.items()}
    end = {kind: like(half, n, states) for kind, n in count.items()}
    message = {"inner": like(half * count["inner"] + tile_rows(half), states, dtype=BF16), "outer": like(half * count["outer"], states, dtype=BF16)}
    both = like(half * cells + tile_rows(half), states, dtype=BF16)
    rows_in_table = table_rows(frames)
    other = {}
    outgoing = {}
    other["inner"], driven, outgoing["inner"], table = call(
        functools.partial(own_kernel, width), [in_hbm(gaps), in_hbm(rates[None, :]), weight_in, video],
        [local["inner"], local["outer"], message["inner"], like(batch, rows_in_table, states)],
        [
            pltpu.VMEM((half * frames * cells, 3 * channels), BF16),
            pltpu.VMEM((half, frames, cells, states), F32),
            pltpu.SMEM(gaps.shape, F32),
            pltpu.VMEM((1, states), F32),
            pltpu.SemaphoreType.DMA((5,)),
        ],
        [HBM] * 2 + [VMEM] * 2, mib=16, flops=own_flops // 2,
    )
    weight = weight_in
    meta_shape = like(6, 8, states)
    halo = like(batch, frames, width, states, dtype=BF16)
    incoming = {"inner": lax.ppermute(outgoing["inner"], "tm", across(0))}
    other["outer"], outgoing["outer"] = call(
        functools.partial(scan_other_kernel, width), [driven, table, weight, swap_video, ring_video],
        [local["outer"], message["outer"]], [pltpu.VMEM((2, half * frames * width, 3 * channels), BF16)], flops=edge_flops // 2,
    )
    incoming["outer"] = lax.ppermute(outgoing["outer"], "tm", across(0))
    own = {}
    own["inner"], own["outer"], ring_local, swap_local = call(
        functools.partial(scan_own_kernel, width), [video, weight, table, swap_video, ring_video, other["outer"]],
        [local["inner"], local["outer"], halo, halo], [pltpu.VMEM((half * frames, cells + 2 * width, 3 * channels), BF16)],
        mib=16, flops=own_flops // 2,
    )
    ring_local = lax.ppermute(ring_local, ("tm", "rows"), ring)
    swap_local = lax.ppermute(swap_local, "rows", swap)

    def join(inner, bit, combine, last, ins, outs):
        results = call(
            functools.partial(join_kernel, frames, inner, bit, combine, last, tuple(ins) + tuple(outs)), list(ins.values()), list(outs.values())
        )
        return dict(zip(outs, results))

    final = rounds - 1
    constant = {"table": table}
    total, before, low, meta = {}, {}, {}, None
    for bit in range(final):
        combine = bit + 1 == final
        for kind in ("inner", "outer"):
            inner = kind == "inner"
            ins = {"message": incoming[kind], **constant}
            outs = {"new_total": end[kind]} if inner or not combine else {}
            if bit == 0:
                ins["local"] = own[kind]
                outs["low"] = end[kind]
            else:
                ins["total"] = total[kind]
                outs["new_before"] = end[kind]
            if bit > 1:
                ins["before"] = before[kind]
            if bit or not inner:
                ins["meta"] = meta
            if inner:
                outs["new_meta"] = meta_shape
            if not combine:
                outs["outgoing"] = message[kind]
            elif not inner:
                ins["inner_total"] = total["inner"]
                outs["outgoing"] = both
            got = join(inner, bit, combine, False, ins, outs)
            total[kind] = got.get("new_total")
            low[kind] = got.get("low", low.get(kind))
            before[kind] = got.get("new_before")
            meta = got.get("new_meta", meta)
            if not combine:
                incoming[kind] = lax.ppermute(got["outgoing"], "tm", across(bit + 1))
            elif not inner:
                incoming["both"] = lax.ppermute(got["outgoing"], "tm", across(final))
    ins = {"message": incoming["both"], **constant, "meta": meta}
    outs = {}
    for kind in ("inner", "outer"):
        ins["low_" + kind] = low[kind]
        if before[kind] is not None:
            ins["before_" + kind] = before[kind]
        outs["incoming_" + kind] = end[kind]
        outs["back_" + kind] = like(*end[kind].shape, dtype=BF16)
    got = join(True, final, True, True, ins, outs)
    into_own = {kind: got["incoming_" + kind] for kind in end}
    into_other = {kind: lax.ppermute(got["back_" + kind], "tm", across(0)) for kind in ("outer", "inner")}

    def mix(part, into, local, flops):
        return call(
            functools.partial(mix_kernel, part, width),
            [into["inner"], into["outer"], local["inner"], local["outer"], table, weight_out, video],
            [like(half, frames, cells - 2 * width, channels, dtype=BF16), like(2, half, frames, width, channels)],
            [pltpu.VMEM((half * frames * cells, 3 * states), BF16)], mib=16, flops=flops,
        )

    inner_own, outer_own = mix(0, into_own, own, own_flops // 2)
    edge = like(batch, width, states, dtype=BF16)
    ring_in, swap_in = call(
        functools.partial(incoming_edges_kernel, width), [into_own["outer"], into_other["outer"]], [edge, edge]
    )
    ring_in = lax.ppermute(ring_in, ("tm", "rows"), ring)
    swap_in = lax.ppermute(swap_in, "rows", swap)
    inner_other, outer_other = mix(1, into_other, other, own_flops // 2)
    common = [outer_own, outer_other]
    framed = pltpu.VMEM((batch * frames * width, 3 * states), BF16)
    edge = like(batch, frames, width, channels, dtype=BF16)
    done, = call(
        functools.partial(finish_swap_kernel, width), common + [swap_local, swap_in, table, weight_out, video],
        [edge], [framed], mib=16, flops=edge_flops // 2,
    )
    out = pl.pallas_call(
        functools.partial(finish_ring_kernel, width),
        out_shape=like(batch, frames, cells, channels, dtype=BF16),
        in_specs=[VMEM] * 10,
        out_specs=HBM,
        scratch_shapes=[framed, pltpu.VMEM(edge.shape, BF16), pltpu.SemaphoreType.DMA((3, 2))],
        name="finish_ring",
        compiler_params=pltpu.CompilerParams(vmem_limit_bytes=16 << 20),
        cost_estimate=pl.CostEstimate(flops=edge_flops // 2, bytes_accessed=1 << 20, transcendentals=0),
    )(*common, ring_local, ring_in, table, weight_out, video, inner_own, inner_other, done)
    return out.reshape(batch, frames, rows, width, channels)


def solution(mesh):
    in_specs = (P(None, "tm", "rows", None, None), P(), P(), P(), P(None, "tm"))
    out_specs = P(None, "tm", "rows", None, None)

    return jax.shard_map(on_device, mesh=mesh, in_specs=in_specs, out_specs=out_specs, check_vma=False)
```

```python
import functools

import jax
import jax.numpy as jnp
from jax import lax
from jax.experimental import pallas as pl
from jax.experimental.pallas import tpu as pltpu
from jax.sharding import PartitionSpec as P


F32 = jnp.float32
BF16 = jnp.bfloat16
SMEM = pl.BlockSpec(memory_space=pltpu.SMEM)
VMEM = pl.BlockSpec(memory_space=pltpu.VMEM)
HBM = pl.BlockSpec(memory_space=pltpu.HBM)


def call(kernel, args, outs, scratch=(), specs=None, mib=8, flops=1 << 20, bytes_accessed=1 << 20):
    return pl.pallas_call(
        kernel,
        out_shape=outs,
        in_specs=specs or [VMEM] * len(args),
        out_specs=[VMEM] * len(outs),
        scratch_shapes=list(scratch),
        compiler_params=pltpu.CompilerParams(vmem_limit_bytes=mib << 20),
        cost_estimate=pl.CostEstimate(flops=flops, bytes_accessed=bytes_accessed, transcendentals=0),
    )(*args)


def like(*shape, dtype=F32):
    return jax.ShapeDtypeStruct(shape, dtype)


def even_strip():
    return lax.axis_index("rows") % 2 == 0


def aligned(start, step):
    return pl.multiple_of(start, step)


def row_places(width, cells):
    even = even_strip()
    last = cells - width
    return aligned(jnp.where(even, last, 0), width), aligned(jnp.where(even, 0, last), width)


def with_shifts(x, width):
    rows = x.shape[0]
    x = x.astype(F32)
    column = lax.broadcasted_iota(jnp.int32, (rows, 1), 0) % width
    left = jnp.where(column == 0, 0.0, pltpu.roll(x, 1, 0))
    right = jnp.where(column == width - 1, 0.0, pltpu.roll(x, rows - 1, 0))
    return left.astype(BF16), x.astype(BF16), right.astype(BF16)


def put(dest, index, x, width):
    c = x.shape[1]
    for i, part in enumerate(with_shifts(x, width)):
        dest[index + (slice(i * c, (i + 1) * c),)] = part


def tile_rows(half):
    return -(-3 * half // 8) * 8


def span_tile(spans):
    rows = []
    for span in spans:
        high = span.astype(BF16).astype(F32)
        rest = span - high
        middle = rest.astype(BF16).astype(F32)
        rows += [high, middle, rest - middle]
    index = lax.broadcasted_iota(jnp.int32, (tile_rows(len(spans)), rows[0].shape[1]), 0)
    tile = jnp.zeros(index.shape, F32)
    for i, row in enumerate(rows):
        tile = jnp.where(index == i, row, tile)
    return tile.astype(BF16)


def spans_of(tile, half):
    tile = tile.astype(F32)
    return [tile[3 * b : 3 * b + 1] + tile[3 * b + 1 : 3 * b + 2] + tile[3 * b + 2 : 3 * b + 3] for b in range(half)]


def lanes(half):
    high = lax.axis_index("tm") % 2
    return high * half, (1 - high) * half


def edges_kernel(width, video_hbm, ring, swap, video, sems):
    half = video.shape[0] // 2
    last = video.shape[2] - width
    even = even_strip()
    copies = [
        pltpu.make_async_copy(video_hbm.at[pl.ds(first, half)], video.at[pl.ds(lane * half, half)], sems.at[lane])
        for lane, first in enumerate(lanes(half))
    ]
    for copy in copies:
        copy.start()
    for copy in copies:
        copy.wait()
    for start, dest in ((jnp.where(even, 0, last), ring), (jnp.where(even, last, 0), swap)):
        dest[...] = video[:, :, pl.ds(aligned(start, width), width), :]


def own_kernel(width, gaps_hbm, rates_hbm, weight, video, local, driven_swap, driven_ring, table, framed, full, gaps, rates, sems):
    half, frames, inner, states = local.shape
    batch, cells, channels = video.shape[0], video.shape[2], video.shape[3]
    first = lanes(half)
    copies = [pltpu.make_async_copy(gaps_hbm, gaps, sems.at[0]), pltpu.make_async_copy(rates_hbm, rates, sems.at[1])]
    for copy in copies:
        copy.start()
    for b in range(half):
        put(framed, (pl.ds(b * frames * cells, frames * cells),), video[half + b].reshape(frames * cells, channels), width)
    less = cells - width
    block = framed[...]
    frame = block.reshape(half * frames, cells, 3 * channels)
    total = jnp.dot(block, weight[1], preferred_element_type=F32)
    full[...] = total.reshape(half, frames, cells, states)
    above = jnp.dot(frame[:, :less].reshape(-1, 3 * channels), weight[0], preferred_element_type=F32)
    full[:, :, width:, :] += above.reshape(half, frames, less, states)
    below = jnp.dot(frame[:, width:].reshape(-1, 3 * channels), weight[2], preferred_element_type=F32)
    full[:, :, :less, :] += below.reshape(half, frames, less, states)
    for copy in copies:
        copy.wait()
    rate = rates[...]
    for b in range(batch):
        span = None
        for t in range(frames):
            gap = gaps[first[b // half] + b % half, t]
            span = gap if span is None else span + gap
            decay = jnp.exp(-rate * gap)
            table[b, t : t + 1] = decay
            table[b, frames + t : frames + t + 1] = jnp.sqrt(1.0 - decay * decay)
            table[b, 2 * frames + t : 2 * frames + t + 1] = jnp.exp(-rate * span)
        table[b, 3 * frames : 3 * frames + 1] = jnp.zeros((1, states), F32) + span
        table[b, 3 * frames + 1 : 3 * frames + 2] = rate
    swap_row, ring_row = row_places(width, cells)
    for b in range(half):
        driven_swap[b] = full[b, :, pl.ds(swap_row, width), :]
        driven_ring[b] = full[b, :, pl.ds(ring_row, width), :]
        for r in range(0, inner, width):

            def value_of(t):
                return full[b, t, width + r : 2 * width + r]

            recurrence(b, half + b, slice(r, r + width), table, local, value_of)


def table_rows(frames):
    return -(-(3 * frames + 2) // 8) * 8


def ring_open():
    strip = lax.axis_index("rows")
    return jnp.logical_and(strip != 0, strip != lax.axis_size("rows") - 1)


def halo_block(first, half, halo, product=None, incoming=None):
    frames, width, c = halo.shape[1:]
    x = halo[first : first + half]
    if product is None:
        return x.reshape(half * frames * width, c)
    pieces = []
    for b in range(half):
        more = incoming[first + b].astype(F32)
        pieces += [x[b, t].astype(F32) + product(b, t) * more for t in range(frames)]
    return jnp.concatenate(pieces, axis=0)


def recurrence(b, at, rows, table, local, value_of):
    frames = local.shape[1]
    state = None
    for t in range(frames):
        value = table[at, frames + t : frames + t + 1] * value_of(t)
        state = value if state is None else table[at, t : t + 1] * state + value
        local[b, t, rows] = state
    return state


def scan_edge_kernel(late, width, driven, table, weight, halo, *refs):
    if late:
        local, message, framed = refs
    else:
        inner, local, message, framed = refs
    half, frames = local.shape[:2]
    below = even_strip().astype(jnp.int32)
    x = halo_block(half, half, halo)
    if late:
        below = 1 - below
        x = jnp.where(ring_open(), x, jnp.zeros_like(x))
    put(framed, (slice(None),), x, width)
    more = jnp.dot(framed[...], weight[2 * below], preferred_element_type=F32)
    for b in range(half):

        def value_of(t):
            at = (b * frames + t) * width
            return driven[b, t] + more[at : at + width]

        state = recurrence(b, half + b, slice(0, width), table, local, value_of)
        if late:
            message[b * width : (b + 1) * width] = state.astype(BF16)
        else:
            many = inner.shape[2]
            at = b * (many + width)
            message[at : at + many] = inner[b, frames - 1].astype(BF16)
            message[at + many : at + many + width] = state.astype(BF16)
    if not late:
        rows = message.shape[0]
        message[rows - tile_rows(half) : rows] = span_tile([table[half + b, 3 * frames : 3 * frames + 1] for b in range(half)])


def scan_own_kernel(
    width, video, weight, table, swap, ring, other_swap, other_ring,
    inner, swap_local, ring_local, end_early, end_late, ring_out, swap_out, framed, full,
):
    half, frames, many, states = inner.shape
    cells, channels = video.shape[2:]
    even = even_strip()
    swap_at = aligned(jnp.where(even, cells + width, 0), width)
    ring_at = aligned(jnp.where(even, 0, cells + width), width)
    swap_row, ring_row = row_places(width, cells)
    open_ring = ring_open()
    for b in range(half):
        for t in range(frames):
            f = b * frames + t
            put(framed, (f, pl.ds(width, cells)), video[b, t], width)
            put(framed, (f, pl.ds(swap_at, width)), swap[b, t], width)
            x = ring[b, t]
            put(framed, (f, pl.ds(ring_at, width)), jnp.where(open_ring, x, jnp.zeros_like(x)), width)
    for b in range(half):
        total = None
        for d in range(3):
            lhs = framed[b * frames : (b + 1) * frames, d * width : d * width + cells].reshape(frames * cells, 3 * channels)
            term = jnp.dot(lhs, weight[d], preferred_element_type=F32)
            total = term if total is None else total + term
        full[b] = total.reshape(frames, cells, states)
        for r in range(0, many, width):
            end_early[b, r : r + width] = recurrence(
                b, b, slice(r, r + width), table, inner, lambda t: full[b, t, width + r : 2 * width + r]
            )
        every = slice(0, width)
        end_early[b, many : many + width] = recurrence(b, b, every, table, swap_local, lambda t: full[b, t, pl.ds(swap_row, width), :])
        end_late[b] = recurrence(b, b, every, table, ring_local, lambda t: full[b, t, pl.ds(ring_row, width), :])
    swap_out[:half] = swap_local[...].astype(BF16)
    swap_out[half:] = other_swap[...].astype(BF16)
    ring_out[:half] = ring_local[...].astype(BF16)
    ring_out[half:] = other_ring[...].astype(BF16)


SPAN, PREFIX, LOW, THEIRS, MINE, BEFORE = range(6)


def join_kernel(frames, early, bit, combine, last, names, *refs):
    ref = dict(zip(names, refs))
    table, message = ref["table"], ref["message"]
    place = lax.axis_index("tm")
    upper = (place >> bit) % 2 == 1
    high = place % 2 == 1
    if last:
        join_last(frames, ref, upper, high)
        return
    new = ref.get("new_total")
    half, count = ref["low" if bit == 0 else "new_before"].shape[:2]
    if early:
        partner = spans_of(message[half * count :, :], half)
        ref["new_meta"][...] = jnp.zeros_like(ref["new_meta"])
    spans = []
    for b in range(half):
        row = slice(b, b + 1)
        rate = table[b, 3 * frames + 1 : 3 * frames + 2]
        if early:
            meta = ref["new_meta"]
            mine = table[b, 3 * frames : 3 * frames + 1] if bit == 0 else ref["meta"][SPAN, row]
            prefix = jnp.zeros_like(mine) if bit == 0 else ref["meta"][PREFIX, row]
            meta[MINE, row] = mine
            meta[BEFORE, row] = prefix
            meta[THEIRS, row] = partner[b]
            meta[SPAN, row] = mine + partner[b]
            if bit == 0:
                meta[LOW, row] = jnp.where(high, partner[b], mine)
            else:
                meta[LOW, row] = ref["meta"][LOW, row]
                meta[PREFIX, row] = prefix + jnp.where(upper, partner[b], 0.0)
            theirs_span = partner[b]
        else:
            meta = ref["meta"]
            mine, prefix, theirs_span = meta[MINE, row], meta[BEFORE, row], meta[THEIRS, row]
        spans.append(mine + theirs_span)
        theirs = message[b * count : (b + 1) * count].astype(F32)
        own = ref["end"][b] if bit == 0 else ref["total"][b]
        keep = jnp.where(upper, 1.0, jnp.exp(-rate * theirs_span))
        add = jnp.where(upper, jnp.exp(-rate * mine), 1.0)
        whole = keep * own + add * theirs
        if new is not None:
            new[b] = whole
        if bit == 0:
            ref["low"][b] = jnp.where(high, theirs, own)
        else:
            now = jnp.where(upper, jnp.exp(-rate * prefix), 0.0) * theirs
            ref["new_before"][b] = now if bit == 1 else ref["before"][b] + now
        if not combine:
            ref["outgoing"][b * count : (b + 1) * count] = whole.astype(BF16)
        elif not early:
            many = ref["early_total"].shape[1]
            ref["outgoing"][b * many : (b + 1) * many] = ref["early_total"][b].astype(BF16)
            at = half * many + b * count
            ref["outgoing"][at : at + count] = whole.astype(BF16)
    if early != combine:
        rows = ref["outgoing"].shape[0]
        ref["outgoing"][rows - tile_rows(half) : rows] = span_tile(spans)


def join_last(frames, ref, upper, high):
    message, meta = ref["message"], ref["meta"]
    half, many = ref["low_early"].shape[:2]
    for b in range(half):
        row = slice(b, b + 1)
        rate = ref["table"][b, 3 * frames + 1 : 3 * frames + 2]
        scale = jnp.where(upper, jnp.exp(-rate * meta[PREFIX, row]), 0.0)
        low_decay = jnp.exp(-rate * meta[LOW, row])
        for kind in ("early", "late"):
            low = ref["low_" + kind]
            count = low.shape[1]
            at = b * count + (half * many if kind == "late" else 0)
            now = scale * message[at : at + count].astype(F32)
            if "before_" + kind in ref:
                now = now + ref["before_" + kind][b]
            below = low_decay * now + low[b]
            ref["incoming_" + kind][b] = jnp.where(high, below, now)
            ref["back_" + kind][b] = jnp.where(high, now, below).astype(BF16)


def incoming_edges_kernel(width, own, other, edge):
    half, count = own.shape[:2]
    edge[:half] = own[:, count - width :].astype(BF16)
    edge[half:] = other[:, count - width :]


def gelu(x):
    return 0.5 * x * (1.0 + lax.erf(x * 0.7071067811865476))


def mix_kernel(part, width, in_early, in_late, local_inner, local_swap, local_ring, table, weight, video, inner, outer, framed):
    half, frames, many, states = local_inner.shape
    cells, channels = video.shape[2:]
    first = part * half
    swap_row, ring_row = row_places(width, cells)
    for b in range(half):
        for t in range(frames):
            product = table[first + b, 2 * frames + t : 2 * frames + t + 1]
            at = (b * frames + t) * cells
            x = local_inner[b, t] + product * in_early[b, :many].astype(F32)
            put(framed, (pl.ds(at + width, many),), x, width)
            x = local_swap[b, t] + product * in_early[b, many:].astype(F32)
            put(framed, (pl.ds(aligned(at + swap_row, width), width),), x, width)
            x = local_ring[b, t] + product * in_late[b].astype(F32)
            put(framed, (pl.ds(aligned(at + ring_row, width), width),), x, width)
    less = cells - width
    for b in range(half):
        block = framed[pl.ds(b * frames * cells, frames * cells), :]
        frame = block.reshape(frames, cells, 3 * states)
        total = jnp.dot(block, weight[1], preferred_element_type=F32).reshape(frames, cells, channels)
        above = jnp.dot(frame[:, :less].reshape(-1, 3 * states), weight[0], preferred_element_type=F32).reshape(frames, less, channels)
        below = jnp.dot(frame[:, width:].reshape(-1, 3 * states), weight[2], preferred_element_type=F32).reshape(frames, less, channels)
        outer[0, b] = total[:, :width] + below[:, :width]
        outer[1, b] = total[:, less:] + above[:, less - width :]
        middle = total[:, width:less] + above[:, : less - width] + below[:, width:]
        inner[b] = (video[first + b, :, width:less].astype(F32) + gelu(middle)).astype(BF16)


def edge_rows(side, width, outer_own, outer_other, halo_local, halo_in, table, weight, video, framed, edge, then):
    batch, frames, cells, channels = video.shape
    half = batch // 2

    def product(b, t):
        return table[b, 2 * frames + t : 2 * frames + t + 1]

    even = even_strip()
    below = even if side == 0 else jnp.logical_not(even)
    below = below.astype(jnp.int32)
    x = halo_block(0, batch, halo_local, product, halo_in)
    if side == 1:
        x = jnp.where(ring_open(), x, jnp.zeros_like(x))
    put(framed, (slice(None),), x, width)
    more = jnp.dot(framed[...], weight[2 * below], preferred_element_type=F32).reshape(batch, frames, width, channels)
    row = aligned(below * (cells - width), width)
    for lane, outer in enumerate((outer_own, outer_other)):
        at = slice(lane * half, (lane + 1) * half)
        mixed = outer[below] + more[at]
        edge[at] = (video[at, :, pl.ds(row, width), :].astype(F32) + gelu(mixed)).astype(BF16)
        then(lane, row)


def finish_swap_kernel(width, outer_own, outer_other, halo_local, halo_in, table, weight, video, edge, framed):
    edge_rows(0, width, outer_own, outer_other, halo_local, halo_in, table, weight, video, framed, edge, lambda lane, row: None)


def finish_ring_kernel(
    width, outer_own, outer_other, halo_local, halo_in, table, weight, video, inner_own, inner_other, done, out, framed, edge, sems
):
    batch, _, cells, _ = video.shape
    half = batch // 2
    first = lanes(half)
    copies = []

    def write(source, lane, row, count, kind):
        dest = out.at[pl.ds(first[lane], half), :, pl.ds(row, count), :]
        copies.append(pltpu.make_async_copy(source, dest, sems.at[kind, lane]))
        copies[-1].start()

    swap_row = aligned(even_strip().astype(jnp.int32) * (cells - width), width)
    for lane, inner in enumerate((inner_own, inner_other)):
        write(inner, lane, width, cells - 2 * width, 0)
        write(done.at[pl.ds(lane * half, half)], lane, swap_row, width, 1)

    def then(lane, row):
        write(edge.at[pl.ds(lane * half, half)], lane, row, width, 2)

    edge_rows(1, width, outer_own, outer_other, halo_local, halo_in, table, weight, video, framed, edge, then)
    for copy in copies:
        copy.wait()


def on_device(video, weight_in, weight_out, rates, gaps):
    batch, frames, rows, width, channels = video.shape
    states = weight_in.shape[3]
    half = batch // 2
    cells = rows * width
    blocks = lax.axis_size("tm")
    strips = lax.axis_size("rows")
    rounds = blocks.bit_length() - 1
    swap = [(i, i ^ 1) for i in range(strips)]

    def ring_partner(block, strip):
        if strip in (0, strips - 1):
            return block ^ 1, strip
        return block, strip + 1 if strip % 2 else strip - 1

    places = [(block, strip) for block in range(blocks) for strip in range(strips)]
    ring = [(place[0] * strips + place[1], partner[0] * strips + partner[1]) for place in places for partner in [ring_partner(*place)]]

    def across(bit):
        mask = 1 if bit == 0 else 2 ** (bit + 1) - 2
        return [(i, i ^ mask) for i in range(blocks)]

    def in_hbm(x):
        return pltpu.with_memory_space_constraint(x, pltpu.HBM)

    video = in_hbm(video.reshape(batch, frames, cells, channels))
    weight_in = weight_in.reshape(3, 3 * channels, states)
    weight_out = weight_out.reshape(3, 3 * states, channels)
    edge_flops = 2 * batch * frames * width * 6 * channels * states
    own_flops = 5 * edge_flops

    edge = like(batch, frames, width, channels, dtype=BF16)
    ring_video, swap_video, video = call(
        functools.partial(edges_kernel, width), [video], [edge, edge, like(*video.shape, dtype=BF16)],
        [pltpu.SemaphoreType.DMA((2,))], [HBM], flops=1 << 31, bytes_accessed=1 << 26,
    )
    ring_video = lax.ppermute(ring_video, ("tm", "rows"), ring)
    swap_video = lax.ppermute(swap_video, "rows", swap)

    many = cells - 2 * width
    count = {"early": many + width, "late": width}
    local_inner = like(half, frames, many, states)
    local_edge = like(half, frames, width, states)
    end = {kind: like(half, n, states) for kind, n in count.items()}
    message = {"early": like(half * count["early"] + tile_rows(half), states, dtype=BF16), "late": like(half * width, states, dtype=BF16)}
    both = like(half * (many + 2 * width) + tile_rows(half), states, dtype=BF16)
    rows_in_table = table_rows(frames)
    inner_other, driven_swap, driven_ring, table = call(
        functools.partial(own_kernel, width), [in_hbm(gaps), in_hbm(rates[None, :]), weight_in, video],
        [local_inner, local_edge, local_edge, like(batch, rows_in_table, states)],
        [
            pltpu.VMEM((half * frames * cells, 3 * channels), BF16),
            pltpu.VMEM((half, frames, cells, states), F32),
            pltpu.SMEM(gaps.shape, F32),
            pltpu.VMEM((1, states), F32),
            pltpu.SemaphoreType.DMA((2,)),
        ],
        [HBM] * 2 + [VMEM] * 2, mib=16, flops=own_flops // 2,
    )
    weight = weight_in
    meta_shape = like(6, 8, states)
    halo = like(batch, frames, width, states, dtype=BF16)
    framed = pltpu.VMEM((half * frames * width, 3 * channels), BF16)
    incoming = {}
    swap_other, outgoing = call(
        functools.partial(scan_edge_kernel, False, width), [driven_swap, table, weight, swap_video, inner_other],
        [local_edge, message["early"]], [framed], flops=edge_flops // 4,
    )
    incoming["early"] = lax.ppermute(outgoing, "tm", across(0))
    ring_other, outgoing = call(
        functools.partial(scan_edge_kernel, True, width), [driven_ring, table, weight, ring_video],
        [local_edge, message["late"]], [framed], flops=edge_flops // 4,
    )
    incoming["late"] = lax.ppermute(outgoing, "tm", across(0))
    inner_own, swap_own, ring_own, *ends, ring_local, swap_local = call(
        functools.partial(scan_own_kernel, width), [video, weight, table, swap_video, ring_video, swap_other, ring_other],
        [local_inner, local_edge, local_edge, end["early"], end["late"], halo, halo],
        [pltpu.VMEM((half * frames, cells + 2 * width, 3 * channels), BF16), pltpu.VMEM((half, frames, cells, states), F32)],
        mib=16, flops=own_flops // 2,
    )
    own_end = dict(zip(("early", "late"), ends))
    ring_local = lax.ppermute(ring_local, ("tm", "rows"), ring)
    swap_local = lax.ppermute(swap_local, "rows", swap)

    def join(early, bit, combine, last, ins, outs):
        results = call(
            functools.partial(join_kernel, frames, early, bit, combine, last, tuple(ins) + tuple(outs)), list(ins.values()), list(outs.values())
        )
        return dict(zip(outs, results))

    final = rounds - 1
    constant = {"table": table}
    total, before, low, meta = {}, {}, {}, None
    for bit in range(final):
        combine = bit + 1 == final
        for kind in ("early", "late"):
            early = kind == "early"
            ins = {"message": incoming[kind], **constant}
            outs = {"new_total": end[kind]} if early or not combine else {}
            if bit == 0:
                ins["end"] = own_end[kind]
                outs["low"] = end[kind]
            else:
                ins["total"] = total[kind]
                outs["new_before"] = end[kind]
            if bit > 1:
                ins["before"] = before[kind]
            if bit or not early:
                ins["meta"] = meta
            if early:
                outs["new_meta"] = meta_shape
            if not combine:
                outs["outgoing"] = message[kind]
            elif not early:
                ins["early_total"] = total["early"]
                outs["outgoing"] = both
            got = join(early, bit, combine, False, ins, outs)
            total[kind] = got.get("new_total")
            low[kind] = got.get("low", low.get(kind))
            before[kind] = got.get("new_before")
            meta = got.get("new_meta", meta)
            if not combine:
                incoming[kind] = lax.ppermute(got["outgoing"], "tm", across(bit + 1))
            elif not early:
                incoming["both"] = lax.ppermute(got["outgoing"], "tm", across(final))
    ins = {"message": incoming["both"], **constant, "meta": meta}
    outs = {}
    for kind in ("early", "late"):
        ins["low_" + kind] = low[kind]
        if before[kind] is not None:
            ins["before_" + kind] = before[kind]
        outs["incoming_" + kind] = end[kind]
        outs["back_" + kind] = like(*end[kind].shape, dtype=BF16)
    got = join(True, final, True, True, ins, outs)
    into_own = {kind: got["incoming_" + kind] for kind in end}
    into_other = {kind: lax.ppermute(got["back_" + kind], "tm", across(0)) for kind in ("late", "early")}

    def mix(part, into, local, flops):
        return call(
            functools.partial(mix_kernel, part, width),
            [into["early"], into["late"], *local, table, weight_out, video],
            [like(half, frames, cells - 2 * width, channels, dtype=BF16), like(2, half, frames, width, channels)],
            [pltpu.VMEM((half * frames * cells, 3 * states), BF16)], mib=16, flops=flops,
        )

    inner_own, outer_own = mix(0, into_own, (inner_own, swap_own, ring_own), own_flops // 2)
    edge = like(batch, width, states, dtype=BF16)

    def edges(kind):
        kernel = functools.partial(incoming_edges_kernel, width)
        edges, = call(kernel, [into_own[kind], into_other[kind]], [edge])
        return edges

    ring_in = lax.ppermute(edges("late"), ("tm", "rows"), ring)
    swap_in = lax.ppermute(edges("early"), "rows", swap)
    inner_other, outer_other = mix(1, into_other, (inner_other, swap_other, ring_other), own_flops // 2)
    common = [outer_own, outer_other]
    framed = pltpu.VMEM((batch * frames * width, 3 * states), BF16)
    edge = like(batch, frames, width, channels, dtype=BF16)
    done, = call(
        functools.partial(finish_swap_kernel, width), common + [swap_local, swap_in, table, weight_out, video],
        [edge], [framed], mib=16, flops=edge_flops // 2,
    )
    out = pl.pallas_call(
        functools.partial(finish_ring_kernel, width),
        out_shape=like(batch, frames, cells, channels, dtype=BF16),
        in_specs=[VMEM] * 10,
        out_specs=HBM,
        scratch_shapes=[framed, pltpu.VMEM(edge.shape, BF16), pltpu.SemaphoreType.DMA((3, 2))],
        name="finish_ring",
        compiler_params=pltpu.CompilerParams(vmem_limit_bytes=16 << 20),
        cost_estimate=pl.CostEstimate(flops=edge_flops // 2, bytes_accessed=1 << 20, transcendentals=0),
    )(*common, ring_local, ring_in, table, weight_out, video, inner_own, inner_other, done)
    return out.reshape(batch, frames, rows, width, channels)


def solution(mesh):
    in_specs = (P(None, "tm", "rows", None, None), P(), P(), P(), P(None, "tm"))
    out_specs = P(None, "tm", "rows", None, None)

    return jax.shard_map(on_device, mesh=mesh, in_specs=in_specs, out_specs=out_specs, check_vma=False)
```

```python
import functools

import jax
import jax.numpy as jnp
from jax import lax
from jax.experimental import pallas as pl
from jax.experimental.pallas import tpu as pltpu
from jax.sharding import PartitionSpec as P


F32 = jnp.float32
BF16 = jnp.bfloat16
SMEM = pl.BlockSpec(memory_space=pltpu.SMEM)
VMEM = pl.BlockSpec(memory_space=pltpu.VMEM)
HBM = pl.BlockSpec(memory_space=pltpu.HBM)


def call(kernel, args, outs, scratch=(), specs=None, mib=8, flops=1 << 20, bytes_accessed=1 << 20, out_space=VMEM):
    return pl.pallas_call(
        kernel,
        out_shape=outs,
        in_specs=specs or [VMEM] * len(args),
        out_specs=[out_space] * len(outs),
        scratch_shapes=list(scratch),
        compiler_params=pltpu.CompilerParams(vmem_limit_bytes=mib << 20),
        cost_estimate=pl.CostEstimate(flops=flops, bytes_accessed=bytes_accessed, transcendentals=0),
    )(*args)


def like(*shape, dtype=F32):
    return jax.ShapeDtypeStruct(shape, dtype)


def even_strip():
    return lax.axis_index("rows") % 2 == 0


def aligned(start, step):
    return pl.multiple_of(start, step)


def row_places(width, cells):
    even = even_strip()
    last = cells - width
    return aligned(jnp.where(even, last, 0), width), aligned(jnp.where(even, 0, last), width)


def with_shifts(x, width):
    rows = x.shape[0]
    x = x.astype(F32)
    column = lax.broadcasted_iota(jnp.int32, (rows, 1), 0) % width
    left = jnp.where(column == 0, 0.0, pltpu.roll(x, 1, 0))
    right = jnp.where(column == width - 1, 0.0, pltpu.roll(x, rows - 1, 0))
    return left.astype(BF16), x.astype(BF16), right.astype(BF16)


def put(dest, index, x, width):
    c = x.shape[1]
    for i, part in enumerate(with_shifts(x, width)):
        dest[index + (slice(i * c, (i + 1) * c),)] = part


def tile_rows(half):
    return -(-3 * half // 8) * 8


def span_tile(spans):
    rows = []
    for span in spans:
        high = span.astype(BF16).astype(F32)
        rest = span - high
        middle = rest.astype(BF16).astype(F32)
        rows += [high, middle, rest - middle]
    index = lax.broadcasted_iota(jnp.int32, (tile_rows(len(spans)), rows[0].shape[1]), 0)
    tile = jnp.zeros(index.shape, F32)
    for i, row in enumerate(rows):
        tile = jnp.where(index == i, row, tile)
    return tile.astype(BF16)


def spans_of(tile, half):
    tile = tile.astype(F32)
    return [tile[3 * b : 3 * b + 1] + tile[3 * b + 1 : 3 * b + 2] + tile[3 * b + 2 : 3 * b + 3] for b in range(half)]


def lanes(half):
    high = lax.axis_index("tm") % 2
    return high * half, (1 - high) * half


def edges_kernel(width, video, ring, swap, other, sems):
    half = other.shape[0]
    swap_row, ring_row = row_places(width, video.shape[2])
    first = lanes(half)
    copies = [pltpu.make_async_copy(video.at[pl.ds(first[1], half)], other, sems.at[2, 0])]
    for i, (row, dest) in enumerate(((ring_row, ring), (swap_row, swap))):
        for lane in range(2):
            source = video.at[pl.ds(first[lane], half), :, pl.ds(row, width), :]
            copies.insert(0, pltpu.make_async_copy(source, dest.at[pl.ds(lane * half, half)], sems.at[i, lane]))
    for copy in copies:
        copy.start()
    for copy in copies:
        copy.wait()


def own_kernel(width, gaps_hbm, rates_hbm, weight, video, local, driven_swap, driven_ring, table, framed, full, gaps, rates, sems):
    half, frames, inner, states = local.shape
    batch, cells, channels = table.shape[0], video.shape[2], video.shape[3]
    first = lanes(half)
    copies = [pltpu.make_async_copy(gaps_hbm, gaps, sems.at[0]), pltpu.make_async_copy(rates_hbm, rates, sems.at[1])]
    for copy in copies:
        copy.start()
    for b in range(half):
        put(framed, (pl.ds(b * frames * cells, frames * cells),), video[b].reshape(frames * cells, channels), width)
    less = cells - width
    block = framed[...]
    frame = block.reshape(half * frames, cells, 3 * channels)
    total = jnp.dot(block, weight[1], preferred_element_type=F32)
    full[...] = total.reshape(half, frames, cells, states)
    above = jnp.dot(frame[:, :less].reshape(-1, 3 * channels), weight[0], preferred_element_type=F32)
    full[:, :, width:, :] += above.reshape(half, frames, less, states)
    below = jnp.dot(frame[:, width:].reshape(-1, 3 * channels), weight[2], preferred_element_type=F32)
    full[:, :, :less, :] += below.reshape(half, frames, less, states)
    for copy in copies:
        copy.wait()
    rate = rates[...]
    for b in range(batch):
        span = None
        for t in range(frames):
            gap = gaps[first[b // half] + b % half, t]
            span = gap if span is None else span + gap
            decay = jnp.exp(-rate * gap)
            table[b, t : t + 1] = decay
            table[b, frames + t : frames + t + 1] = jnp.sqrt(1.0 - decay * decay)
            table[b, 2 * frames + t : 2 * frames + t + 1] = jnp.exp(-rate * span)
        table[b, 3 * frames : 3 * frames + 1] = jnp.zeros((1, states), F32) + span
        table[b, 3 * frames + 1 : 3 * frames + 2] = rate
    swap_row, ring_row = row_places(width, cells)
    for b in range(half):
        driven_swap[b] = full[b, :, pl.ds(swap_row, width), :]
        driven_ring[b] = full[b, :, pl.ds(ring_row, width), :]
        for r in range(0, inner, width):

            def value_of(t):
                return full[b, t, width + r : 2 * width + r]

            recurrence(b, half + b, slice(r, r + width), table, local, value_of)


def table_rows(frames):
    return -(-(3 * frames + 2) // 8) * 8


def ring_open():
    strip = lax.axis_index("rows")
    return jnp.logical_and(strip != 0, strip != lax.axis_size("rows") - 1)


def halo_block(first, half, halo, product=None, incoming=None):
    frames, width, c = halo.shape[1:]
    x = halo[first : first + half]
    if product is None:
        return x.reshape(half * frames * width, c)
    pieces = []
    for b in range(half):
        more = incoming(first + b).astype(F32)
        pieces += [x[b, t].astype(F32) + product(b, t) * more for t in range(frames)]
    return jnp.concatenate(pieces, axis=0)


def recurrence(b, at, rows, table, local, value_of):
    frames = local.shape[1]
    state = None
    for t in range(frames):
        value = table[at, frames + t : frames + t + 1] * value_of(t)
        state = value if state is None else table[at, t : t + 1] * state + value
        local[b, t, rows] = state
    return state


def scan_edge_kernel(late, width, driven, table, weight, halo, *refs):
    if late:
        local, message, framed = refs
    else:
        inner, local, message, framed = refs
    half, frames = local.shape[:2]
    below = even_strip().astype(jnp.int32)
    x = halo_block(half, half, halo)
    if late:
        below = 1 - below
        x = jnp.where(ring_open(), x, jnp.zeros_like(x))
    put(framed, (slice(None),), x, width)
    more = jnp.dot(framed[...], weight[2 * below], preferred_element_type=F32)
    for b in range(half):

        def value_of(t):
            at = (b * frames + t) * width
            return driven[b, t] + more[at : at + width]

        state = recurrence(b, half + b, slice(0, width), table, local, value_of)
        if late:
            message[b * width : (b + 1) * width] = state.astype(BF16)
        else:
            many = inner.shape[2]
            at = b * (many + width)
            message[at : at + many] = inner[b, frames - 1].astype(BF16)
            message[at + many : at + many + width] = state.astype(BF16)
    if not late:
        rows = message.shape[0]
        message[rows - tile_rows(half) : rows] = span_tile([table[half + b, 3 * frames : 3 * frames + 1] for b in range(half)])


def scan_own_kernel(
    width, video, weight, table, swap, ring, other_swap, other_ring,
    inner, swap_local, ring_local, end_early, end_late, ring_out, swap_out, framed, full,
):
    half, frames, many, states = inner.shape
    cells, channels = video.shape[2:]
    even = even_strip()
    first = lanes(half)[0]
    swap_row, ring_row = row_places(width, cells)
    open_ring = ring_open()
    for b in range(half):
        for t in range(frames):
            f = b * frames + t
            put(framed, (f, pl.ds(width, cells)), video[first + b, t], width)
            x = ring[b, t]
            x = jnp.where(open_ring, x, jnp.zeros_like(x))
            put(framed, (f, pl.ds(0, width)), jnp.where(even, x, swap[b, t]), width)
            put(framed, (f, pl.ds(cells + width, width)), jnp.where(even, swap[b, t], x), width)
    for b in range(half):
        total = None
        for d in range(3):
            lhs = framed[b * frames : (b + 1) * frames, d * width : d * width + cells].reshape(frames * cells, 3 * channels)
            term = jnp.dot(lhs, weight[d], preferred_element_type=F32)
            total = term if total is None else total + term
        full[b] = total.reshape(frames, cells, states)
        for r in range(0, many, width):
            end_early[b, r : r + width] = recurrence(
                b, b, slice(r, r + width), table, inner, lambda t: full[b, t, width + r : 2 * width + r]
            )
        every = slice(0, width)
        end_early[b, many : many + width] = recurrence(b, b, every, table, swap_local, lambda t: full[b, t, pl.ds(swap_row, width), :])
        end_late[b] = recurrence(b, b, every, table, ring_local, lambda t: full[b, t, pl.ds(ring_row, width), :])
    swap_out[:half] = swap_local[...].astype(BF16)
    swap_out[half:] = other_swap[...].astype(BF16)
    ring_out[:half] = ring_local[...].astype(BF16)
    ring_out[half:] = other_ring[...].astype(BF16)


SPAN, PREFIX, LOW, THEIRS, MINE, BEFORE = range(6)


class Refs:
    message = table = end = total = before = meta = early_total = early_low = late_low = early_before = late_before = None
    new_total = new_before = new_meta = low = outgoing = incoming = back = ring = diagonal = None

    def __init__(self, names, refs):
        self.__dict__.update(zip(names, refs))


def join_kernel(frames, early, bit, combine, last, names, *refs):
    ref = Refs(names, refs)
    table, message = ref.table, ref.message
    place = lax.axis_index("tm")
    upper = (place >> bit) % 2 == 1
    high = place % 2 == 1
    if last:
        join_last(frames, ref, upper, high)
        return
    half, count = (ref.low if bit == 0 else ref.new_before).shape[:2]
    if early:
        partner = spans_of(message[half * count :, :], half)
        ref.new_meta[...] = jnp.zeros_like(ref.new_meta)
    spans = []
    for b in range(half):
        row = slice(b, b + 1)
        rate = table[b, 3 * frames + 1 : 3 * frames + 2]
        if early:
            meta = ref.new_meta
            mine = table[b, 3 * frames : 3 * frames + 1] if bit == 0 else ref.meta[SPAN, row]
            prefix = jnp.zeros_like(mine) if bit == 0 else ref.meta[PREFIX, row]
            meta[MINE, row] = mine
            meta[BEFORE, row] = prefix
            meta[THEIRS, row] = partner[b]
            meta[SPAN, row] = mine + partner[b]
            if bit == 0:
                meta[LOW, row] = jnp.where(high, partner[b], mine)
            else:
                meta[LOW, row] = ref.meta[LOW, row]
                meta[PREFIX, row] = prefix + jnp.where(upper, partner[b], 0.0)
            theirs_span = partner[b]
        else:
            meta = ref.meta
            mine, prefix, theirs_span = meta[MINE, row], meta[BEFORE, row], meta[THEIRS, row]
        spans.append(mine + theirs_span)
        theirs = message[b * count : (b + 1) * count].astype(F32)
        own = ref.end[b] if bit == 0 else ref.total[b]
        keep = jnp.where(upper, 1.0, jnp.exp(-rate * theirs_span))
        add = jnp.where(upper, jnp.exp(-rate * mine), 1.0)
        whole = keep * own + add * theirs
        if ref.new_total is not None:
            ref.new_total[b] = whole
        if bit == 0:
            ref.low[b] = jnp.where(high, theirs, own)
        else:
            now = jnp.where(upper, jnp.exp(-rate * prefix), 0.0) * theirs
            ref.new_before[b] = now if bit == 1 else ref.before[b] + now
        if not combine:
            ref.outgoing[b * count : (b + 1) * count] = whole.astype(BF16)
        elif not early:
            many = ref.early_total.shape[1]
            ref.outgoing[b * many : (b + 1) * many] = ref.early_total[b].astype(BF16)
            at = half * many + b * count
            ref.outgoing[at : at + count] = whole.astype(BF16)
    if early != combine:
        rows = ref.outgoing.shape[0]
        ref.outgoing[rows - tile_rows(half) : rows] = span_tile(spans)


def join_last(frames, ref, upper, high):
    half, many = ref.early_low.shape[:2]
    for b in range(half):
        row = slice(b, b + 1)
        rate = ref.table[b, 3 * frames + 1 : 3 * frames + 2]
        scale = jnp.where(upper, jnp.exp(-rate * ref.meta[PREFIX, row]), 0.0)
        low_decay = jnp.exp(-rate * ref.meta[LOW, row])
        for late, low, before in ((False, ref.early_low, ref.early_before), (True, ref.late_low, ref.late_before)):
            count = low.shape[1]
            at = b * count + (half * many if late else 0)
            now = scale * ref.message[at : at + count].astype(F32)
            if before is not None:
                now = now + before[b]
            below = low_decay * now + low[b]
            mine = jnp.where(high, below, now)
            theirs = jnp.where(high, now, below).astype(BF16)
            place = slice(many, many + count) if late else slice(0, count)
            ref.incoming[b, place] = mine
            ref.back[b, place] = theirs
            if late:
                ref.ring[b] = mine.astype(BF16)
                ref.diagonal[b] = theirs


def incoming_edges_kernel(width, own, other, edge):
    half, cells = own.shape[:2]
    rows = slice(cells - 2 * width, cells - width)
    edge[:half] = own[:, rows].astype(BF16)
    edge[half:] = other[:, rows]


def gelu(x):
    return 0.5 * x * (1.0 + lax.erf(x * 0.7071067811865476))


def mix_kernel(part, width, incoming, local_inner, local_swap, local_ring, table, weight, video, inner, outer, framed):
    half, frames, many, states = local_inner.shape
    cells, channels = video.shape[2:]
    first = part * half
    even = even_strip()
    for b in range(half):
        for t in range(frames):
            product = table[first + b, 2 * frames + t : 2 * frames + t + 1]
            at = (b * frames + t) * cells
            x = local_inner[b, t] + product * incoming[b, :many].astype(F32)
            put(framed, (pl.ds(at + width, many),), x, width)
            swap = local_swap[b, t] + product * incoming[b, many : many + width].astype(F32)
            ring = local_ring[b, t] + product * incoming[b, many + width :].astype(F32)
            put(framed, (pl.ds(at, width),), jnp.where(even, ring, swap), width)
            put(framed, (pl.ds(at + cells - width, width),), jnp.where(even, swap, ring), width)
    less = cells - width
    for b in range(half):
        block = framed[pl.ds(b * frames * cells, frames * cells), :]
        frame = block.reshape(frames, cells, 3 * states)
        total = jnp.dot(block, weight[1], preferred_element_type=F32).reshape(frames, cells, channels)
        above = jnp.dot(frame[:, :less].reshape(-1, 3 * states), weight[0], preferred_element_type=F32).reshape(frames, less, channels)
        below = jnp.dot(frame[:, width:].reshape(-1, 3 * states), weight[2], preferred_element_type=F32).reshape(frames, less, channels)
        outer[0, b] = total[:, :width] + below[:, :width]
        outer[1, b] = total[:, less:] + above[:, less - width :]
        middle = total[:, width:less] + above[:, : less - width] + below[:, width:]
        inner[b] = (video[lanes(half)[part] + b, :, width:less].astype(F32) + gelu(middle)).astype(BF16)


def edge_rows(side, width, outer_own, outer_other, halo_local, incoming, table, weight, video, framed, edge, then):
    batch, frames, cells, channels = video.shape
    half = batch // 2

    def product(b, t):
        return table[b, 2 * frames + t : 2 * frames + t + 1]

    even = even_strip()
    below = even if side == 0 else jnp.logical_not(even)
    below = below.astype(jnp.int32)
    x = halo_block(0, batch, halo_local, product, incoming)
    if side == 1:
        x = jnp.where(ring_open(), x, jnp.zeros_like(x))
    put(framed, (slice(None),), x, width)
    more = jnp.dot(framed[...], weight[2 * below], preferred_element_type=F32).reshape(batch, frames, width, channels)
    row = aligned(below * (cells - width), width)
    for lane, outer in enumerate((outer_own, outer_other)):
        at = slice(lane * half, (lane + 1) * half)
        mixed = outer[below] + more[at]
        edge[at] = (video[pl.ds(lanes(half)[lane], half), :, pl.ds(row, width), :].astype(F32) + gelu(mixed)).astype(BF16)
        then(lane, row)


def finish_swap_kernel(width, outer_own, outer_other, halo_local, halo_in, table, weight, video, edge, framed):
    def incoming(b):
        return halo_in[b]

    edge_rows(0, width, outer_own, outer_other, halo_local, incoming, table, weight, video, framed, edge, lambda lane, row: None)


def finish_ring_kernel(
    width, outer_own, outer_other, halo_local, own_in, other_in, table, weight, video, inner_own, inner_other, done, out, framed, edge, sems
):
    def incoming(b):
        return own_in[b] if b < half else other_in[b - half]

    batch, _, cells, _ = video.shape
    half = batch // 2
    first = lanes(half)
    copies = []

    def write(source, lane, row, count, kind):
        dest = out.at[pl.ds(first[lane], half), :, pl.ds(row, count), :]
        copies.append(pltpu.make_async_copy(source, dest, sems.at[kind, lane]))
        copies[-1].start()

    swap_row = aligned(even_strip().astype(jnp.int32) * (cells - width), width)
    for lane, inner in enumerate((inner_own, inner_other)):
        write(inner, lane, width, cells - 2 * width, 0)
        write(done.at[pl.ds(lane * half, half)], lane, swap_row, width, 1)

    def then(lane, row):
        write(edge.at[pl.ds(lane * half, half)], lane, row, width, 2)

    edge_rows(1, width, outer_own, outer_other, halo_local, incoming, table, weight, video, framed, edge, then)
    for copy in copies:
        copy.wait()


def on_device(video, weight_in, weight_out, rates, gaps):
    batch, frames, rows, width, channels = video.shape
    states = weight_in.shape[3]
    half = batch // 2
    cells = rows * width
    blocks = lax.axis_size("tm")
    strips = lax.axis_size("rows")
    rounds = blocks.bit_length() - 1
    swap = [(i, i ^ 1) for i in range(strips)]

    def ring_partner(block, strip):
        if strip in (0, strips - 1):
            return block ^ 1, strip
        return block, strip + 1 if strip % 2 else strip - 1

    def diagonal_partner(block, strip):
        return block ^ 1, ring_partner(block, strip)[1]

    places = [(block, strip) for block in range(blocks) for strip in range(strips)]

    def linear(partner):
        return [(block * strips + strip, partner(block, strip)[0] * strips + partner(block, strip)[1]) for block, strip in places]

    ring, diagonal = linear(ring_partner), linear(diagonal_partner)

    def across(bit):
        mask = 1 if bit == 0 else 2 ** (bit + 1) - 2
        return [(i, i ^ mask) for i in range(blocks)]

    def in_hbm(x):
        return pltpu.with_memory_space_constraint(x, pltpu.HBM)

    video = video.reshape(batch, frames, cells, channels)
    weight_in = weight_in.reshape(3, 3 * channels, states)
    weight_out = weight_out.reshape(3, 3 * states, channels)
    edge_flops = 2 * batch * frames * width * 6 * channels * states
    own_flops = 5 * edge_flops

    edge = like(batch, frames, width, channels, dtype=BF16)
    ring_video, swap_video, video_other = call(
        functools.partial(edges_kernel, width), [in_hbm(video)], [edge, edge, like(half, frames, cells, channels, dtype=BF16)],
        [pltpu.SemaphoreType.DMA((3, 2))], [HBM], flops=1 << 31, bytes_accessed=1 << 26,
    )
    ring_video = lax.ppermute(ring_video, ("tm", "rows"), ring)
    swap_video = lax.ppermute(swap_video, "rows", swap)

    many = cells - 2 * width
    count = (many + width, width)
    local_inner = like(half, frames, many, states)
    local_edge = like(half, frames, width, states)
    end = [like(half, n, states) for n in count]
    message = [like(half * count[0] + tile_rows(half), states, dtype=BF16), like(half * width, states, dtype=BF16)]
    both = like(half * (many + 2 * width) + tile_rows(half), states, dtype=BF16)
    rows_in_table = table_rows(frames)
    inner_other, driven_swap, driven_ring, table = call(
        functools.partial(own_kernel, width), [in_hbm(gaps), in_hbm(rates[None, :]), weight_in, video_other],
        [local_inner, local_edge, local_edge, like(batch, rows_in_table, states)],
        [
            pltpu.VMEM((half * frames * cells, 3 * channels), BF16),
            pltpu.VMEM((half, frames, cells, states), F32),
            pltpu.SMEM(gaps.shape, F32),
            pltpu.VMEM((1, states), F32),
            pltpu.SemaphoreType.DMA((2,)),
        ],
        [HBM] * 2 + [VMEM] * 2, mib=16, flops=own_flops // 2,
    )
    weight = weight_in
    meta_shape = like(6, 8, states)
    halo = like(batch, frames, width, states, dtype=BF16)
    framed = pltpu.VMEM((half * frames * width, 3 * channels), BF16)
    incoming = [None, None]
    swap_other, outgoing = call(
        functools.partial(scan_edge_kernel, False, width), [driven_swap, table, weight, swap_video, inner_other],
        [local_edge, message[0]], [framed], flops=edge_flops // 4,
    )
    incoming[0] = lax.ppermute(outgoing, "tm", across(0))
    ring_other, outgoing = call(
        functools.partial(scan_edge_kernel, True, width), [driven_ring, table, weight, ring_video],
        [local_edge, message[1]], [framed], flops=edge_flops // 4,
    )
    incoming[1] = lax.ppermute(outgoing, "tm", across(0))
    inner_own, swap_own, ring_own, *own_end, ring_local, swap_local = call(
        functools.partial(scan_own_kernel, width), [video, weight, table, swap_video, ring_video, swap_other, ring_other],
        [local_inner, local_edge, local_edge, *end, halo, halo],
        [pltpu.VMEM((half * frames, cells + 2 * width, 3 * channels), BF16), pltpu.VMEM((half, frames, cells, states), F32)],
        mib=16, flops=own_flops // 2,
    )
    ring_local = lax.ppermute(ring_local, ("tm", "rows"), ring)
    swap_local = lax.ppermute(swap_local, "rows", swap)

    def join(early, bit, combine, last, ins, outs):
        kernel = functools.partial(join_kernel, frames, early, bit, combine, last, tuple(ins) + tuple(outs))
        return Refs(outs, call(kernel, list(ins.values()), list(outs.values())))

    final = rounds - 1
    total, before, low, meta = [None, None], [None, None], [None, None], None
    for bit in range(final):
        combine = bit + 1 == final
        for late in range(2):
            ins = dict(message=incoming[late], table=table)
            outs = dict() if late and combine else dict(new_total=end[late])
            if bit == 0:
                ins.update(end=own_end[late])
                outs.update(low=end[late])
            else:
                ins.update(total=total[late])
                outs.update(new_before=end[late])
            if bit > 1:
                ins.update(before=before[late])
            if bit or late:
                ins.update(meta=meta)
            if not late:
                outs.update(new_meta=meta_shape)
            if not combine:
                outs.update(outgoing=message[late])
            elif late:
                ins.update(early_total=total[0])
                outs.update(outgoing=both)
            got = join(not late, bit, combine, False, ins, outs)
            total[late] = got.new_total
            before[late] = got.new_before
            if bit == 0:
                low[late] = got.low
            if not late:
                meta = got.new_meta
            if got.outgoing is not None:
                incoming[late] = lax.ppermute(got.outgoing, "tm", across(bit + 1))
    ins = dict(message=incoming[1], table=table, meta=meta, early_low=low[0], late_low=low[1])
    if before[0] is not None:
        ins.update(early_before=before[0], late_before=before[1])
    edge = like(half, width, states, dtype=BF16)
    outs = dict(incoming=like(half, cells, states), back=like(half, cells, states, dtype=BF16), ring=edge, diagonal=edge)
    got = join(True, final, True, True, ins, outs)
    into_other = lax.ppermute(got.back, "tm", across(0))
    diagonal = lax.ppermute(got.diagonal, ("tm", "rows"), diagonal)
    ring_in = lax.ppermute(got.ring, ("tm", "rows"), ring)

    def mix(part, into, local, flops):
        return call(
            functools.partial(mix_kernel, part, width), [into, *local, table, weight_out, video],
            [like(half, frames, cells - 2 * width, channels, dtype=BF16), like(2, half, frames, width, channels)],
            [pltpu.VMEM((half * frames * cells, 3 * states), BF16)], mib=16, flops=flops,
        )

    inner_own, outer_own = mix(0, got.incoming, (inner_own, swap_own, ring_own), own_flops // 2)
    edge = like(batch, width, states, dtype=BF16)
    swap_in, = call(functools.partial(incoming_edges_kernel, width), [got.incoming, into_other], [edge])
    swap_in = lax.ppermute(swap_in, "rows", swap)
    inner_other, outer_other = mix(1, into_other, (inner_other, swap_other, ring_other), own_flops // 2)
    common = [outer_own, outer_other]
    framed = pltpu.VMEM((batch * frames * width, 3 * states), BF16)
    edge = like(batch, frames, width, channels, dtype=BF16)
    done, = call(
        functools.partial(finish_swap_kernel, width), common + [swap_local, swap_in, table, weight_out, video],
        [edge], [framed], mib=16, flops=edge_flops // 2,
    )
    out, = call(
        functools.partial(finish_ring_kernel, width),
        common + [ring_local, ring_in, diagonal, table, weight_out, video, inner_own, inner_other, done],
        [like(batch, frames, cells, channels, dtype=BF16)],
        [framed, pltpu.VMEM(edge.shape, BF16), pltpu.SemaphoreType.DMA((3, 2))], mib=16, flops=edge_flops // 2, out_space=HBM,
    )
    return out.reshape(batch, frames, rows, width, channels)


def solution(mesh):
    in_specs = (P(None, "tm", "rows", None, None), P(), P(), P(), P(None, "tm"))
    out_specs = P(None, "tm", "rows", None, None)

    return jax.shard_map(on_device, mesh=mesh, in_specs=in_specs, out_specs=out_specs, check_vma=False)
```

```python
import functools

import jax
import jax.numpy as jnp
from jax import lax
from jax.experimental import pallas as pl
from jax.experimental.pallas import tpu as pltpu
from jax.sharding import PartitionSpec as P


F32 = jnp.float32
BF16 = jnp.bfloat16
SMEM = pl.BlockSpec(memory_space=pltpu.SMEM)
VMEM = pl.BlockSpec(memory_space=pltpu.VMEM)
HBM = pl.BlockSpec(memory_space=pltpu.HBM)


def call(kernel, args, outs, scratch=(), specs=None, mib=8, flops=1 << 20, bytes_accessed=1 << 20, out_space=VMEM):
    return pl.pallas_call(
        kernel,
        out_shape=outs,
        in_specs=specs or [VMEM] * len(args),
        out_specs=[out_space] * len(outs),
        scratch_shapes=list(scratch),
        compiler_params=pltpu.CompilerParams(vmem_limit_bytes=mib << 20),
        cost_estimate=pl.CostEstimate(flops=flops, bytes_accessed=bytes_accessed, transcendentals=0),
    )(*args)


def like(*shape, dtype=F32):
    return jax.ShapeDtypeStruct(shape, dtype)


def even_strip():
    return lax.axis_index("rows") % 2 == 0


def aligned(start, step):
    return pl.multiple_of(start, step)


def row_places(width, cells):
    even = even_strip()
    last = cells - width
    return aligned(jnp.where(even, last, 0), width), aligned(jnp.where(even, 0, last), width)


def with_shifts(x, width):
    rows = x.shape[0]
    x = x.astype(F32)
    column = lax.broadcasted_iota(jnp.int32, (rows, 1), 0) % width
    left = jnp.where(column == 0, 0.0, pltpu.roll(x, 1, 0))
    right = jnp.where(column == width - 1, 0.0, pltpu.roll(x, rows - 1, 0))
    return left.astype(BF16), x.astype(BF16), right.astype(BF16)


def put(dest, index, x, width):
    c = x.shape[1]
    for i, part in enumerate(with_shifts(x, width)):
        dest[index + (slice(i * c, (i + 1) * c),)] = part


def tile_rows(half):
    return -(-3 * half // 8) * 8


def span_tile(spans):
    rows = []
    for span in spans:
        high = span.astype(BF16).astype(F32)
        rest = span - high
        middle = rest.astype(BF16).astype(F32)
        rows += [high, middle, rest - middle]
    index = lax.broadcasted_iota(jnp.int32, (tile_rows(len(spans)), rows[0].shape[1]), 0)
    tile = jnp.zeros(index.shape, F32)
    for i, row in enumerate(rows):
        tile = jnp.where(index == i, row, tile)
    return tile.astype(BF16)


def spans_of(tile, half):
    tile = tile.astype(F32)
    return [tile[3 * b : 3 * b + 1] + tile[3 * b + 1 : 3 * b + 2] + tile[3 * b + 2 : 3 * b + 3] for b in range(half)]


def lanes(half):
    high = lax.axis_index("tm") % 2
    return high * half, (1 - high) * half


def edges_kernel(width, video_hbm, ring, swap, video, sems):
    half = video.shape[0] // 2
    copies = [
        pltpu.make_async_copy(video_hbm.at[pl.ds(first, half)], video.at[pl.ds(lane * half, half)], sems.at[lane])
        for lane, first in enumerate(lanes(half))
    ]
    for copy in copies:
        copy.start()
    for copy in copies:
        copy.wait()
    swap_row, ring_row = row_places(width, video.shape[2])
    ring[...] = video[:, :, pl.ds(ring_row, width), :]
    swap[...] = video[:, :, pl.ds(swap_row, width), :]


def own_kernel(width, gaps_hbm, rates_hbm, weight, video, local, driven_swap, driven_ring, table, framed, full, gaps, rates, sems):
    half, frames, inner, states = local.shape
    batch, cells, channels = table.shape[0], video.shape[2], video.shape[3]
    first = lanes(half)
    copies = [pltpu.make_async_copy(gaps_hbm, gaps, sems.at[0]), pltpu.make_async_copy(rates_hbm, rates, sems.at[1])]
    for copy in copies:
        copy.start()
    for b in range(half):
        put(framed, (pl.ds(b * frames * cells, frames * cells),), video[half + b].reshape(frames * cells, channels), width)
    less = cells - width
    block = framed[...]
    frame = block.reshape(half * frames, cells, 3 * channels)
    total = jnp.dot(block, weight[1], preferred_element_type=F32)
    full[...] = total.reshape(half, frames, cells, states)
    above = jnp.dot(frame[:, :less].reshape(-1, 3 * channels), weight[0], preferred_element_type=F32)
    full[:, :, width:, :] += above.reshape(half, frames, less, states)
    below = jnp.dot(frame[:, width:].reshape(-1, 3 * channels), weight[2], preferred_element_type=F32)
    full[:, :, :less, :] += below.reshape(half, frames, less, states)
    for copy in copies:
        copy.wait()
    rate = rates[...]
    for b in range(batch):
        span = None
        for t in range(frames):
            gap = gaps[first[b // half] + b % half, t]
            span = gap if span is None else span + gap
            decay = jnp.exp(-rate * gap)
            table[b, t : t + 1] = decay
            table[b, frames + t : frames + t + 1] = jnp.sqrt(1.0 - decay * decay)
            table[b, 2 * frames + t : 2 * frames + t + 1] = jnp.exp(-rate * span)
        table[b, 3 * frames : 3 * frames + 1] = jnp.zeros((1, states), F32) + span
        table[b, 3 * frames + 1 : 3 * frames + 2] = rate
    swap_row, ring_row = row_places(width, cells)
    for b in range(half):
        driven_swap[b] = full[b, :, pl.ds(swap_row, width), :]
        driven_ring[b] = full[b, :, pl.ds(ring_row, width), :]
        for r in range(0, inner, width):

            def value_of(t):
                return full[b, t, width + r : 2 * width + r]

            recurrence(b, half + b, slice(r, r + width), table, local, value_of)


def table_rows(frames):
    return -(-(3 * frames + 2) // 8) * 8


def ring_open():
    strip = lax.axis_index("rows")
    return jnp.logical_and(strip != 0, strip != lax.axis_size("rows") - 1)


def halo_block(first, half, halo, product=None, incoming=None):
    frames, width, c = halo.shape[1:]
    x = halo[first : first + half]
    if product is None:
        return x.reshape(half * frames * width, c)
    pieces = []
    for b in range(half):
        more = incoming(first + b).astype(F32)
        pieces += [x[b, t].astype(F32) + product(b, t) * more for t in range(frames)]
    return jnp.concatenate(pieces, axis=0)


def recurrence(b, at, rows, table, local, value_of):
    frames = local.shape[1]
    state = None
    for t in range(frames):
        value = table[at, frames + t : frames + t + 1] * value_of(t)
        state = value if state is None else table[at, t : t + 1] * state + value
        local[b, t, rows] = state
    return state


def scan_edge_kernel(late, width, driven, table, weight, halo, *refs):
    if late:
        local, message, framed = refs
    else:
        inner, local, message, framed = refs
    half, frames = local.shape[:2]
    below = even_strip().astype(jnp.int32)
    x = halo_block(half, half, halo)
    if late:
        below = 1 - below
        x = jnp.where(ring_open(), x, jnp.zeros_like(x))
    put(framed, (slice(None),), x, width)
    more = jnp.dot(framed[...], weight[2 * below], preferred_element_type=F32)
    for b in range(half):

        def value_of(t):
            at = (b * frames + t) * width
            return driven[b, t] + more[at : at + width]

        state = recurrence(b, half + b, slice(0, width), table, local, value_of)
        if late:
            message[b * width : (b + 1) * width] = state.astype(BF16)
        else:
            many = inner.shape[2]
            at = b * (many + width)
            message[at : at + many] = inner[b, frames - 1].astype(BF16)
            message[at + many : at + many + width] = state.astype(BF16)
    if not late:
        rows = message.shape[0]
        message[rows - tile_rows(half) : rows] = span_tile([table[half + b, 3 * frames : 3 * frames + 1] for b in range(half)])


def scan_own_kernel(
    width, video, weight, table, swap, ring, other_swap, other_ring,
    inner, swap_local, ring_local, end_early, end_late, ring_out, swap_out, framed, full,
):
    half, frames, many, states = inner.shape
    cells, channels = video.shape[2:]
    even = even_strip()
    swap_row, ring_row = row_places(width, cells)
    open_ring = ring_open()
    for b in range(half):
        for t in range(frames):
            f = b * frames + t
            put(framed, (f, pl.ds(width, cells)), video[b, t], width)
            x = ring[b, t]
            x = jnp.where(open_ring, x, jnp.zeros_like(x))
            put(framed, (f, pl.ds(0, width)), jnp.where(even, x, swap[b, t]), width)
            put(framed, (f, pl.ds(cells + width, width)), jnp.where(even, swap[b, t], x), width)
    for b in range(half):
        total = None
        for d in range(3):
            lhs = framed[b * frames : (b + 1) * frames, d * width : d * width + cells].reshape(frames * cells, 3 * channels)
            term = jnp.dot(lhs, weight[d], preferred_element_type=F32)
            total = term if total is None else total + term
        full[b] = total.reshape(frames, cells, states)
        for r in range(0, many, width):
            end_early[b, r : r + width] = recurrence(
                b, b, slice(r, r + width), table, inner, lambda t: full[b, t, width + r : 2 * width + r]
            )
        every = slice(0, width)
        end_early[b, many : many + width] = recurrence(b, b, every, table, swap_local, lambda t: full[b, t, pl.ds(swap_row, width), :])
        end_late[b] = recurrence(b, b, every, table, ring_local, lambda t: full[b, t, pl.ds(ring_row, width), :])
    swap_out[:half] = swap_local[...].astype(BF16)
    swap_out[half:] = other_swap[...].astype(BF16)
    ring_out[:half] = ring_local[...].astype(BF16)
    ring_out[half:] = other_ring[...].astype(BF16)


SPAN, PREFIX, LOW, THEIRS, MINE, BEFORE = range(6)


class Refs:
    message = table = end = total = before = meta = early_total = early_low = late_low = early_before = late_before = None
    new_total = new_before = new_meta = low = outgoing = incoming = back = ring = diagonal = None

    def __init__(self, names, refs):
        self.__dict__.update(zip(names, refs))


def join_kernel(frames, early, bit, combine, last, names, *refs):
    ref = Refs(names, refs)
    table, message = ref.table, ref.message
    place = lax.axis_index("tm")
    upper = (place >> bit) % 2 == 1
    high = place % 2 == 1
    if last:
        join_last(frames, ref, upper, high)
        return
    half, count = (ref.low if bit == 0 else ref.new_before).shape[:2]
    if early:
        partner = spans_of(message[half * count :, :], half)
        ref.new_meta[...] = jnp.zeros_like(ref.new_meta)
    spans = []
    for b in range(half):
        row = slice(b, b + 1)
        rate = table[b, 3 * frames + 1 : 3 * frames + 2]
        if early:
            meta = ref.new_meta
            mine = table[b, 3 * frames : 3 * frames + 1] if bit == 0 else ref.meta[SPAN, row]
            prefix = jnp.zeros_like(mine) if bit == 0 else ref.meta[PREFIX, row]
            meta[MINE, row] = mine
            meta[BEFORE, row] = prefix
            meta[THEIRS, row] = partner[b]
            meta[SPAN, row] = mine + partner[b]
            if bit == 0:
                meta[LOW, row] = jnp.where(high, partner[b], mine)
            else:
                meta[LOW, row] = ref.meta[LOW, row]
                meta[PREFIX, row] = prefix + jnp.where(upper, partner[b], 0.0)
            theirs_span = partner[b]
        else:
            meta = ref.meta
            mine, prefix, theirs_span = meta[MINE, row], meta[BEFORE, row], meta[THEIRS, row]
        spans.append(mine + theirs_span)
        theirs = message[b * count : (b + 1) * count].astype(F32)
        own = ref.end[b] if bit == 0 else ref.total[b]
        keep = jnp.where(upper, 1.0, jnp.exp(-rate * theirs_span))
        add = jnp.where(upper, jnp.exp(-rate * mine), 1.0)
        whole = keep * own + add * theirs
        if ref.new_total is not None:
            ref.new_total[b] = whole
        if bit == 0:
            ref.low[b] = jnp.where(high, theirs, own)
        else:
            now = jnp.where(upper, jnp.exp(-rate * prefix), 0.0) * theirs
            ref.new_before[b] = now if bit == 1 else ref.before[b] + now
        if not combine:
            ref.outgoing[b * count : (b + 1) * count] = whole.astype(BF16)
        elif not early:
            many = ref.early_total.shape[1]
            ref.outgoing[b * many : (b + 1) * many] = ref.early_total[b].astype(BF16)
            at = half * many + b * count
            ref.outgoing[at : at + count] = whole.astype(BF16)
    if early != combine:
        rows = ref.outgoing.shape[0]
        ref.outgoing[rows - tile_rows(half) : rows] = span_tile(spans)


def join_last(frames, ref, upper, high):
    half, many = ref.early_low.shape[:2]
    for b in range(half):
        row = slice(b, b + 1)
        rate = ref.table[b, 3 * frames + 1 : 3 * frames + 2]
        scale = jnp.where(upper, jnp.exp(-rate * ref.meta[PREFIX, row]), 0.0)
        low_decay = jnp.exp(-rate * ref.meta[LOW, row])
        for late, low, before in ((False, ref.early_low, ref.early_before), (True, ref.late_low, ref.late_before)):
            count = low.shape[1]
            at = b * count + (half * many if late else 0)
            now = scale * ref.message[at : at + count].astype(F32)
            if before is not None:
                now = now + before[b]
            below = low_decay * now + low[b]
            mine = jnp.where(high, below, now)
            theirs = jnp.where(high, now, below).astype(BF16)
            place = slice(many, many + count) if late else slice(0, count)
            ref.incoming[b, place] = mine
            ref.back[b, place] = theirs
            if late:
                ref.ring[b] = mine.astype(BF16)
                ref.diagonal[b] = theirs


def incoming_edges_kernel(width, own, other, edge):
    half, cells = own.shape[:2]
    rows = slice(cells - 2 * width, cells - width)
    edge[:half] = own[:, rows].astype(BF16)
    edge[half:] = other[:, rows]


def gelu(x):
    return 0.5 * x * (1.0 + lax.erf(x * 0.7071067811865476))


def mix_kernel(part, width, incoming, local_inner, local_swap, local_ring, table, weight, video, inner, outer, framed):
    half, frames, many, states = local_inner.shape
    cells, channels = video.shape[2:]
    first = part * half
    even = even_strip()
    for b in range(half):
        for t in range(frames):
            product = table[first + b, 2 * frames + t : 2 * frames + t + 1]
            at = (b * frames + t) * cells
            x = local_inner[b, t] + product * incoming[b, :many].astype(F32)
            put(framed, (pl.ds(at + width, many),), x, width)
            swap = local_swap[b, t] + product * incoming[b, many : many + width].astype(F32)
            ring = local_ring[b, t] + product * incoming[b, many + width :].astype(F32)
            put(framed, (pl.ds(at, width),), jnp.where(even, ring, swap), width)
            put(framed, (pl.ds(at + cells - width, width),), jnp.where(even, swap, ring), width)
    less = cells - width
    block = framed[...]
    frame = block.reshape(half, frames, cells, 3 * states)
    total = jnp.dot(block, weight[1], preferred_element_type=F32).reshape(half, frames, cells, channels)
    above = jnp.dot(frame[:, :, :less].reshape(-1, 3 * states), weight[0], preferred_element_type=F32).reshape(half, frames, less, channels)
    below = jnp.dot(frame[:, :, width:].reshape(-1, 3 * states), weight[2], preferred_element_type=F32).reshape(half, frames, less, channels)
    for b in range(half):
        outer[0, b] = total[b, :, :width] + below[b, :, :width]
        outer[1, b] = total[b, :, less:] + above[b, :, less - width :]
        middle = total[b, :, width:less] + above[b, :, : less - width] + below[b, :, width:]
        inner[b] = (video[first + b, :, width:less].astype(F32) + gelu(middle)).astype(BF16)


def edge_rows(side, width, outer_own, outer_other, halo_local, incoming, table, weight, video, framed, edge, then):
    batch, frames, cells, channels = video.shape
    half = batch // 2

    def product(b, t):
        return table[b, 2 * frames + t : 2 * frames + t + 1]

    even = even_strip()
    below = even if side == 0 else jnp.logical_not(even)
    below = below.astype(jnp.int32)
    x = halo_block(0, batch, halo_local, product, incoming)
    if side == 1:
        x = jnp.where(ring_open(), x, jnp.zeros_like(x))
    put(framed, (slice(None),), x, width)
    more = jnp.dot(framed[...], weight[2 * below], preferred_element_type=F32).reshape(batch, frames, width, channels)
    row = aligned(below * (cells - width), width)
    for lane, outer in enumerate((outer_own, outer_other)):
        at = slice(lane * half, (lane + 1) * half)
        mixed = outer[below] + more[at]
        edge[at] = (video[at, :, pl.ds(row, width), :].astype(F32) + gelu(mixed)).astype(BF16)
        then(lane, row)


def finish_kernel(
    width, outer_own, outer_other, swap_local, swap_in, ring_local, own_in, other_in, table, weight, video, inner_own, inner_other,
    out, framed, edge, sems,
):
    batch, _, cells, _ = video.shape
    half = batch // 2
    first = lanes(half)
    copies = []

    def write(source, lane, row, count, kind):
        dest = out.at[pl.ds(first[lane], half), :, pl.ds(row, count), :]
        copies.append(pltpu.make_async_copy(source, dest, sems.at[kind, lane]))
        copies[-1].start()

    for lane, inner in enumerate((inner_own, inner_other)):
        write(inner, lane, width, cells - 2 * width, 2)

    def from_swap(b):
        return swap_in[b]

    def from_ring(b):
        return own_in[b] if b < half else other_in[b - half]

    for side, local, incoming in ((0, swap_local, from_swap), (1, ring_local, from_ring)):

        def then(lane, row):
            write(edge.at[side, pl.ds(lane * half, half)], lane, row, width, side)

        edge_rows(side, width, outer_own, outer_other, local, incoming, table, weight, video, framed.at[side], edge.at[side], then)
    for copy in copies:
        copy.wait()


def on_device(video, weight_in, weight_out, rates, gaps):
    batch, frames, rows, width, channels = video.shape
    states = weight_in.shape[3]
    half = batch // 2
    cells = rows * width
    blocks = lax.axis_size("tm")
    strips = lax.axis_size("rows")
    rounds = blocks.bit_length() - 1
    swap = [(i, i ^ 1) for i in range(strips)]

    def ring_partner(block, strip):
        if strip in (0, strips - 1):
            return block ^ 1, strip
        return block, strip + 1 if strip % 2 else strip - 1

    def diagonal_partner(block, strip):
        return block ^ 1, ring_partner(block, strip)[1]

    places = [(block, strip) for block in range(blocks) for strip in range(strips)]

    def linear(partner):
        return [(block * strips + strip, partner(block, strip)[0] * strips + partner(block, strip)[1]) for block, strip in places]

    ring, diagonal = linear(ring_partner), linear(diagonal_partner)

    def across(bit):
        mask = 1 if bit == 0 else 2 ** (bit + 1) - 2
        return [(i, i ^ mask) for i in range(blocks)]

    def in_hbm(x):
        return pltpu.with_memory_space_constraint(x, pltpu.HBM)

    video = video.reshape(batch, frames, cells, channels)
    weight_in = weight_in.reshape(3, 3 * channels, states)
    weight_out = weight_out.reshape(3, 3 * states, channels)
    edge_flops = 2 * batch * frames * width * 6 * channels * states
    own_flops = 5 * edge_flops

    edge = like(batch, frames, width, channels, dtype=BF16)
    ring_video, swap_video, video = call(
        functools.partial(edges_kernel, width), [in_hbm(video)], [edge, edge, like(*video.shape, dtype=BF16)],
        [pltpu.SemaphoreType.DMA((2,))], [HBM], flops=1 << 31, bytes_accessed=1 << 26,
    )
    ring_video = lax.ppermute(ring_video, ("tm", "rows"), ring)
    swap_video = lax.ppermute(swap_video, "rows", swap)

    many = cells - 2 * width
    count = (many + width, width)
    local_inner = like(half, frames, many, states)
    local_edge = like(half, frames, width, states)
    end = [like(half, n, states) for n in count]
    message = [like(half * count[0] + tile_rows(half), states, dtype=BF16), like(half * width, states, dtype=BF16)]
    both = like(half * (many + 2 * width) + tile_rows(half), states, dtype=BF16)
    rows_in_table = table_rows(frames)
    inner_other, driven_swap, driven_ring, table = call(
        functools.partial(own_kernel, width), [in_hbm(gaps), in_hbm(rates[None, :]), weight_in, video],
        [local_inner, local_edge, local_edge, like(batch, rows_in_table, states)],
        [
            pltpu.VMEM((half * frames * cells, 3 * channels), BF16),
            pltpu.VMEM((half, frames, cells, states), F32),
            pltpu.SMEM(gaps.shape, F32),
            pltpu.VMEM((1, states), F32),
            pltpu.SemaphoreType.DMA((2,)),
        ],
        [HBM] * 2 + [VMEM] * 2, mib=16, flops=own_flops // 2,
    )
    weight = weight_in
    meta_shape = like(6, 8, states)
    halo = like(batch, frames, width, states, dtype=BF16)
    framed = pltpu.VMEM((half * frames * width, 3 * channels), BF16)
    incoming = [None, None]
    swap_other, outgoing = call(
        functools.partial(scan_edge_kernel, False, width), [driven_swap, table, weight, swap_video, inner_other],
        [local_edge, message[0]], [framed], flops=edge_flops // 4,
    )
    incoming[0] = lax.ppermute(outgoing, "tm", across(0))
    ring_other, outgoing = call(
        functools.partial(scan_edge_kernel, True, width), [driven_ring, table, weight, ring_video],
        [local_edge, message[1]], [framed], flops=edge_flops // 4,
    )
    incoming[1] = lax.ppermute(outgoing, "tm", across(0))
    inner_own, swap_own, ring_own, *own_end, ring_local, swap_local = call(
        functools.partial(scan_own_kernel, width), [video, weight, table, swap_video, ring_video, swap_other, ring_other],
        [local_inner, local_edge, local_edge, *end, halo, halo],
        [pltpu.VMEM((half * frames, cells + 2 * width, 3 * channels), BF16), pltpu.VMEM((half, frames, cells, states), F32)],
        mib=16, flops=own_flops // 2,
    )
    ring_local = lax.ppermute(ring_local, ("tm", "rows"), ring)
    swap_local = lax.ppermute(swap_local, "rows", swap)

    def join(early, bit, combine, last, ins, outs):
        kernel = functools.partial(join_kernel, frames, early, bit, combine, last, tuple(ins) + tuple(outs))
        return Refs(outs, call(kernel, list(ins.values()), list(outs.values())))

    final = rounds - 1
    total, before, low, meta = [None, None], [None, None], [None, None], None
    for bit in range(final):
        combine = bit + 1 == final
        for late in range(2):
            ins = dict(message=incoming[late], table=table)
            outs = dict() if late and combine else dict(new_total=end[late])
            if bit == 0:
                ins.update(end=own_end[late])
                outs.update(low=end[late])
            else:
                ins.update(total=total[late])
                outs.update(new_before=end[late])
            if bit > 1:
                ins.update(before=before[late])
            if bit or late:
                ins.update(meta=meta)
            if not late:
                outs.update(new_meta=meta_shape)
            if not combine:
                outs.update(outgoing=message[late])
            elif late:
                ins.update(early_total=total[0])
                outs.update(outgoing=both)
            got = join(not late, bit, combine, False, ins, outs)
            total[late] = got.new_total
            before[late] = got.new_before
            if bit == 0:
                low[late] = got.low
            if not late:
                meta = got.new_meta
            if got.outgoing is not None:
                incoming[late] = lax.ppermute(got.outgoing, "tm", across(bit + 1))
    ins = dict(message=incoming[1], table=table, meta=meta, early_low=low[0], late_low=low[1])
    if before[0] is not None:
        ins.update(early_before=before[0], late_before=before[1])
    edge = like(half, width, states, dtype=BF16)
    outs = dict(incoming=like(half, cells, states), back=like(half, cells, states, dtype=BF16), ring=edge, diagonal=edge)
    got = join(True, final, True, True, ins, outs)
    into_other = lax.ppermute(got.back, "tm", across(0))
    diagonal = lax.ppermute(got.diagonal, ("tm", "rows"), diagonal)
    ring_in = lax.ppermute(got.ring, ("tm", "rows"), ring)

    def mix(part, into, local, flops):
        return call(
            functools.partial(mix_kernel, part, width), [into, *local, table, weight_out, video],
            [like(half, frames, cells - 2 * width, channels, dtype=BF16), like(2, half, frames, width, channels)],
            [pltpu.VMEM((half * frames * cells, 3 * states), BF16)], mib=16, flops=flops,
        )

    inner_own, outer_own = mix(0, got.incoming, (inner_own, swap_own, ring_own), own_flops // 2)
    edge = like(batch, width, states, dtype=BF16)
    swap_in, = call(functools.partial(incoming_edges_kernel, width), [got.incoming, into_other], [edge])
    swap_in = lax.ppermute(swap_in, "rows", swap)
    inner_other, outer_other = mix(1, into_other, (inner_other, swap_other, ring_other), own_flops // 2)
    out, = call(
        functools.partial(finish_kernel, width),
        [outer_own, outer_other, swap_local, swap_in, ring_local, ring_in, diagonal, table, weight_out, video, inner_own, inner_other],
        [like(batch, frames, cells, channels, dtype=BF16)],
        [
            pltpu.VMEM((2, batch * frames * width, 3 * states), BF16),
            pltpu.VMEM((2, batch, frames, width, channels), BF16),
            pltpu.SemaphoreType.DMA((3, 2)),
        ],
        mib=16, flops=edge_flops, out_space=HBM,
    )
    return out.reshape(batch, frames, rows, width, channels)


def solution(mesh):
    in_specs = (P(None, "tm", "rows", None, None), P(), P(), P(), P(None, "tm"))
    out_specs = P(None, "tm", "rows", None, None)

    return jax.shard_map(on_device, mesh=mesh, in_specs=in_specs, out_specs=out_specs, check_vma=False)
```

```python
import functools

import jax
import jax.numpy as jnp
from jax import lax
from jax.experimental import pallas as pl
from jax.experimental.pallas import tpu as pltpu
from jax.sharding import PartitionSpec as P


F32 = jnp.float32
BF16 = jnp.bfloat16
SMEM = pl.BlockSpec(memory_space=pltpu.SMEM)
VMEM = pl.BlockSpec(memory_space=pltpu.VMEM)
HBM = pl.BlockSpec(memory_space=pltpu.HBM)


def call(kernel, args, outs, scratch=(), specs=None, mib=8, flops=1 << 20, bytes_accessed=1 << 20, out_space=VMEM):
    return pl.pallas_call(
        kernel,
        out_shape=outs,
        in_specs=specs or [VMEM] * len(args),
        out_specs=[out_space] * len(outs),
        scratch_shapes=list(scratch),
        compiler_params=pltpu.CompilerParams(vmem_limit_bytes=mib << 20),
        cost_estimate=pl.CostEstimate(flops=flops, bytes_accessed=bytes_accessed, transcendentals=0),
    )(*args)


def like(*shape, dtype=F32):
    return jax.ShapeDtypeStruct(shape, dtype)


def even_strip():
    return lax.axis_index("rows") % 2 == 0


def aligned(start, step):
    return pl.multiple_of(start, step)


def row_places(width, cells):
    even = even_strip()
    last = cells - width
    return aligned(jnp.where(even, last, 0), width), aligned(jnp.where(even, 0, last), width)


def with_shifts(x, width):
    rows = x.shape[0]
    x = x.astype(F32)
    column = lax.broadcasted_iota(jnp.int32, (rows, 1), 0) % width
    left = jnp.where(column == 0, 0.0, pltpu.roll(x, 1, 0))
    right = jnp.where(column == width - 1, 0.0, pltpu.roll(x, rows - 1, 0))
    return left.astype(BF16), x.astype(BF16), right.astype(BF16)


def put(dest, index, x, width):
    c = x.shape[1]
    for i, part in enumerate(with_shifts(x, width)):
        dest[index + (slice(i * c, (i + 1) * c),)] = part


def tile_rows(half):
    return -(-3 * half // 8) * 8


def span_tile(spans):
    rows = []
    for span in spans:
        high = span.astype(BF16).astype(F32)
        rest = span - high
        middle = rest.astype(BF16).astype(F32)
        rows += [high, middle, rest - middle]
    index = lax.broadcasted_iota(jnp.int32, (tile_rows(len(spans)), rows[0].shape[1]), 0)
    tile = jnp.zeros(index.shape, F32)
    for i, row in enumerate(rows):
        tile = jnp.where(index == i, row, tile)
    return tile.astype(BF16)


def spans_of(tile, half):
    tile = tile.astype(F32)
    return [tile[3 * b : 3 * b + 1] + tile[3 * b + 1 : 3 * b + 2] + tile[3 * b + 2 : 3 * b + 3] for b in range(half)]


def lanes(half):
    high = lax.axis_index("tm") % 2
    return high * half, (1 - high) * half


def edges_kernel(width, video, ring, swap, sems):
    half = video.shape[0] // 2
    swap_row, ring_row = row_places(width, video.shape[2])
    copies = []
    for i, (row, dest) in enumerate(((ring_row, ring), (swap_row, swap))):
        for lane, first in enumerate(lanes(half)):
            source = video.at[pl.ds(first, half), :, pl.ds(row, width), :]
            copies.append(pltpu.make_async_copy(source, dest.at[pl.ds(lane * half, half)], sems.at[i, lane]))
            copies[-1].start()
    for copy in copies:
        copy.wait()


def own_kernel(width, gaps_hbm, rates_hbm, weight, video, swap, local, local_swap, driven_ring, message, table, framed, edge, full, gaps, rates, sems):
    half, frames, inner, states = local.shape
    batch, cells, channels = table.shape[0], video.shape[2], video.shape[3]
    first = lanes(half)
    copies = [pltpu.make_async_copy(gaps_hbm, gaps, sems.at[0]), pltpu.make_async_copy(rates_hbm, rates, sems.at[1])]
    for copy in copies:
        copy.start()
    for b in range(half):
        put(framed, (pl.ds(b * frames * cells, frames * cells),), video[first[1] + b].reshape(frames * cells, channels), width)
    less = cells - width
    block = framed[...]
    frame = block.reshape(half * frames, cells, 3 * channels)
    total = jnp.dot(block, weight[1], preferred_element_type=F32)
    full[...] = total.reshape(half, frames, cells, states)
    above = jnp.dot(frame[:, :less].reshape(-1, 3 * channels), weight[0], preferred_element_type=F32)
    full[:, :, width:, :] += above.reshape(half, frames, less, states)
    below = jnp.dot(frame[:, width:].reshape(-1, 3 * channels), weight[2], preferred_element_type=F32)
    full[:, :, :less, :] += below.reshape(half, frames, less, states)
    for copy in copies:
        copy.wait()
    rate = rates[...]
    for b in range(batch):
        span = None
        for t in range(frames):
            gap = gaps[first[b // half] + b % half, t]
            span = gap if span is None else span + gap
            decay = jnp.exp(-rate * gap)
            table[b, t : t + 1] = decay
            table[b, frames + t : frames + t + 1] = jnp.sqrt(1.0 - decay * decay)
            table[b, 2 * frames + t : 2 * frames + t + 1] = jnp.exp(-rate * span)
        table[b, 3 * frames : 3 * frames + 1] = jnp.zeros((1, states), F32) + span
        table[b, 3 * frames + 1 : 3 * frames + 2] = rate
    swap_row, ring_row = row_places(width, cells)
    put(edge, (slice(None),), halo_block(half, half, swap), width)
    more = jnp.dot(edge[...], weight[2 * even_strip().astype(jnp.int32)], preferred_element_type=F32)
    count = inner + width
    for b in range(half):
        driven_ring[b] = full[b, :, pl.ds(ring_row, width), :]
        for r in range(0, inner, width):

            def value_of(t):
                return full[b, t, width + r : 2 * width + r]

            state = recurrence(b, half + b, slice(r, r + width), table, local, value_of)
            message[b * count + r : b * count + r + width] = state.astype(BF16)

        def edge_value(t):
            at = (b * frames + t) * width
            return full[b, t, pl.ds(swap_row, width), :] + more[at : at + width]

        state = recurrence(b, half + b, slice(0, width), table, local_swap, edge_value)
        message[b * count + inner : (b + 1) * count] = state.astype(BF16)
    tile = span_tile([table[half + b, 3 * frames : 3 * frames + 1] for b in range(half)])
    message[half * count : half * count + tile_rows(half)] = tile


def table_rows(frames):
    return -(-(3 * frames + 2) // 8) * 8


def ring_open():
    strip = lax.axis_index("rows")
    return jnp.logical_and(strip != 0, strip != lax.axis_size("rows") - 1)


def halo_block(first, half, halo, product=None, incoming=None):
    frames, width, c = halo.shape[1:]
    x = halo[first : first + half]
    if product is None:
        return x.reshape(half * frames * width, c)
    pieces = []
    for b in range(half):
        more = incoming(first + b).astype(F32)
        pieces += [x[b, t].astype(F32) + product(b, t) * more for t in range(frames)]
    return jnp.concatenate(pieces, axis=0)


def recurrence(b, at, rows, table, local, value_of):
    frames = local.shape[1]
    state = None
    for t in range(frames):
        value = table[at, frames + t : frames + t + 1] * value_of(t)
        state = value if state is None else table[at, t : t + 1] * state + value
        local[b, t, rows] = state
    return state


def scan_ring_kernel(width, driven, table, weight, halo, local, message, framed):
    half, frames = local.shape[:2]
    x = halo_block(half, half, halo)
    put(framed, (slice(None),), jnp.where(ring_open(), x, jnp.zeros_like(x)), width)
    more = jnp.dot(framed[...], weight[2 - 2 * even_strip().astype(jnp.int32)], preferred_element_type=F32)
    for b in range(half):

        def value_of(t):
            at = (b * frames + t) * width
            return driven[b, t] + more[at : at + width]

        state = recurrence(b, half + b, slice(0, width), table, local, value_of)
        message[b * width : (b + 1) * width] = state.astype(BF16)


def scan_own_kernel(
    width, video, weight, table, swap, ring, other_swap, other_ring,
    inner, swap_local, ring_local, end_early, end_late, ring_out, swap_out, framed, full,
):
    half, frames, many, states = inner.shape
    cells, channels = video.shape[2:]
    even = even_strip()
    swap_row, ring_row = row_places(width, cells)
    open_ring = ring_open()
    for b in range(half):
        for t in range(frames):
            f = b * frames + t
            put(framed, (f, pl.ds(width, cells)), video[lanes(half)[0] + b, t], width)
            x = ring[b, t]
            x = jnp.where(open_ring, x, jnp.zeros_like(x))
            put(framed, (f, pl.ds(0, width)), jnp.where(even, x, swap[b, t]), width)
            put(framed, (f, pl.ds(cells + width, width)), jnp.where(even, swap[b, t], x), width)
    for b in range(half):
        total = None
        for d in range(3):
            lhs = framed[b * frames : (b + 1) * frames, d * width : d * width + cells].reshape(frames * cells, 3 * channels)
            term = jnp.dot(lhs, weight[d], preferred_element_type=F32)
            total = term if total is None else total + term
        full[b] = total.reshape(frames, cells, states)
        for r in range(0, many, width):
            end_early[b, r : r + width] = recurrence(
                b, b, slice(r, r + width), table, inner, lambda t: full[b, t, width + r : 2 * width + r]
            )
        every = slice(0, width)
        end_early[b, many : many + width] = recurrence(b, b, every, table, swap_local, lambda t: full[b, t, pl.ds(swap_row, width), :])
        end_late[b] = recurrence(b, b, every, table, ring_local, lambda t: full[b, t, pl.ds(ring_row, width), :])
    swap_out[:half] = swap_local[...].astype(BF16)
    swap_out[half:] = other_swap[...].astype(BF16)
    ring_out[:half] = ring_local[...].astype(BF16)
    ring_out[half:] = other_ring[...].astype(BF16)


SPAN, PREFIX, LOW, THEIRS, MINE, BEFORE = range(6)


class Refs:
    message = table = end = total = before = meta = early_total = early_low = late_low = early_before = late_before = None
    new_total = new_before = new_meta = low = outgoing = incoming = back = ring = diagonal = None

    def __init__(self, names, refs):
        self.__dict__.update(zip(names, refs))


def join_kernel(frames, early, bit, combine, last, names, *refs):
    ref = Refs(names, refs)
    table, message = ref.table, ref.message
    place = lax.axis_index("tm")
    upper = (place >> bit) % 2 == 1
    high = place % 2 == 1
    if last:
        join_last(frames, ref, upper, high)
        return
    half, count = (ref.low if bit == 0 else ref.new_before).shape[:2]
    if early:
        partner = spans_of(message[half * count :, :], half)
        ref.new_meta[...] = jnp.zeros_like(ref.new_meta)
    spans = []
    for b in range(half):
        row = slice(b, b + 1)
        rate = table[b, 3 * frames + 1 : 3 * frames + 2]
        if early:
            meta = ref.new_meta
            mine = table[b, 3 * frames : 3 * frames + 1] if bit == 0 else ref.meta[SPAN, row]
            prefix = jnp.zeros_like(mine) if bit == 0 else ref.meta[PREFIX, row]
            meta[MINE, row] = mine
            meta[BEFORE, row] = prefix
            meta[THEIRS, row] = partner[b]
            meta[SPAN, row] = mine + partner[b]
            if bit == 0:
                meta[LOW, row] = jnp.where(high, partner[b], mine)
            else:
                meta[LOW, row] = ref.meta[LOW, row]
                meta[PREFIX, row] = prefix + jnp.where(upper, partner[b], 0.0)
            theirs_span = partner[b]
        else:
            meta = ref.meta
            mine, prefix, theirs_span = meta[MINE, row], meta[BEFORE, row], meta[THEIRS, row]
        spans.append(mine + theirs_span)
        theirs = message[b * count : (b + 1) * count].astype(F32)
        own = ref.end[b] if bit == 0 else ref.total[b]
        keep = jnp.where(upper, 1.0, jnp.exp(-rate * theirs_span))
        add = jnp.where(upper, jnp.exp(-rate * mine), 1.0)
        whole = keep * own + add * theirs
        if ref.new_total is not None:
            ref.new_total[b] = whole
        if bit == 0:
            ref.low[b] = jnp.where(high, theirs, own)
        else:
            now = jnp.where(upper, jnp.exp(-rate * prefix), 0.0) * theirs
            ref.new_before[b] = now if bit == 1 else ref.before[b] + now
        if not combine:
            ref.outgoing[b * count : (b + 1) * count] = whole.astype(BF16)
        elif not early:
            many = ref.early_total.shape[1]
            ref.outgoing[b * many : (b + 1) * many] = ref.early_total[b].astype(BF16)
            at = half * many + b * count
            ref.outgoing[at : at + count] = whole.astype(BF16)
    if early != combine:
        rows = ref.outgoing.shape[0]
        ref.outgoing[rows - tile_rows(half) : rows] = span_tile(spans)


def join_last(frames, ref, upper, high):
    half, many = ref.early_low.shape[:2]
    for b in range(half):
        row = slice(b, b + 1)
        rate = ref.table[b, 3 * frames + 1 : 3 * frames + 2]
        scale = jnp.where(upper, jnp.exp(-rate * ref.meta[PREFIX, row]), 0.0)
        low_decay = jnp.exp(-rate * ref.meta[LOW, row])
        for late, low, before in ((False, ref.early_low, ref.early_before), (True, ref.late_low, ref.late_before)):
            count = low.shape[1]
            at = b * count + (half * many if late else 0)
            now = scale * ref.message[at : at + count].astype(F32)
            if before is not None:
                now = now + before[b]
            below = low_decay * now + low[b]
            mine = jnp.where(high, below, now)
            theirs = jnp.where(high, now, below).astype(BF16)
            place = slice(many, many + count) if late else slice(0, count)
            ref.incoming[b, place] = mine
            ref.back[b, place] = theirs
            if late:
                ref.ring[b] = mine.astype(BF16)
                ref.diagonal[b] = theirs


def incoming_edges_kernel(width, own, other, edge):
    half, cells = own.shape[:2]
    rows = slice(cells - 2 * width, cells - width)
    edge[:half] = own[:, rows].astype(BF16)
    edge[half:] = other[:, rows]


def gelu(x):
    return 0.5 * x * (1.0 + lax.erf(x * 0.7071067811865476))


def mix_kernel(part, width, incoming, local_inner, local_swap, local_ring, table, weight, video, inner, outer, framed):
    half, frames, many, states = local_inner.shape
    cells, channels = video.shape[2:]
    first = part * half
    even = even_strip()
    for b in range(half):
        for t in range(frames):
            product = table[first + b, 2 * frames + t : 2 * frames + t + 1]
            at = (b * frames + t) * cells
            x = local_inner[b, t] + product * incoming[b, :many].astype(F32)
            put(framed, (pl.ds(at + width, many),), x, width)
            swap = local_swap[b, t] + product * incoming[b, many : many + width].astype(F32)
            ring = local_ring[b, t] + product * incoming[b, many + width :].astype(F32)
            put(framed, (pl.ds(at, width),), jnp.where(even, ring, swap), width)
            put(framed, (pl.ds(at + cells - width, width),), jnp.where(even, swap, ring), width)
    less = cells - width
    block = framed[...]
    frame = block.reshape(half, frames, cells, 3 * states)
    total = jnp.dot(block, weight[1], preferred_element_type=F32).reshape(half, frames, cells, channels)
    above = jnp.dot(frame[:, :, :less].reshape(-1, 3 * states), weight[0], preferred_element_type=F32).reshape(half, frames, less, channels)
    below = jnp.dot(frame[:, :, width:].reshape(-1, 3 * states), weight[2], preferred_element_type=F32).reshape(half, frames, less, channels)
    for b in range(half):
        outer[0, b] = total[b, :, :width] + below[b, :, :width]
        outer[1, b] = total[b, :, less:] + above[b, :, less - width :]
        middle = total[b, :, width:less] + above[b, :, : less - width] + below[b, :, width:]
        inner[b] = (video[lanes(half)[part] + b, :, width:less].astype(F32) + gelu(middle)).astype(BF16)


def edge_rows(side, width, outer_own, outer_other, halo_local, incoming, table, weight, video, framed, edge, then):
    batch, frames, cells, channels = video.shape
    half = batch // 2

    def product(b, t):
        return table[b, 2 * frames + t : 2 * frames + t + 1]

    even = even_strip()
    below = even if side == 0 else jnp.logical_not(even)
    below = below.astype(jnp.int32)
    x = halo_block(0, batch, halo_local, product, incoming)
    if side == 1:
        x = jnp.where(ring_open(), x, jnp.zeros_like(x))
    put(framed, (slice(None),), x, width)
    more = jnp.dot(framed[...], weight[2 * below], preferred_element_type=F32).reshape(batch, frames, width, channels)
    row = aligned(below * (cells - width), width)
    for lane, outer in enumerate((outer_own, outer_other)):
        at = slice(lane * half, (lane + 1) * half)
        mixed = outer[below] + more[at]
        edge[at] = (video[pl.ds(lanes(half)[lane], half), :, pl.ds(row, width), :].astype(F32) + gelu(mixed)).astype(BF16)
        then(lane, row)


def finish_kernel(
    width, outer_own, outer_other, swap_local, swap_in, ring_local, own_in, other_in, table, weight, video, inner_own, inner_other,
    out, framed, edge, sems,
):
    batch, _, cells, _ = video.shape
    half = batch // 2
    first = lanes(half)
    copies = []

    def write(source, lane, row, count, kind):
        dest = out.at[pl.ds(first[lane], half), :, pl.ds(row, count), :]
        copies.append(pltpu.make_async_copy(source, dest, sems.at[kind, lane]))
        copies[-1].start()

    for lane, inner in enumerate((inner_own, inner_other)):
        write(inner, lane, width, cells - 2 * width, 2)

    def from_swap(b):
        return swap_in[b]

    def from_ring(b):
        return own_in[b] if b < half else other_in[b - half]

    for side, local, incoming in ((0, swap_local, from_swap), (1, ring_local, from_ring)):

        def then(lane, row):
            write(edge.at[side, pl.ds(lane * half, half)], lane, row, width, side)

        edge_rows(side, width, outer_own, outer_other, local, incoming, table, weight, video, framed.at[side], edge.at[side], then)
    for copy in copies:
        copy.wait()


def on_device(video, weight_in, weight_out, rates, gaps):
    batch, frames, rows, width, channels = video.shape
    states = weight_in.shape[3]
    half = batch // 2
    cells = rows * width
    blocks = lax.axis_size("tm")
    strips = lax.axis_size("rows")
    rounds = blocks.bit_length() - 1
    swap = [(i, i ^ 1) for i in range(strips)]

    def ring_partner(block, strip):
        if strip in (0, strips - 1):
            return block ^ 1, strip
        return block, strip + 1 if strip % 2 else strip - 1

    def diagonal_partner(block, strip):
        return block ^ 1, ring_partner(block, strip)[1]

    places = [(block, strip) for block in range(blocks) for strip in range(strips)]

    def linear(partner):
        return [(block * strips + strip, partner(block, strip)[0] * strips + partner(block, strip)[1]) for block, strip in places]

    ring, diagonal = linear(ring_partner), linear(diagonal_partner)

    def across(bit):
        mask = 1 if bit == 0 else 2 ** (bit + 1) - 2
        return [(i, i ^ mask) for i in range(blocks)]

    def in_hbm(x):
        return pltpu.with_memory_space_constraint(x, pltpu.HBM)

    video = video.reshape(batch, frames, cells, channels)
    weight_in = weight_in.reshape(3, 3 * channels, states)
    weight_out = weight_out.reshape(3, 3 * states, channels)
    edge_flops = 2 * batch * frames * width * 6 * channels * states
    own_flops = 5 * edge_flops

    edge = like(batch, frames, width, channels, dtype=BF16)
    ring_video, swap_video = call(
        functools.partial(edges_kernel, width), [in_hbm(video)], [edge, edge],
        [pltpu.SemaphoreType.DMA((2, 2))], [HBM], flops=1 << 31, bytes_accessed=1 << 26,
    )
    ring_video = lax.ppermute(ring_video, ("tm", "rows"), ring)
    swap_video = lax.ppermute(swap_video, "rows", swap)

    many = cells - 2 * width
    count = (many + width, width)
    local_inner = like(half, frames, many, states)
    local_edge = like(half, frames, width, states)
    end = [like(half, n, states) for n in count]
    message = [like(half * count[0] + tile_rows(half), states, dtype=BF16), like(half * width, states, dtype=BF16)]
    both = like(half * (many + 2 * width) + tile_rows(half), states, dtype=BF16)
    rows_in_table = table_rows(frames)
    framed = pltpu.VMEM((half * frames * width, 3 * channels), BF16)
    inner_other, swap_other, driven_ring, outgoing, table = call(
        functools.partial(own_kernel, width), [in_hbm(gaps), in_hbm(rates[None, :]), weight_in, video, swap_video],
        [local_inner, local_edge, local_edge, message[0], like(batch, rows_in_table, states)],
        [
            pltpu.VMEM((half * frames * cells, 3 * channels), BF16),
            framed,
            pltpu.VMEM((half, frames, cells, states), F32),
            pltpu.SMEM(gaps.shape, F32),
            pltpu.VMEM((1, states), F32),
            pltpu.SemaphoreType.DMA((2,)),
        ],
        [HBM] * 2 + [VMEM] * 3, mib=16, flops=own_flops // 2,
    )
    weight = weight_in
    meta_shape = like(6, 8, states)
    halo = like(batch, frames, width, states, dtype=BF16)
    incoming = [None, None]
    incoming[0] = lax.ppermute(outgoing, "tm", across(0))
    ring_other, outgoing = call(
        functools.partial(scan_ring_kernel, width), [driven_ring, table, weight, ring_video],
        [local_edge, message[1]], [framed], flops=edge_flops // 4,
    )
    incoming[1] = lax.ppermute(outgoing, "tm", across(0))
    inner_own, swap_own, ring_own, *own_end, ring_local, swap_local = call(
        functools.partial(scan_own_kernel, width), [video, weight, table, swap_video, ring_video, swap_other, ring_other],
        [local_inner, local_edge, local_edge, *end, halo, halo],
        [pltpu.VMEM((half * frames, cells + 2 * width, 3 * channels), BF16), pltpu.VMEM((half, frames, cells, states), F32)],
        mib=16, flops=own_flops // 2,
    )
    ring_local = lax.ppermute(ring_local, ("tm", "rows"), ring)
    swap_local = lax.ppermute(swap_local, "rows", swap)

    def join(early, bit, combine, last, ins, outs):
        kernel = functools.partial(join_kernel, frames, early, bit, combine, last, tuple(ins) + tuple(outs))
        return Refs(outs, call(kernel, list(ins.values()), list(outs.values())))

    final = rounds - 1
    total, before, low, meta = [None, None], [None, None], [None, None], None
    for bit in range(final):
        combine = bit + 1 == final
        for late in range(2):
            ins = dict(message=incoming[late], table=table)
            outs = dict() if late and combine else dict(new_total=end[late])
            if bit == 0:
                ins.update(end=own_end[late])
                outs.update(low=end[late])
            else:
                ins.update(total=total[late])
                outs.update(new_before=end[late])
            if bit > 1:
                ins.update(before=before[late])
            if bit or late:
                ins.update(meta=meta)
            if not late:
                outs.update(new_meta=meta_shape)
            if not combine:
                outs.update(outgoing=message[late])
            elif late:
                ins.update(early_total=total[0])
                outs.update(outgoing=both)
            got = join(not late, bit, combine, False, ins, outs)
            total[late] = got.new_total
            before[late] = got.new_before
            if bit == 0:
                low[late] = got.low
            if not late:
                meta = got.new_meta
            if got.outgoing is not None:
                incoming[late] = lax.ppermute(got.outgoing, "tm", across(bit + 1))
    ins = dict(message=incoming[1], table=table, meta=meta, early_low=low[0], late_low=low[1])
    if before[0] is not None:
        ins.update(early_before=before[0], late_before=before[1])
    edge = like(half, width, states, dtype=BF16)
    outs = dict(incoming=like(half, cells, states), back=like(half, cells, states, dtype=BF16), ring=edge, diagonal=edge)
    got = join(True, final, True, True, ins, outs)
    into_other = lax.ppermute(got.back, "tm", across(0))
    diagonal = lax.ppermute(got.diagonal, ("tm", "rows"), diagonal)
    ring_in = lax.ppermute(got.ring, ("tm", "rows"), ring)

    def mix(part, into, local, flops):
        return call(
            functools.partial(mix_kernel, part, width), [into, *local, table, weight_out, video],
            [like(half, frames, cells - 2 * width, channels, dtype=BF16), like(2, half, frames, width, channels)],
            [pltpu.VMEM((half * frames * cells, 3 * states), BF16)], mib=16, flops=flops,
        )

    inner_own, outer_own = mix(0, got.incoming, (inner_own, swap_own, ring_own), own_flops // 2)
    edge = like(batch, width, states, dtype=BF16)
    swap_in, = call(functools.partial(incoming_edges_kernel, width), [got.incoming, into_other], [edge])
    swap_in = lax.ppermute(swap_in, "rows", swap)
    inner_other, outer_other = mix(1, into_other, (inner_other, swap_other, ring_other), own_flops // 2)
    out, = call(
        functools.partial(finish_kernel, width),
        [outer_own, outer_other, swap_local, swap_in, ring_local, ring_in, diagonal, table, weight_out, video, inner_own, inner_other],
        [like(batch, frames, cells, channels, dtype=BF16)],
        [
            pltpu.VMEM((2, batch * frames * width, 3 * states), BF16),
            pltpu.VMEM((2, batch, frames, width, channels), BF16),
            pltpu.SemaphoreType.DMA((3, 2)),
        ],
        mib=16, flops=edge_flops, out_space=HBM,
    )
    return out.reshape(batch, frames, rows, width, channels)


def solution(mesh):
    in_specs = (P(None, "tm", "rows", None, None), P(), P(), P(), P(None, "tm"))
    out_specs = P(None, "tm", "rows", None, None)

    return jax.shard_map(on_device, mesh=mesh, in_specs=in_specs, out_specs=out_specs, check_vma=False)
```
